32 devices in a mesh: pairs: 16 (over z, y, core), mod: 2 (over x).
Axes of the slice: x: 2, y: 2, z: 4, core: 2. Of those that a mesh axis runs over, the one named last changes fastest.
Arguments:
- tokens: bfloat16 [64, 280, 768], P('pairs', 'mod'), may hold values from -6 to 6
- patch_counts: int32 [64], P('pairs'), may hold values from 100 to 240, as said below
- token_mask: int32 [64, 280], P('pairs', 'mod'), may hold values from 0 to 1, as said below
- ln1_gain: float32 [768], replicated, may hold values from 0.5 to 1.5
- ln1_bias: float32 [768], replicated, may hold values from -1 to 1
- qkv_weight: bfloat16 [768, 2304], replicated, may hold values from -0.3125 to 0.3125
- qv_bias: float32 [1536], replicated, may hold values from -1 to 1
- out_weight: bfloat16 [768, 768], replicated, may hold values from -0.625 to 0.625
- out_bias: float32 [768], replicated, may hold values from -1 to 1
- ln2_gain: float32 [768], replicated, may hold values from 0.5 to 1.5
- ln2_bias: float32 [768], replicated, may hold values from -1 to 1
- up_weight: bfloat16 [768, 3072], replicated, may hold values from -0.21875 to 0.21875
- up_bias: float32 [3072], replicated, may hold values from -1 to 1
- down_weight: bfloat16 [3072, 768], replicated, may hold values from -0.15625 to 0.15625
- down_bias: float32 [768], replicated, may hold values from -1 to 1
- cotangent: bfloat16 [64, 280, 768], P('pairs', 'mod'), may hold values from -6 to 6
Outputs:
- layer_out: bfloat16 [64, 280, 768], P('pairs', 'mod')
- input_grad: bfloat16 [64, 280, 768], P('pairs', 'mod')
- ln1_gain_grad: float32 [768], P(('pairs', 'mod'))
- ln1_bias_grad: float32 [768], P(('pairs', 'mod'))
- qkv_weight_grad: float32 [768, 2304], P(('pairs', 'mod'))
- qv_bias_grad: float32 [1536], P(('pairs', 'mod'))
- out_weight_grad: float32 [768, 768], P(('pairs', 'mod'))
- out_bias_grad: float32 [768], P(('pairs', 'mod'))
- ln2_gain_grad: float32 [768], P(('pairs', 'mod'))
- ln2_bias_grad: float32 [768], P(('pairs', 'mod'))
- up_weight_grad: float32 [768, 3072], P(('pairs', 'mod'))
- up_bias_grad: float32 [3072], P(('pairs', 'mod'))
- down_weight_grad: float32 [3072, 768], P(('pairs', 'mod'))
- down_bias_grad: float32 [768], P(('pairs', 'mod'))
The draws below stay inside these ranges and needn't reach their ends.
Inputs may be any that keep to these rules, and one draw needn't show every extreme that they name: `patch_counts`: each pair's number of patches; some pair has 240 and some 100. `token_mask`: row 0 of every pair is 1; the text rows of a pair are 1 up to a drawn text length and 0 after it.
All inputs are finite; a program needn't handle non-finite values.
Results may differ from the reference program's by a relative error of at most 0.015.
Values may be sent and summed in bfloat16 or wider, within the bound.
No kernel may reach another device: no remote copies, remote signals or barrier semaphores. Data moves between devices by JAX's collectives and lax.ppermute only.
A program may use at most 192 MiB of HBM per device.

```python
import jax
import jax.numpy as jnp
from jax import lax

D = 768
HEADS = 12
HEAD_DIM = 64
FF = 3072
TXT = 40
PAT_MAX = 240
PAT_MIN = 100
PPD = 4
PAIRS = 64
ROWS = 280
N_PAIRS = 16


def draw_patch_counts(key, part):
    drawn = jax.random.randint(key, (PAIRS,), PAT_MIN, PAT_MAX + 1, dtype=jnp.int32)
    return drawn.at[0].set(PAT_MAX).at[1].set(PAT_MIN)


def draw_token_mask(key, part):
    key_len, key_keep = jax.random.split(key)
    text_len = jax.random.randint(key_len, (PAIRS, 1), 1, TXT + 1, dtype=jnp.int32)
    keep = jax.random.randint(key_keep, (PAIRS, ROWS), 0, 8, dtype=jnp.int32)
    row_ids = jnp.arange(ROWS, dtype=jnp.int32)[None, :]
    text_part = (row_ids < text_len).astype(jnp.int32)
    patch_part = (keep > 0).astype(jnp.int32)
    return jnp.where(row_ids < TXT, text_part, patch_part)


def levels(rng, dims, cuts, smallest, top_value):
    level = 1.0
    for dim, parts in cuts:
        steps = jax.random.uniform(jax.random.fold_in(jax.random.fold_in(rng, 6), dim), (parts,), jnp.float32, smallest / len(cuts), top_value / len(cuts))
        level = level * jnp.repeat(jnp.exp(steps), dims[dim] // parts).reshape((-1,) + (1,) * (len(dims) - 1 - dim))
    return level


def centred(stream_key, extent, width, reach, cuts=(), kind=jnp.bfloat16):
    entries = jax.random.normal(stream_key, extent, jnp.float32) * width
    if len(cuts) > 0:
        entries = levels(stream_key, extent, cuts, -0.22, 0.18) * entries
    return jnp.clip(entries, min=-reach, max=reach).astype(kind)


def setup_inputs(seed: int = 0) -> dict:
    key_list = jax.random.split(jax.random.key(seed), 17)
    return {
        "tokens": centred(key_list[0], (PAIRS, ROWS, D), 1.0, 6.0, ((0, 16), (1, 2))),
        "patch_counts": draw_patch_counts(jax.random.fold_in(key_list[16], 71), 0),
        "token_mask": draw_token_mask(jax.random.fold_in(key_list[16], 71), 0),
        "ln1_gain": jnp.clip(1.0 + 0.1 * jax.random.normal(key_list[3], (D,), jnp.float32), 0.5, 1.5),
        "ln1_bias": centred(key_list[4], (D,), 0.2, 1.0, (), jnp.float32),
        "qkv_weight": centred(key_list[5], (D, 3 * D), (D // 2) ** -0.5, 0.3125),
        "qv_bias": centred(key_list[6], (2 * D,), 0.2, 1.0, (), jnp.float32),
        "out_weight": centred(key_list[7], (D, D), (D // 8) ** -0.5, 0.625),
        "out_bias": centred(key_list[8], (D,), 0.2, 1.0, (), jnp.float32),
        "ln2_gain": jnp.clip(1.0 + 0.1 * jax.random.normal(key_list[9], (D,), jnp.float32), 0.5, 1.5),
        "ln2_bias": centred(key_list[10], (D,), 0.2, 1.0, (), jnp.float32),
        "up_weight": centred(key_list[11], (D, FF), D ** -0.5, 0.21875),
        "up_bias": centred(key_list[12], (FF,), 0.2, 1.0, (), jnp.float32),
        "down_weight": centred(key_list[13], (FF, D), (FF // 2) ** -0.5, 0.15625),
        "down_bias": centred(key_list[14], (D,), 0.2, 1.0, (), jnp.float32),
        "cotangent": centred(key_list[15], (PAIRS, ROWS, D), 1.0, 6.0, ((0, 16), (1, 2))),
    }


@jax.custom_vjp
def low(v):
    return lax.optimization_barrier(v.astype(jnp.bfloat16)).astype(jnp.float32)

@jax.custom_vjp
def low_back(v):
    return v

def low_keep(v):
    return (low(v), None)

def low_pass(kept, grad):
    return (grad,)

def back_keep(v):
    return (v, None)

def back_low(kept, grad):
    return (low(grad),)
low.defvjp(low_keep, low_pass)
low_back.defvjp(back_keep, back_low)
EPS = 1e-06
MASKED = -1e+30
HIGH = lax.Precision.HIGHEST

def norm_rows(rows_in, gain, shift):
    center = rows_in - lax.optimization_barrier(jnp.mean(rows_in, axis=-1, keepdims=True))
    spread = lax.optimization_barrier(jnp.mean(center * center, axis=-1, keepdims=True))
    return center * lax.rsqrt(spread + EPS) * gain + shift

def group_forward(params, inputs, counts, masks):
    ln1_gain, ln1_bias, qkv_weight, qv_bias, out_weight, out_bias, ln2_gain, ln2_bias, up_weight, up_bias, down_weight, down_bias = params
    group = inputs.shape[0]
    row_ids = jnp.arange(ROWS, dtype=jnp.int32)
    live = row_ids[None, :] < (TXT + counts)[:, None]
    key_ok = jnp.logical_and(live, masks == 1)
    first_norm = low(norm_rows(inputs, ln1_gain, ln1_bias))
    projected = jnp.einsum('gtd,de->gte', first_norm, qkv_weight, precision=HIGH)
    queries = low(low_back(projected[..., :D] + qv_bias[:D]))
    keys = low(low_back(projected[..., D:2 * D]))
    values = low(low_back(projected[..., 2 * D:] + qv_bias[D:]))
    shape4 = (group, ROWS, HEADS, HEAD_DIM)
    scores = jnp.einsum('gqhd,gkhd->ghqk', queries.reshape(shape4), keys.reshape(shape4), precision=HIGH)
    scores = low_back(scores * HEAD_DIM ** (-0.5))
    scores = jnp.where(key_ok[:, None, None, :], scores, MASKED)
    probs = low(jax.nn.softmax(scores, axis=-1))
    mixed = jnp.einsum('ghqk,gkhd->gqhd', probs, values.reshape(shape4), precision=HIGH)
    mixed = low(low_back(mixed.reshape(group, ROWS, D)))
    branch = low_back(jnp.einsum('gtd,de->gte', mixed, out_weight, precision=HIGH) + out_bias)
    attended = inputs + branch
    second_norm = low(norm_rows(attended, ln2_gain, ln2_bias))
    pre_act = low_back(jnp.einsum('gtd,df->gtf', second_norm, up_weight, precision=HIGH) + up_bias)
    hidden = low(jax.nn.gelu(pre_act, approximate=False))
    final = attended + jnp.einsum('gtf,fd->gtd', hidden, down_weight, precision=HIGH) + down_bias
    return jnp.where(live[..., None], final, 0.0)

def reference(tokens, patch_counts, token_mask, ln1_gain, ln1_bias, qkv_weight, qv_bias, out_weight, out_bias, ln2_gain, ln2_bias, up_weight, up_bias, down_weight, down_bias, cotangent):
    params = tuple((arr.astype(jnp.float32) for arr in (ln1_gain, ln1_bias, qkv_weight, qv_bias, out_weight, out_bias, ln2_gain, ln2_bias, up_weight, up_bias, down_weight, down_bias)))
    inputs = tokens.astype(jnp.float32).reshape(N_PAIRS, PPD, ROWS, D)
    counts = patch_counts.reshape(N_PAIRS, PPD)
    masks = token_mask.reshape(N_PAIRS, PPD, ROWS)

    def whole(params_in, inputs_in):

        def step(carry, item):
            return (carry, jax.checkpoint(group_forward)(params_in, item[0], item[1], item[2]))
        return lax.scan(step, None, (inputs_in, counts, masks))[1]
    result, pull = jax.vjp(whole, params, inputs)
    grad_params, grad_inputs = pull(cotangent.astype(jnp.float32).reshape(N_PAIRS, PPD, ROWS, D))
    return (result.reshape(PAIRS, ROWS, D).astype(jnp.bfloat16), grad_inputs.reshape(PAIRS, ROWS, D).astype(jnp.bfloat16), grad_params[0], grad_params[1], grad_params[2], grad_params[3], grad_params[4], grad_params[5], grad_params[6], grad_params[7], grad_params[8], grad_params[9], grad_params[10], grad_params[11])
```

```python
from functools import partial

import jax
import jax.numpy as jnp
import numpy as np
from jax import lax
from jax.experimental import pallas as pl
from jax.experimental.pallas import tpu as pltpu
from jax.sharding import PartitionSpec as P

HEAD_DIM = 64
TXT = 40
EPS = 1e-06
MASKED = -1e30
AXES = ("pairs", "mod")
BF16 = jnp.bfloat16
F32 = jnp.float32
LANES = 128
MIB = 1 << 20

CORE_BIT = 2
ORDERS = ((4, 8, 1, 16), (8, 4, 1, 16))


def dot_nn(a, b):
    return jnp.dot(a, b, preferred_element_type=F32)


def dot_nt(a, b):
    return lax.dot_general(a, b, (((1,), (1,)), ((), ())), preferred_element_type=F32)


def dot_tn(a, b):
    return lax.dot_general(a, b, (((0,), (0,)), ((), ())), preferred_element_type=F32)


def norm_parts(v):
    center = v - jnp.mean(v, axis=-1, keepdims=True)
    rstd = lax.rsqrt(jnp.mean(center * center, axis=-1, keepdims=True) + EPS)
    return center * rstd, rstd


def norm_back(grad, unit, rstd, gain):
    d = grad * gain
    return rstd * (
        d
        - jnp.mean(d, axis=-1, keepdims=True)
        - unit * jnp.mean(d * unit, axis=-1, keepdims=True)
    )


def gelu_and_slope(v):
    u = jnp.abs(v) * 0.7071067811865476
    t = 1.0 / (1.0 + 0.3275911 * u)
    bell = jnp.exp(-u * u)
    poly = t * (
        0.127414796
        + t * (-0.142248368 + t * (0.7107068705 + t * (-0.7265760135 + t * 0.5307027145)))
    )
    tail = poly * bell
    phi = jnp.where(v >= 0, 1.0 - tail, tail)
    return v * phi, phi + v * bell * 0.3989422804014327


def norm_qkv_kernel(x_ref, g_ref, b_ref, w_ref, qvb_ref, fn_ref, qkv_ref):
    j = pl.program_id(0)
    rows, width = fn_ref.shape[0] * fn_ref.shape[1], fn_ref.shape[2]

    @pl.when(j == 0)
    def _():
        x = x_ref[...].reshape(rows, width).astype(F32)
        unit, _ = norm_parts(x)
        fn_ref[...] = (unit * g_ref[...] + b_ref[...]).astype(BF16).reshape(fn_ref.shape)

    fn = fn_ref[...].reshape(rows, width)
    bias = jnp.where(j == 1, 0.0, 1.0) * qvb_ref[0]
    out = dot_nn(fn, w_ref[...]) + bias
    qkv_ref[...] = out.astype(BF16).reshape(qkv_ref.shape)


def norm_qkv(x, gain, shift, weight, qv_bias):
    pairs, half, width = x.shape
    whole = lambda j: (0, 0, 0)
    return pl.pallas_call(
        norm_qkv_kernel,
        grid=(3,),
        in_specs=[
            pl.BlockSpec((pairs, half, width), whole),
            pl.BlockSpec((1, width), lambda j: (0, 0)),
            pl.BlockSpec((1, width), lambda j: (0, 0)),
            pl.BlockSpec((width, width), lambda j: (0, j)),
            pl.BlockSpec((1, 1, width), lambda j: (j // 2, 0, 0)),
        ],
        out_specs=[
            pl.BlockSpec((pairs, half, width), whole),
            pl.BlockSpec((pairs, half, width), lambda j: (0, 0, j)),
        ],
        out_shape=[
            jax.ShapeDtypeStruct((pairs, half, width), BF16),
            jax.ShapeDtypeStruct((pairs, half, 3 * width), BF16),
        ],
        compiler_params=pltpu.CompilerParams(vmem_limit_bytes=24 * MIB),
        cost_estimate=pl.CostEstimate(
            flops=2 * pairs * half * width * 3 * width,
            bytes_accessed=2 * (3 * width * width + 5 * pairs * half * width),
            transcendentals=0,
        ),
        name="norm_qkv",
    )(x, gain, shift, weight, qv_bias)


def attend_kernel(
    qo, qr, xo, xr, okrow, ow, ob, g2, b2, mixed_ref, att_ref, sn_ref, p_ref, mix_s
):
    half, width = xo.shape[1], xo.shape[2]
    rows = 2 * half
    key_ok = (okrow[0] + xr[0, half - 4 : half - 3, :]).astype(F32)[:, :rows] > 0.5
    bias = jnp.where(key_ok, 0.0, MASKED)
    first = lax.broadcasted_iota(jnp.int32, (1, LANES), 1) < HEAD_DIM
    zero = jnp.zeros((), BF16)

    def both(col):
        cols = pl.ds(pl.multiple_of(col, LANES), LANES)
        return jnp.concatenate([qo[0, :, cols], qr[0, :, cols]], axis=0)

    def two_heads(hp, carry):
        q = both(hp * LANES) * jnp.asarray(HEAD_DIM**-0.5, BF16)
        k = both(width + hp * LANES)
        v = both(2 * width + hp * LANES)
        outs = []
        for h in range(2):
            kh = jnp.where(first if h == 0 else jnp.logical_not(first), k, zero)
            s = dot_nt(q, kh) + bias
            e = jnp.exp(s - jnp.max(s, axis=-1, keepdims=True))
            p = (e * (1.0 / jnp.sum(e, axis=-1, keepdims=True))).astype(BF16)
            p_ref[0, 2 * hp + h] = p
            outs.append(dot_nn(p, v))
        cols = pl.ds(pl.multiple_of(hp * LANES, LANES), LANES)
        mix_s[:, cols] = jnp.where(first, outs[0], outs[1]).astype(BF16)
        return carry

    lax.fori_loop(0, width // LANES, two_heads, 0)
    mixed = mix_s[...]
    mixed_ref[...] = mixed.reshape(mixed_ref.shape)
    x = jnp.concatenate([xo[0], xr[0]], axis=0).astype(F32)
    att = x + dot_nn(mixed, ow[...]) + ob[...]
    att_ref[...] = att.reshape(att_ref.shape)
    unit, _ = norm_parts(att)
    sn_ref[...] = (unit * g2[...] + b2[...]).astype(BF16).reshape(sn_ref.shape)


def attend(qkv_own, qkv_far, x_own, x_far, okrow, out_weight, out_bias, gain, shift):
    pairs, half, width = x_own.shape
    heads = width // HEAD_DIM
    rows = 2 * half
    pair3 = lambda p: (p, 0, 0)
    const = lambda p: (0, 0)
    both = lambda p: (0, p, 0, 0)
    return pl.pallas_call(
        attend_kernel,
        grid=(pairs,),
        in_specs=[
            pl.BlockSpec((1, half, 3 * width), pair3),
            pl.BlockSpec((1, half, 3 * width), pair3),
            pl.BlockSpec((1, half, width), pair3),
            pl.BlockSpec((1, half, width), pair3),
            pl.BlockSpec((1, 1, width), pair3),
            pl.BlockSpec((width, width), const),
            pl.BlockSpec((1, width), const),
            pl.BlockSpec((1, width), const),
            pl.BlockSpec((1, width), const),
        ],
        out_specs=[
            pl.BlockSpec((2, 1, half, width), both),
            pl.BlockSpec((2, 1, half, width), both),
            pl.BlockSpec((2, 1, half, width), both),
            pl.BlockSpec((1, heads, rows, rows), lambda p: (p, 0, 0, 0)),
        ],
        out_shape=[
            jax.ShapeDtypeStruct((2, pairs, half, width), BF16),
            jax.ShapeDtypeStruct((2, pairs, half, width), F32),
            jax.ShapeDtypeStruct((2, pairs, half, width), BF16),
            jax.ShapeDtypeStruct((pairs, heads, rows, rows), BF16),
        ],
        scratch_shapes=[pltpu.VMEM((rows, width), BF16)],
        compiler_params=pltpu.CompilerParams(vmem_limit_bytes=40 * MIB),
        cost_estimate=pl.CostEstimate(
            flops=pairs * heads * 8 * rows * rows * LANES,
            bytes_accessed=2 * pairs * rows * width * 8 + 2 * pairs * heads * rows * rows,
            transcendentals=pairs * heads * rows * rows,
        ),
        name="attend",
    )(qkv_own, qkv_far, x_own, x_far, okrow, out_weight, out_bias, gain, shift)


def live_rows(info, p, far, half):
    side = info[2] if far == 0 else 1 - info[2]
    row = lax.broadcasted_iota(jnp.int32, (half, 1), 0)
    real = half - 4
    limit = jnp.minimum(TXT + info[p] - side * real, real)
    return row < limit


def mlp_up_kernel(
    info, inv, sn, att, co, cr, up, upb, down, downb,
    slope_ref, own_ref, far_ref, gy_ref, dbg_ref, keep_ref, send_ref, acc, wdn,
    *, shard,
):
    j = pl.program_id(0)
    last = pl.num_programs(0) - 1
    pairs, half, width = co.shape
    tile = up.shape[1]

    @pl.when(j == 0)
    def _():
        for far, c in enumerate((co, cr)):
            for p in range(pairs):
                at = (far * pairs + p) * half
                gy_ref[at : at + half, :] = jnp.where(
                    live_rows(info, p, far, half), c[p].astype(F32), 0.0
                ).astype(BF16)
        dbg_ref[...] = jnp.sum(gy_ref[...].astype(F32), axis=0, keepdims=True)

    h, slope = gelu_and_slope(dot_nn(sn[...], up[...]) + upb[...])
    slope_ref[...] = slope.astype(BF16)
    h = h.astype(BF16)
    part = dot_nn(h, down[...])

    @pl.when(j == 0)
    def _():
        acc[...] = part

    @pl.when(j > 0)
    def _():
        acc[...] += part

    wdn[pl.ds(pl.multiple_of(j * tile, tile), tile), :] = dot_tn(h, gy_ref[...]).astype(wdn.dtype)

    @pl.when(j == last)
    def _():
        final = att[...] + acc[...] + downb[...]
        for far, o in enumerate((own_ref, far_ref)):
            for p in range(pairs):
                at = (far * pairs + p) * half
                o[p] = jnp.where(
                    live_rows(info, p, far, half), final[at : at + half, :], 0.0
                ).astype(BF16)
        if shard:
            n = keep_ref.shape[0]

            def fill(p, carry):
                at = lambda q: pl.ds(pl.multiple_of(inv[q] * shard, shard), shard)
                keep_ref[p] = wdn[at(p), :]
                send_ref[p] = wdn[at(n + p), :]
                return carry

            lax.fori_loop(0, n, fill, 0)
        else:
            keep_ref[...] = wdn[...]
            send_ref[...] = jnp.zeros_like(send_ref)


def mlp_up(info, inv, sn, att, cot_own, cot_far, up, up_bias, down, down_bias, shards, packed):
    pairs, half, width = cot_own.shape
    rows = 2 * pairs * half
    ff = up.shape[1]
    tile = width
    shard = ff // shards
    if packed:
        wire = [jax.ShapeDtypeStruct((shards // 2, shard, width), BF16)] * 2
    else:
        wire = [jax.ShapeDtypeStruct((ff, width), F32), jax.ShapeDtypeStruct((8, LANES), F32)]
    z = lambda j, *_: (0, 0)
    z3 = lambda j, *_: (0, 0, 0)
    return pl.pallas_call(
        partial(mlp_up_kernel, shard=shard if packed else 0),
        grid_spec=pltpu.PrefetchScalarGridSpec(
            num_scalar_prefetch=2,
            grid=(ff // tile,),
            in_specs=[
                pl.BlockSpec((rows, width), z),
                pl.BlockSpec((rows, width), z),
                pl.BlockSpec((pairs, half, width), z3),
                pl.BlockSpec((pairs, half, width), z3),
                pl.BlockSpec((width, tile), lambda j, *_: (0, j)),
                pl.BlockSpec((1, tile), lambda j, *_: (0, j)),
                pl.BlockSpec((tile, width), lambda j, *_: (j, 0)),
                pl.BlockSpec((1, width), z),
            ],
            out_specs=[
                pl.BlockSpec((rows, tile), lambda j, *_: (0, j)),
                pl.BlockSpec((pairs, half, width), z3),
                pl.BlockSpec((pairs, half, width), z3),
                pl.BlockSpec((rows, width), z),
                pl.BlockSpec((1, width), z),
            ]
            + [pl.BlockSpec(w.shape, z3 if packed else z) for w in wire],
            scratch_shapes=[
                pltpu.VMEM((rows, width), F32),
                pltpu.VMEM((ff, width), BF16 if packed else F32),
            ],
        ),
        out_shape=[
            jax.ShapeDtypeStruct((rows, ff), BF16),
            jax.ShapeDtypeStruct((pairs, half, width), BF16),
            jax.ShapeDtypeStruct((pairs, half, width), BF16),
            jax.ShapeDtypeStruct((rows, width), BF16),
            jax.ShapeDtypeStruct((1, width), F32),
        ]
        + wire,
        compiler_params=pltpu.CompilerParams(vmem_limit_bytes=(48 if packed else 60) * MIB),
        cost_estimate=pl.CostEstimate(
            flops=6 * rows * width * ff, bytes_accessed=24 * MIB, transcendentals=rows * ff
        ),
        name="mlp_up",
    )(info, inv, sn, att, cot_own, cot_far, up, up_bias, down, down_bias)


def pack_tile(acc, inv, keep_ref, send_ref, t, rows):
    n = keep_ref.shape[0]
    groups, cut = rows // 8, acc.shape[1] // 2

    def fill(ref, base):
        def one(p, carry):
            top = inv[base + p] * rows
            for g in range(groups):
                blk = acc[pl.ds(pl.multiple_of(top + 8 * g, 8), 8), :]
                val = jnp.concatenate([blk[:, :cut], blk[:, cut:]], axis=0).astype(BF16)
                ref[p, :, pl.ds(pl.multiple_of((t * groups + g) * cut, LANES), cut)] = val
            return carry

        lax.fori_loop(0, n, one, 0, unroll=2)

    fill(keep_ref, 0)
    fill(send_ref, n)


def mlp_back_kernel(
    inv, gs_in, gy, slope, sn, up, down, gs_ref, upb_ref, keep_ref, send_ref, tile_acc, *, shard, first
):
    j = pl.program_id(0)
    gh = dot_nt(gy[...], down[...])
    gp = gh * slope[...].astype(F32)
    gp = gp.astype(BF16)
    upb_ref[...] = jnp.sum(gp.astype(F32), axis=0, keepdims=True)
    part = dot_nt(gp, up[...])

    @pl.when(j == 0)
    def _():
        gs_ref[...] = part if first else gs_in[...] + part

    @pl.when(j > 0)
    def _():
        gs_ref[...] += part

    if shard:
        tile_acc[...] = dot_tn(sn[...], gp)
        pack_tile(tile_acc, inv, keep_ref, send_ref, j, shard)
    else:
        keep_ref[...] = dot_tn(sn[...], gp)
        send_ref[...] = jnp.zeros_like(send_ref)


def mlp_back(inv, gs, gy, slope, sn, up, down, start, tiles, shards, packed):
    rows, width = gy.shape
    tile = width
    shard = width // shards
    first = gs is None
    if first:
        gs, gs_spec = jnp.zeros((8, LANES), F32), pl.BlockSpec((8, LANES), lambda j, *_: (0, 0))
    else:
        gs_spec = pl.BlockSpec((rows, width), lambda j, *_: (0, 0))
    z = lambda j, *_: (0, 0)
    z3 = lambda j, *_: (0, 0, 0)
    cols = lambda j, *_: (0, j + start)
    own = lambda j, *_: (0, j)
    if packed:
        wire = [jax.ShapeDtypeStruct((shards // 2, 16, shard * tiles * tile // 16), BF16)] * 2
        wire_specs = [pl.BlockSpec(w.shape, z3) for w in wire]
    else:
        wire = [
            jax.ShapeDtypeStruct((width, tiles * tile), F32),
            jax.ShapeDtypeStruct((8, LANES), F32),
        ]
        wire_specs = [pl.BlockSpec((width, tile), own), pl.BlockSpec((8, LANES), z)]
    return pl.pallas_call(
        partial(mlp_back_kernel, shard=shard if packed else 0, first=first),
        grid_spec=pltpu.PrefetchScalarGridSpec(
            num_scalar_prefetch=1,
            grid=(tiles,),
            in_specs=[
                gs_spec,
                pl.BlockSpec((rows, width), z),
                pl.BlockSpec((rows, tile), cols),
                pl.BlockSpec((rows, width), z),
                pl.BlockSpec((width, tile), cols),
                pl.BlockSpec((tile, width), lambda j, *_: (j + start, 0)),
            ],
            out_specs=[pl.BlockSpec((rows, width), z), pl.BlockSpec((1, tile), own)] + wire_specs,
            scratch_shapes=[pltpu.VMEM((width, tile), F32)],
        ),
        out_shape=[
            jax.ShapeDtypeStruct((rows, width), F32),
            jax.ShapeDtypeStruct((1, tiles * tile), F32),
        ]
        + wire,
        compiler_params=pltpu.CompilerParams(vmem_limit_bytes=48 * MIB),
        cost_estimate=pl.CostEstimate(
            flops=6 * rows * width * tile * tiles, bytes_accessed=10 * MIB, transcendentals=0
        ),
        name="mlp_back",
    )(inv, gs, gy, slope, sn, up, down)


def attend_back_kernel(
    gs, gy, att, xo, xr, qo, qr, p_ref, qkvw, ow, g1, g2,
    own_ref, far_ref, vec_ref, dqkv, gbs, gms,
):
    half, width = xo.shape[1], xo.shape[2]
    rows = 2 * half
    first = lax.broadcasted_iota(jnp.int32, (1, LANES), 1) < HEAD_DIM
    zero = jnp.zeros((), BF16)
    scale = HEAD_DIM**-0.5

    def set_vec(i, value):
        vec_ref[i : i + 1, :] = jnp.sum(value, axis=0, keepdims=True)

    grad_second = gs[...].reshape(rows, width)
    unit, rstd = norm_parts(att[...].reshape(rows, width))
    set_vec(5, grad_second * unit)
    set_vec(6, grad_second)
    grad_att = gy[...].reshape(rows, width).astype(F32) + norm_back(
        grad_second, unit, rstd, g2[...]
    )
    branch = grad_att.astype(BF16)
    set_vec(4, branch.astype(F32))
    vec_ref[7:8, :] = jnp.zeros((1, width), F32)
    gbs[...] = branch
    gms[...] = dot_nt(branch, ow[...]).astype(BF16)

    def both(col):
        cols = pl.ds(pl.multiple_of(col, LANES), LANES)
        return jnp.concatenate([qo[0, :, cols], qr[0, :, cols]], axis=0)

    def two_heads(hp, carry):
        q = both(hp * LANES) * jnp.asarray(scale, BF16)
        k = both(width + hp * LANES) * jnp.asarray(scale, BF16)
        v = both(2 * width + hp * LANES)
        gm = gms[:, pl.ds(pl.multiple_of(hp * LANES, LANES), LANES)]
        dq, dk, dv = [], [], []
        for h in range(2):
            vh = jnp.where(first if h == 0 else jnp.logical_not(first), v, zero)
            prob = p_ref[0, 2 * hp + h]
            dp = dot_nt(gm, vh)
            pf = prob.astype(F32)
            delta = jnp.sum(dp * pf, axis=-1, keepdims=True)
            ds = (pf * (dp - delta)).astype(BF16)
            dv.append(dot_tn(prob, gm))
            dq.append(dot_nn(ds, k))
            dk.append(dot_tn(ds, q))
        for i, pair_of in enumerate((dq, dk, dv)):
            cols = pl.ds(pl.multiple_of(i * width + hp * LANES, LANES), LANES)
            dqkv[:, cols] = jnp.where(first, pair_of[0], pair_of[1]).astype(BF16)
        return carry

    lax.fori_loop(0, width // LANES, two_heads, 0)
    mine = dqkv[...]
    grad_first = dot_nt(mine, qkvw[...])
    x = jnp.concatenate([xo[0], xr[0]], axis=0).astype(F32)
    unit1, rstd1 = norm_parts(x)
    set_vec(0, grad_first * unit1)
    set_vec(1, grad_first)
    set_vec(2, mine[:, :width].astype(F32))
    set_vec(3, mine[:, 2 * width :].astype(F32))
    result = (grad_att + norm_back(grad_first, unit1, rstd1, g1[...])).astype(BF16)
    own_ref[...] = result[:half]
    far_ref[...] = result[half:]


def attend_back(
    pair, gs, gy, att, x_own, x_far, qkv_own, qkv_far, probs, qkv_weight, out_weight, gain1, gain2,
):
    pairs, half, width = x_own.shape
    rows = 2 * half
    heads = width // HEAD_DIM
    pair3 = lambda i: (pair, 0, 0)
    both = lambda i: (0, pair, 0, 0)
    const = lambda i: (0, 0)
    return pl.pallas_call(
        attend_back_kernel,
        grid=(1,),
        in_specs=[
            pl.BlockSpec((2, 1, half, width), both),
            pl.BlockSpec((2, 1, half, width), both),
            pl.BlockSpec((2, 1, half, width), both),
            pl.BlockSpec((1, half, width), pair3),
            pl.BlockSpec((1, half, width), pair3),
            pl.BlockSpec((1, half, 3 * width), pair3),
            pl.BlockSpec((1, half, 3 * width), pair3),
            pl.BlockSpec((1, heads, rows, rows), lambda i: (pair, 0, 0, 0)),
            pl.BlockSpec((width, 3 * width), const),
            pl.BlockSpec((width, width), const),
            pl.BlockSpec((1, width), const),
            pl.BlockSpec((1, width), const),
        ],
        out_specs=[
            pl.BlockSpec((half, width), const),
            pl.BlockSpec((half, width), const),
            pl.BlockSpec((8, width), const),
            pl.BlockSpec((rows, 3 * width), const),
            pl.BlockSpec((rows, width), const),
        ],
        scratch_shapes=[pltpu.VMEM((rows, width), BF16)],
        out_shape=[
            jax.ShapeDtypeStruct((half, width), BF16),
            jax.ShapeDtypeStruct((half, width), BF16),
            jax.ShapeDtypeStruct((8, width), F32),
            jax.ShapeDtypeStruct((rows, 3 * width), BF16),
            jax.ShapeDtypeStruct((rows, width), BF16),
        ],
        compiler_params=pltpu.CompilerParams(vmem_limit_bytes=36 * MIB),
        cost_estimate=pl.CostEstimate(
            flops=heads * 16 * rows * rows * LANES + 8 * rows * width * width,
            bytes_accessed=12 * MIB,
            transcendentals=0,
        ),
        name="attend_back",
    )(gs, gy, att, x_own, x_far, qkv_own, qkv_far, probs, qkv_weight, out_weight, gain1, gain2)


def weight_grads_kernel(
    inv, dq0, dq1, gb0, gb1, mixed, fno, fnr, v0, v1, upa, upb, dbg,
    vec_ref, keep_ref, send_ref, dqkv, gbs, fns, mxs, tile_acc, *, shard,
):
    pairs, half, width = fno.shape
    rows = 2 * half
    for i, (d, g) in enumerate(((dq0, gb0), (dq1, gb1))):
        at = i * rows
        dqkv[at : at + rows, :] = d[...]
        gbs[at : at + rows, :] = g[...]
        fns[at : at + half, :] = fno[i]
        fns[at + half : at + rows, :] = fnr[i]
        mxs[at : at + rows, :] = mixed[:, i].reshape(rows, width)
    vec_ref[0:8, :] = v0[...] + v1[...]
    vec_ref[7:8, :] = dbg[...]
    for i in range(4):
        src = (upa, upb)[i // 2]
        vec_ref[8 + i : 9 + i, :] = src[:, i % 2 * width : (i % 2 + 1) * width]
    vec_ref[12:16, :] = jnp.zeros((4, width), F32)

    for t in range(4):
        if t < 3:
            val = dot_tn(fns[...], dqkv[:, t * width : (t + 1) * width])
        else:
            val = dot_tn(mxs[...], gbs[...])
        if shard:
            tile_acc[...] = val
            pack_tile(tile_acc, inv, keep_ref, send_ref, t, shard)
        elif t < 3:
            keep_ref[:, t * width : (t + 1) * width] = val
        else:
            send_ref[...] = val
    if shard:
        n = keep_ref.shape[0]
        at = keep_ref.shape[2] - LANES
        v = vec_ref[...]
        small = jnp.concatenate([v[0:2], v[4:8], v[0:2]], axis=0)
        rowid = lax.broadcasted_iota(jnp.int32, (8, LANES), 0)
        per_q, per_u = width // (2 * shard), width // (4 * shard)

        def piece(block, start):
            return pltpu.roll(block, lax.rem(width - start, width), 1)[:, :LANES]

        def block(i):
            a = piece(small, i * shard)
            b = piece(v[2:4], lax.rem(i, per_q) * 2 * shard)
            brow = jnp.where(i < per_q, b[0:1], b[1:2])
            c = piece(v[8:12], lax.rem(i, per_u) * 4 * shard)
            ci = lax.div(i, per_u)
            crow = jnp.where(
                ci == 0, c[0:1], jnp.where(ci == 1, c[1:2], jnp.where(ci == 2, c[2:3], c[3:4]))
            )
            top = jnp.where(rowid < 6, a, jnp.where(rowid == 6, brow, crow))
            return jnp.concatenate([top, jnp.zeros_like(top)], axis=0).astype(BF16)

        def fill(p, carry):
            keep_ref[p, :, at : at + LANES] = block(inv[p])
            send_ref[p, :, at : at + LANES] = block(inv[n + p])
            return carry

        lax.fori_loop(0, n, fill, 0)


def weight_grads(
    inv, dqkv0, dqkv1, gb0, gb1, mixed, fn_own, fn_far, vec0, vec1, upa, upb, dbg, shards, packed
):
    pairs, half, width = fn_own.shape
    rows = 2 * half
    shard = width // shards
    if packed:
        wire = [jax.ShapeDtypeStruct((shards // 2, 16, shard * 4 * width // 16 + LANES), BF16)] * 2
    else:
        wire = [
            jax.ShapeDtypeStruct((width, 3 * width), F32),
            jax.ShapeDtypeStruct((width, width), F32),
        ]
    full = lambda a: pl.BlockSpec(a.shape, lambda i, *_: (0,) * len(a.shape))
    args = (dqkv0, dqkv1, gb0, gb1, mixed, fn_own, fn_far, vec0, vec1, upa, upb, dbg)
    outs = [jax.ShapeDtypeStruct((16, width), F32)] + wire
    return pl.pallas_call(
        partial(weight_grads_kernel, shard=shard if packed else 0),
        grid_spec=pltpu.PrefetchScalarGridSpec(
            num_scalar_prefetch=1,
            grid=(1,),
            in_specs=[full(a) for a in args],
            out_specs=[full(o) for o in outs],
            scratch_shapes=[
                pltpu.VMEM((pairs * rows, 3 * width), BF16),
                pltpu.VMEM((pairs * rows, width), BF16),
                pltpu.VMEM((pairs * rows, width), BF16),
                pltpu.VMEM((pairs * rows, width), BF16),
                pltpu.VMEM((width, width), F32),
            ],
        ),
        out_shape=outs,
        compiler_params=pltpu.CompilerParams(vmem_limit_bytes=48 * MIB),
        cost_estimate=pl.CostEstimate(
            flops=8 * pairs * rows * width * width, bytes_accessed=14 * MIB, transcendentals=0
        ),
        name="weight_grads",
    )(inv, *args)


def core_of(i):
    return 1 if i & CORE_BIT else 0


def shard_order(me, shards):
    half = shards // 2
    bits = half.bit_length() - 1
    tables = []
    for order in ORDERS:
        row = []
        for p in range(half):
            rel = 0
            for i, bit in enumerate(order):
                if p >> (bits - 1 - i) & 1:
                    rel |= bit
            row.append(rel)
        tables.append(row)
    tables = jnp.asarray(np.array(tables, np.int32))
    core = jnp.where(me & CORE_BIT, 1, 0)
    keep = jnp.where(core == 0, tables[0], tables[1])
    send = jnp.where(core == 0, tables[1], tables[0]) | CORE_BIT
    return me ^ jnp.concatenate([keep, send])


def add_up(terms):
    total = terms[0].astype(F32)
    for t in terms[1:]:
        total = total + t.astype(F32)
    return total


class Reduction:
    def __init__(self, keep, send, shards):
        self.shards, self.stage, self.n = shards, 0, keep.shape[0]
        self.terms = [keep]
        self.incoming = lax.ppermute(send, AXES, [(i, i ^ CORE_BIT) for i in range(shards)])

    def step(self, *after):
        recv = lax.optimization_barrier((self.incoming,) + after)[0]
        self.terms.append(recv)
        self.n //= 2
        out = add_up([t[self.n :] for t in self.terms]).astype(BF16)
        self.terms = [t[: self.n] for t in self.terms]
        route = [(i, i ^ ORDERS[core_of(i)][self.stage]) for i in range(self.shards)]
        self.incoming = lax.ppermute(out, AXES, route)
        self.stage += 1
        return out

    def result(self):
        return add_up(self.terms + [self.incoming])[0]


def unpack_rows(block, tiles, rows):
    groups = rows // 8
    cut = block.shape[1] // (tiles * groups)
    block = block.reshape(2, 8, tiles, groups, cut)
    return block.transpose(3, 1, 2, 0, 4).reshape(rows, tiles * 2 * cut)


def tie(*values):
    return lax.optimization_barrier(values)


def swap_sides(block):
    return lax.ppermute(block, "mod", [(0, 1), (1, 0)])


def on_device(
    tokens, patch_counts, token_mask, ln1_gain, ln1_bias, qkv_weight, qv_bias, out_weight,
    out_bias, ln2_gain, ln2_bias, up_weight, up_bias, down_weight, down_bias, cotangent,
):
    shards = lax.axis_size("pairs") * lax.axis_size("mod")
    pairs_here, real, width = tokens.shape
    pairs = pairs_here // 2
    half = real + 4
    packed = shards == 32 and width % (8 * shards) == 0
    side = lax.axis_index("mod")
    me = lax.axis_index("pairs") * 2 + side
    mine, theirs = side * pairs, (1 - side) * pairs

    def pick(arr, at):
        return lax.dynamic_slice_in_dim(arr, at, pairs, 0)

    row_ids = side * real + jnp.arange(real, dtype=jnp.int32)
    live = row_ids[None, :] < (TXT + patch_counts)[:, None]
    ok = jnp.logical_and(live, token_mask == 1).astype(BF16)
    ok_send = jnp.pad(pick(ok, theirs), ((0, 0), (half, width - half - real)))
    ok_own = jnp.pad(pick(ok, mine), ((0, 0), (0, width - real)))[:, None, :]
    pad3 = ((0, 0), (0, 4), (0, 0))
    tok_send = jnp.concatenate(
        [pick(tokens, theirs), ok_send[:, None, :], jnp.zeros((pairs, 3, width), BF16)], axis=1
    )
    x_far = swap_sides(tok_send)
    x_own = jnp.pad(pick(tokens, mine), pad3)
    cot_own = jnp.pad(pick(cotangent, mine), pad3)
    cot_send = jnp.pad(pick(cotangent, theirs), pad3)

    counts = pick(patch_counts, mine)
    info = jnp.concatenate([counts, side[None].astype(jnp.int32)])
    if packed:
        inv = shard_order(me, shards).astype(jnp.int32)
    else:
        inv = jnp.zeros((8,), jnp.int32)

    row = lambda v: v.reshape(1, -1)
    g1, b1, g2, b2 = row(ln1_gain), row(ln1_bias), row(ln2_gain), row(ln2_bias)
    qvb = qv_bias.reshape(2, 1, width)
    fn_own, qkv_own = norm_qkv(x_own, g1, b1, qkv_weight, qvb)
    x_far, cot_send = tie(x_far, cot_send)
    cot_far = swap_sides(cot_send)
    fn_far, qkv_far = norm_qkv(x_far, g1, b1, qkv_weight, qvb)
    mixed, att, sn, probs = attend(
        qkv_own, qkv_far, x_own, x_far, ok_own, out_weight, row(out_bias), g2, b2
    )
    flat = lambda a: a.reshape(-1, width)
    slope, lo_own, lo_far, gy, dbg, keep1, send1 = mlp_up(
        info, inv, flat(sn), flat(att), cot_own, cot_far, up_weight, row(up_bias),
        down_weight, row(down_bias), shards, packed,
    )
    lo_back = swap_sides(lo_far)
    tiles = up_weight.shape[1] // width // 2
    back = lambda gs, gy, start: mlp_back(
        inv, gs, gy, slope, flat(sn), up_weight, down_weight, start, tiles, shards, packed
    )
    if packed:
        r1 = Reduction(keep1, send1, shards)
    gs, upa, keep2, send2 = back(None, gy, 0)
    if packed:
        sent = r1.step(upa)
        r2 = Reduction(keep2, send2, shards)
        gs, sent = tie(gs, sent)
    gs, upb, keep3, send3 = back(gs, gy, tiles)
    shape4 = (2, pairs, half, width)
    gy4, gs4 = gy.reshape(shape4), gs.reshape(shape4)
    pair_back = lambda pair, gs4: attend_back(
        pair, gs4, gy4, att, x_own, x_far, qkv_own, qkv_far, probs, qkv_weight, out_weight, g1, g2
    )
    if packed:
        sent = r1.step(upb), r2.step(upb)
        r3 = Reduction(keep3, send3, shards)
        gs4, _ = tie(gs4, sent)
    own0, far0, vec0, dqkv0, gb0 = pair_back(0, gs4)
    if packed:
        sent = r1.step(vec0), r2.step(vec0), r3.step(vec0)
        gs4, _ = tie(gs4, sent)
    own1, far1, vec1, dqkv1, gb1 = pair_back(1, gs4)
    if packed:
        sent = r1.step(vec1), r2.step(vec1), r3.step(vec1)
        dqkv1, _ = tie(dqkv1, sent)
    vec, keep4, send4 = weight_grads(
        inv, dqkv0, dqkv1, gb0, gb1, mixed, fn_own, fn_far, vec0, vec1, upa, upb, dbg, shards, packed
    )
    ig_back = swap_sides(jnp.stack([far0, far1]))
    ig_own = jnp.stack([own0, own1])

    def settle(own, back):
        own, back = own[:, :real], back[:, :real]
        return jnp.where(
            side == 0, jnp.concatenate([own, back]), jnp.concatenate([back, own])
        )

    layer_out = settle(lo_own, lo_back)

    if packed:
        r4 = Reduction(keep4, send4, shards)
        r2.step(vec), r3.step(vec), r4.step()
        rows = width // shards
        down_g = r1.result()
        r3.step(), r4.step()
        up_g = jnp.concatenate(
            [unpack_rows(r.result(), tiles, rows) for r in (r2, r3)], axis=1
        )
        r4.step(), r4.step()
        rest = r4.result()
        mats = unpack_rows(rest[:, :-LANES], 4, rows)
        qkv_g, out_g = mats[:, : 3 * width], mats[:, 3 * width :]
        vecs = rest[:, -LANES:]
        one = lambda i: vecs[i, :rows]
        ln1g, ln1b, outb, ln2g, ln2b, downb = (one(i) for i in range(6))
        qvg, upg = vecs[6, : 2 * rows], vecs[7, : 4 * rows]
    else:
        total = lambda v: lax.psum_scatter(v, AXES, scatter_dimension=0, tiled=True)
        up_all = jnp.concatenate([keep2, keep3], axis=1)
        down_g, up_g, qkv_g, out_g = total(keep1), total(up_all), total(keep4), total(send4)
        ln1g, ln1b, outb, ln2g, ln2b, downb = (total(vec[i]) for i in (0, 1, 4, 5, 6, 7))
        qvg, upg = total(vec[2:4].reshape(-1)), total(vec[8:12].reshape(-1))
    input_grad = settle(ig_own, ig_back)
    return (
        layer_out, input_grad, ln1g, ln1b, qkv_g, qvg, out_g, outb, ln2g, ln2b, up_g, upg,
        down_g, downb,
    )


def solution(mesh):
    rows3 = P("pairs", "mod", None)
    vec, mat = P(AXES), P(AXES, None)
    return jax.shard_map(
        on_device,
        mesh=mesh,
        in_specs=(rows3, P("pairs"), P("pairs", "mod")) + (P(),) * 12 + (rows3,),
        out_specs=(rows3, rows3, vec, vec, mat, vec, mat, vec, vec, vec, mat, vec, mat, vec),
        check_vma=False,
    )
```

```python
from functools import partial

import jax
import jax.numpy as jnp
import numpy as np
from jax import lax
from jax.experimental import pallas as pl
from jax.experimental.pallas import tpu as pltpu
from jax.sharding import PartitionSpec as P

HEAD_DIM = 64
TXT = 40
EPS = 1e-06
MASKED = -1e30
AXES = ("pairs", "mod")
BF16 = jnp.bfloat16
F32 = jnp.float32
LANES = 128
PAD = 4
MIB = 1 << 20

CORE_BIT = 2
ORDERS = ((4, 8, 1, 16), (8, 4, 1, 16))
EARLY = 4


def dot_nn(a, b):
    return jnp.dot(a, b, preferred_element_type=F32)


def dot_nt(a, b):
    return lax.dot_general(a, b, (((1,), (1,)), ((), ())), preferred_element_type=F32)


def dot_tn(a, b):
    return lax.dot_general(a, b, (((0,), (0,)), ((), ())), preferred_element_type=F32)


def norm_parts(v):
    center = v - jnp.mean(v, axis=-1, keepdims=True)
    rstd = lax.rsqrt(jnp.mean(center * center, axis=-1, keepdims=True) + EPS)
    return center * rstd, rstd


def norm_back(grad, unit, rstd, gain):
    d = grad * gain
    return rstd * (
        d
        - jnp.mean(d, axis=-1, keepdims=True)
        - unit * jnp.mean(d * unit, axis=-1, keepdims=True)
    )


def gelu_and_slope(v):
    phi = 0.5 + 0.5 * lax.erf(v * 0.7071067811865476)
    bell = jnp.exp2(v * v * -0.7213475204444817)
    return v * phi, phi + v * bell * 0.3989422804014327


def lane_block(i, size=LANES):
    return pl.ds(pl.multiple_of(i * size, LANES), size)


def spec_of(a):
    return pl.BlockSpec(a.shape, lambda *_: (0,) * len(a.shape))


def struct(shape, dtype):
    return jax.ShapeDtypeStruct(shape, dtype)


def kept(shape, dtype):
    return pltpu.HBM(shape, dtype)


def params_of(mib):
    return pltpu.CompilerParams(vmem_limit_bytes=mib * MIB)


def column_sums(value):
    return jnp.sum(value, axis=0, keepdims=True)


def wire_rows(left, inv, tall, out, shard):
    tall[...] = jnp.transpose(left.astype(F32))
    count = tall.shape[0] // shard

    def two(i, carry):
        rows = [
            tall[pl.ds(pl.multiple_of(inv[2 * i + k] * shard + 8 * g, 8), 8), :]
            for k in range(2)
            for g in range(shard // 8)
        ]
        at = pl.multiple_of(2 * shard * i, 2 * shard)
        out[pl.ds(at, 2 * shard), :] = jnp.concatenate(rows, axis=0).astype(BF16)
        return carry

    lax.fori_loop(0, count // 2, two, 0)


def own_rows(info, p, far, half):
    side = info[2] if far == 0 else 1 - info[2]
    real = half - PAD
    row = lax.broadcasted_iota(jnp.int32, (half, 1), 0)
    return row < jnp.minimum(TXT + info[p] - side * real, real)


def norm_qkv_kernel(x_ref, g_ref, b_ref, w_ref, qvb_ref, fn_ref, qkv_ref):
    j = pl.program_id(0)
    rows, width = fn_ref.shape[0] * fn_ref.shape[1], fn_ref.shape[2]

    @pl.when(j == 0)
    def _():
        unit, _ = norm_parts(x_ref[...].reshape(rows, width).astype(F32))
        fn_ref[...] = (unit * g_ref[...] + b_ref[...]).astype(BF16).reshape(fn_ref.shape)

    fn = fn_ref[...].reshape(rows, width)
    out = dot_nn(fn, w_ref[...]) + jnp.where(j == 1, 0.0, 1.0) * qvb_ref[0]
    qkv_ref[...] = out.astype(BF16).reshape(qkv_ref.shape)


def norm_qkv(x, gain, shift, weight, qv_bias):
    pairs, half, width = x.shape
    return pl.pallas_call(
        norm_qkv_kernel,
        grid=(3,),
        in_specs=[
            spec_of(x),
            spec_of(gain),
            spec_of(shift),
            pl.BlockSpec((width, width), lambda j: (0, j)),
            pl.BlockSpec((1, 1, width), lambda j: (j // 2, 0, 0)),
        ],
        out_specs=[spec_of(x), pl.BlockSpec((pairs, half, width), lambda j: (0, 0, j))],
        out_shape=[kept((pairs, half, width), BF16), kept((pairs, half, 3 * width), BF16)],
        compiler_params=params_of(24),
        cost_estimate=pl.CostEstimate(
            flops=6 * pairs * half * width * width,
            bytes_accessed=2 * (3 * width * width + 5 * pairs * half * width),
            transcendentals=0,
        ),
        name="norm_qkv",
    )(x, gain, shift, weight, qv_bias)


def stacked(block):
    first = lax.broadcasted_iota(jnp.int32, (1, LANES), 1) < HEAD_DIM
    zero = jnp.zeros((), block.dtype)
    return jnp.concatenate([jnp.where(first, block, zero), jnp.where(first, zero, block)], axis=0)


def attend_kernel(
    qo, qr, xo, xr, okrow, ow, ob, g2, b2, mixed_ref, att_ref, sn_ref, p_ref, mix_s
):
    half, width = xo.shape[1], xo.shape[2]
    rows = 2 * half
    ok8 = jnp.concatenate([okrow[0].astype(F32), jnp.zeros((7, rows), F32)], axis=0).astype(BF16)
    ok_col = dot_tn(ok8, jnp.ones((8, LANES), BF16))
    bias = jnp.where(ok_col > 0.5, 0.0, MASKED)[:, :1]

    def both(col):
        cols = lane_block(col)
        return jnp.concatenate([qo[0, :, cols], qr[0, :, cols]], axis=0)

    tiles = width // LANES

    def two_heads(hp, carry):
        q = both(hp) * jnp.asarray(HEAD_DIM**-0.5, BF16)
        s = dot_nt(stacked(both(tiles + hp)), q)
        probs = []
        for h in range(2):
            sh = s[h * rows : (h + 1) * rows, :] + bias
            e = jnp.exp(sh - jnp.max(sh, axis=0, keepdims=True))
            probs.append((e * (1.0 / column_sums(e))).astype(BF16))
        prob = jnp.concatenate(probs, axis=0)
        p_ref[0, hp] = prob
        mix_s[:, lane_block(hp)] = dot_tn(prob, stacked(both(2 * tiles + hp))).astype(BF16)
        return carry

    lax.fori_loop(0, tiles, two_heads, 0)
    mixed = mix_s[...]
    mixed_ref[...] = mixed.reshape(mixed_ref.shape)
    x = jnp.concatenate([xo[0], xr[0]], axis=0).astype(F32)
    att = x + dot_nn(mixed, ow[...]) + ob[...]
    att_ref[...] = att.reshape(att_ref.shape)
    unit, _ = norm_parts(att)
    sn_ref[...] = (unit * g2[...] + b2[...]).astype(BF16).reshape(sn_ref.shape)


def attend(qkv_own, qkv_far, x_own, x_far, okrow, out_weight, out_bias, gain, shift):
    pairs, half, width = x_own.shape
    tiles = width // LANES
    rows = 2 * half
    pair3 = lambda p: (p, 0, 0)
    rows4 = pl.BlockSpec((2, 1, half, width), lambda p: (0, p, 0, 0))
    return pl.pallas_call(
        attend_kernel,
        grid=(pairs,),
        in_specs=[
            pl.BlockSpec((1, half, 3 * width), pair3),
            pl.BlockSpec((1, half, 3 * width), pair3),
            pl.BlockSpec((1, half, width), pair3),
            pl.BlockSpec((1, half, width), pair3),
            pl.BlockSpec((1, 1, rows), pair3),
        ]
        + [spec_of(a) for a in (out_weight, out_bias, gain, shift)],
        out_specs=[
            rows4,
            rows4,
            rows4,
            pl.BlockSpec((1, tiles, 2 * rows, rows), lambda p: (p, 0, 0, 0)),
        ],
        out_shape=[
            kept((2, pairs, half, width), BF16),
            kept((2, pairs, half, width), F32),
            struct((2, pairs, half, width), BF16),
            kept((pairs, tiles, 2 * rows, rows), BF16),
        ],
        scratch_shapes=[pltpu.VMEM((rows, width), BF16)],
        compiler_params=params_of(32),
        cost_estimate=pl.CostEstimate(
            flops=pairs * 16 * tiles * rows * rows * LANES,
            bytes_accessed=2 * pairs * rows * width * 8 + 4 * pairs * tiles * rows * rows,
            transcendentals=2 * pairs * tiles * rows * rows,
        ),
        name="attend",
    )(qkv_own, qkv_far, x_own, x_far, okrow, out_weight, out_bias, gain, shift)


def mlp_up_kernel(
    info, place, sn, att, co, cr, up, upb, down, downb,
    slope_ref, own_ref, far_ref, gy_ref, dbg_ref, keep, send, acc, wbuf, sems, *, shard,
):
    j = pl.program_id(0)
    last = pl.num_programs(0) - 1
    pairs, half, width = co.shape
    tile = up.shape[1]

    @pl.when(j == 0)
    def _():
        for far, c in enumerate((co, cr)):
            for p in range(pairs):
                at = (far * pairs + p) * half
                gy_ref[at : at + half, :] = jnp.where(
                    own_rows(info, p, far, half), c[p].astype(F32), 0.0
                ).astype(BF16)
        dbg_ref[...] = column_sums(gy_ref[...].astype(F32))

    h, slope = gelu_and_slope(dot_nn(sn[...], up[...]) + upb[...])
    slope_ref[...] = slope.astype(BF16)
    h = h.astype(BF16)
    part = dot_nn(h, down[...])

    @pl.when(j == 0)
    def _():
        acc[...] = part

    @pl.when(j > 0)
    def _():
        acc[...] += part

    grad = dot_tn(h, gy_ref[...])
    if not shard:
        keep[...] = grad
        send[...] = jnp.zeros_like(send)
    else:
        count = tile // shard
        slot = lax.rem(j, 2)

        def copy_of(step, i, act):
            pos = place[step * count + i]
            src = wbuf.at[lax.rem(step, 2), pl.ds(i * shard, shard), :]
            n = keep.shape[0] // shard
            for ref, ours in ((keep, pos < n), (send, pos >= n)):

                @pl.when(ours)
                def _():
                    at = pl.multiple_of(lax.rem(pos, n) * shard, shard)
                    act(pltpu.make_async_copy(src, ref.at[pl.ds(at, shard), :], sems.at[lax.rem(step, 2), i]))

        @pl.when(j > 1)
        def _():
            for i in range(count):
                copy_of(j - 2, i, lambda c: c.wait())

        wbuf[slot] = grad.astype(BF16)
        for i in range(count):
            copy_of(j, i, lambda c: c.start())

    @pl.when(j == last)
    def _():
        final = att[...] + acc[...] + downb[...]
        for far, o in enumerate((own_ref, far_ref)):
            for p in range(pairs):
                at = (far * pairs + p) * half
                o[p] = jnp.where(
                    own_rows(info, p, far, half), final[at : at + half, :], 0.0
                ).astype(BF16)
        if shard:
            for step in (last - 1, last):
                for i in range(count):
                    copy_of(step, i, lambda c: c.wait())


def mlp_up(info, place, sn, att, cot_own, cot_far, up, up_bias, down, down_bias, shards, packed):
    pairs, half, width = cot_own.shape
    rows = 2 * pairs * half
    ff = up.shape[1]
    tile = width
    shard = ff // shards
    tiled = lambda j, *_: (j, 0)
    if packed:
        wire = [kept((ff // 2, width), BF16)] * 2
        wire_specs = [pl.BlockSpec(memory_space=pl.ANY)] * 2
        count = tile // shard
    else:
        wire = [struct((ff, width), F32), struct((8, LANES), F32)]
        wire_specs = [pl.BlockSpec((tile, width), tiled), spec_of(wire[1])]
        count = 1
    rows3 = kept((pairs, half, width), BF16)
    return pl.pallas_call(
        partial(mlp_up_kernel, shard=shard if packed else 0),
        grid_spec=pltpu.PrefetchScalarGridSpec(
            num_scalar_prefetch=2,
            grid=(ff // tile,),
            in_specs=[
                spec_of(sn),
                spec_of(att),
                spec_of(cot_own),
                spec_of(cot_far),
                pl.BlockSpec((width, tile), lambda j, *_: (0, j)),
                pl.BlockSpec((1, tile), lambda j, *_: (0, j)),
                pl.BlockSpec((tile, width), tiled),
                spec_of(down_bias),
            ],
            out_specs=[
                pl.BlockSpec((rows, tile), lambda j, *_: (0, j)),
                spec_of(rows3),
                spec_of(rows3),
                spec_of(sn),
                spec_of(down_bias),
            ]
            + wire_specs,
            scratch_shapes=[
                pltpu.VMEM((rows, width), F32),
                pltpu.VMEM((2, tile, width), BF16),
                pltpu.SemaphoreType.DMA((2, count)),
            ],
        ),
        out_shape=[struct((rows, ff), BF16), rows3, rows3, struct((rows, width), BF16), kept((1, width), F32)]
        + wire,
        compiler_params=params_of(40),
        cost_estimate=pl.CostEstimate(
            flops=6 * rows * width * ff, bytes_accessed=22 * MIB, transcendentals=2 * rows * ff
        ),
        name="mlp_up",
    )(info, place, sn, att, cot_own, cot_far, up, up_bias, down, down_bias)


def mlp_back_kernel(
    inv, gy, slope, sn, up, down, gs_ref, upb_ref, keep, send, tall, snt, wbuf, sems, *, shard
):
    j = pl.program_id(0)
    last = pl.num_programs(0) - 1
    gp = (dot_nt(gy[...], down[...]) * slope[...].astype(F32)).astype(BF16)
    upb_ref[...] = column_sums(gp.astype(F32))
    part = dot_nt(gp, up[...])

    @pl.when(j == 0)
    def _():
        gs_ref[...] = part

    @pl.when(j > 0)
    def _():
        gs_ref[...] += part

    if not shard:
        keep[...] = dot_tn(sn[...], gp)
        send[...] = jnp.zeros_like(send)
        return

    @pl.when(j == 0)
    def _():
        wire_rows(sn[...], inv, tall, snt, shard)

    n, tile = keep.shape[0], up.shape[1]

    def copies(step):
        slot = lax.rem(step, 2)
        cols = lane_block(step, tile)
        for i, ref in enumerate((keep, send)):
            yield pltpu.make_async_copy(
                wbuf.at[slot, pl.ds(i * n, n), :], ref.at[:, cols], sems.at[slot, i]
            )

    @pl.when(j > 1)
    def _():
        for c in copies(j - 2):
            c.wait()

    wbuf[lax.rem(j, 2)] = dot_nn(snt[...], gp).astype(BF16)
    for c in copies(j):
        c.start()

    @pl.when(j == last)
    def _():
        for step in (last - 1, last):
            for c in copies(step):
                c.wait()


def mlp_back(inv, gy, slope, sn, up, down, shards, packed):
    rows, width = gy.shape
    ff = up.shape[1]
    tile = width
    cols = lambda j, *_: (0, j)
    if packed:
        wire = [kept((width // 2, ff), BF16)] * 2
        wire_specs = [pl.BlockSpec(memory_space=pl.ANY)] * 2
    else:
        wire = [struct((width, ff), F32), struct((8, LANES), F32)]
        wire_specs = [pl.BlockSpec((width, tile), cols), spec_of(wire[1])]
    return pl.pallas_call(
        partial(mlp_back_kernel, shard=width // shards if packed else 0),
        grid_spec=pltpu.PrefetchScalarGridSpec(
            num_scalar_prefetch=1,
            grid=(ff // tile,),
            in_specs=[
                spec_of(gy),
                pl.BlockSpec((rows, tile), cols),
                spec_of(sn),
                pl.BlockSpec((width, tile), cols),
                pl.BlockSpec((tile, width), lambda j, *_: (j, 0)),
            ],
            out_specs=[spec_of(gy), pl.BlockSpec((1, tile), cols)] + wire_specs,
            scratch_shapes=[
                pltpu.VMEM((width, rows), F32),
                pltpu.VMEM((width, rows), BF16),
                pltpu.VMEM((2, width, tile), BF16),
                pltpu.SemaphoreType.DMA((2, 2)),
            ],
        ),
        out_shape=[struct((rows, width), F32), kept((1, ff), F32)] + wire,
        compiler_params=params_of(40),
        cost_estimate=pl.CostEstimate(
            flops=6 * rows * width * ff, bytes_accessed=20 * MIB, transcendentals=0
        ),
        name="mlp_back",
    )(inv, gy, slope, sn, up, down)


def heads_back(qo, qr, gm_ref, p_ref, dqkv, base, rows, hp0, count):
    first = lax.broadcasted_iota(jnp.int32, (1, LANES), 1) < HEAD_DIM
    tiles = gm_ref.shape[-1] // LANES
    scale = jnp.asarray(HEAD_DIM**-0.5, BF16)

    def both(col):
        cols = lane_block(col)
        return jnp.concatenate([qo[0, :, cols], qr[0, :, cols]], axis=0)

    def two_heads(i, carry):
        hp = hp0 + i
        gm = gm_ref[:, lane_block(hp)]
        dp = dot_nt(stacked(both(2 * tiles + hp)), gm)
        prob = p_ref[0, i]
        ds = []
        for h in range(2):
            dph = dp[h * rows : (h + 1) * rows, :]
            pf = prob[h * rows : (h + 1) * rows, :].astype(F32)
            ds.append((pf * (dph - column_sums(dph * pf))).astype(BF16))
        ds = jnp.concatenate(ds, axis=0)
        dv = dot_nn(prob, gm)
        dk = dot_nn(ds, both(hp) * scale)
        dq = dot_tn(ds, stacked(both(tiles + hp) * scale))
        pick = lambda d: jnp.where(first, d[:rows, :], d[rows:, :])
        for part, d in enumerate((dq, pick(dk), pick(dv))):
            dqkv[pl.ds(base, rows), lane_block(part * count + i)] = d.astype(BF16)
        return carry

    lax.fori_loop(0, count, two_heads, 0)


def wire_out(left_t, right, keep, send, at):
    n = keep.shape[0]
    grad = dot_nn(left_t, right).astype(BF16)
    keep[:, at : at + grad.shape[1]] = grad[:n]
    send[:, at : at + grad.shape[1]] = grad[n:]


def attend_back_kernel(
    inv, gs, gy, att, mixed, fno, fnr, qo, qr, p_ref, ow, g2,
    ga_ref, gm_ref, dqkv, fnt, vec_ref, keep, send, gbs, fns, mxs, tall, *, shard,
):
    pair = pl.program_id(0)
    half, width = fno.shape[1], fno.shape[2]
    rows = 2 * half

    @pl.when(pair == 0)
    def _():
        vec_ref[...] = jnp.zeros_like(vec_ref)

    grad_second = gs[...].reshape(rows, width)
    unit, rstd = norm_parts(att[...].reshape(rows, width))
    grad_att = gy[...].reshape(rows, width).astype(F32) + norm_back(
        grad_second, unit, rstd, g2[...]
    )
    ga_ref[0] = grad_att
    branch = grad_att.astype(BF16)
    for i, v in enumerate((branch.astype(F32), grad_second * unit, grad_second)):
        vec_ref[i : i + 1, :] += column_sums(v)
    base = pl.multiple_of(pair * rows, rows)
    gbs[pl.ds(base, rows), :] = branch
    gm_ref[0] = dot_nt(branch, ow[...]).astype(BF16)
    fns[pl.ds(base, half), :] = fno[0]
    fns[pl.ds(base + half, half), :] = fnr[0]
    mxs[pl.ds(base, rows), :] = mixed[...].reshape(rows, width)
    heads_back(qo, qr, gm_ref.at[0], p_ref, dqkv, base, rows, 0, EARLY)

    @pl.when(pair == pl.num_programs(0) - 1)
    def _():
        early = dqkv.shape[1]
        if not shard:
            keep[:, :early] = dot_tn(fns[...], dqkv[...])
            keep[:, early:] = dot_tn(mxs[...], gbs[...])
            fnt[...] = jnp.transpose(fns[...].astype(F32)).astype(BF16)
            send[...] = jnp.zeros_like(send)
            return
        wire_rows(mxs[...], inv, tall, fnt, shard)
        wire_out(fnt[...], gbs[...], keep, send, early)
        wire_rows(fns[...], inv, tall, fnt, shard)
        for at in range(0, early, width):
            wire_out(fnt[...], dqkv[:, at : at + width], keep, send, at)


def attend_back(
    inv, gs, gy, att, mixed, fn_own, fn_far, qkv_own, qkv_far, probs, out_weight, gain, shards, packed
):
    pairs, half, width = fn_own.shape
    rows = 2 * half
    early = 3 * EARLY * LANES
    pair3 = lambda p, *_: (p, 0, 0)
    rows4 = pl.BlockSpec((2, 1, half, width), lambda p, *_: (0, p, 0, 0))
    if packed:
        wire = [kept((width // 2, early + width), BF16)] * 2
    else:
        wire = [struct((width, early + width), F32), struct((8, LANES), F32)]
    outs = [
        struct((pairs * rows, early), BF16),
        struct((width, pairs * rows), BF16),
        kept((8, width), F32),
    ] + wire
    return pl.pallas_call(
        partial(attend_back_kernel, shard=width // shards if packed else 0),
        grid_spec=pltpu.PrefetchScalarGridSpec(
            num_scalar_prefetch=1,
            grid=(pairs,),
            in_specs=[
                rows4,
                rows4,
                rows4,
                rows4,
                pl.BlockSpec((1, half, width), pair3),
                pl.BlockSpec((1, half, width), pair3),
                pl.BlockSpec((1, half, 3 * width), pair3),
                pl.BlockSpec((1, half, 3 * width), pair3),
                pl.BlockSpec((1, EARLY, 2 * rows, rows), lambda p, *_: (p, 0, 0, 0)),
                spec_of(out_weight),
                spec_of(gain),
            ],
            out_specs=[
                pl.BlockSpec((1, rows, width), pair3),
                pl.BlockSpec((1, rows, width), pair3),
            ]
            + [spec_of(o) for o in outs],
            scratch_shapes=[
                pltpu.VMEM((pairs * rows, width), BF16),
                pltpu.VMEM((pairs * rows, width), BF16),
                pltpu.VMEM((pairs * rows, width), BF16),
                pltpu.VMEM((width, pairs * rows), F32),
            ],
        ),
        out_shape=[struct((pairs, rows, width), F32), struct((pairs, rows, width), BF16)] + outs,
        compiler_params=params_of(44),
        cost_estimate=pl.CostEstimate(
            flops=pairs * 32 * EARLY * rows * rows * LANES + 8 * pairs * rows * width * width,
            bytes_accessed=20 * MIB,
            transcendentals=0,
        ),
        name="attend_back",
    )(inv, gs, gy, att, mixed, fn_own, fn_far, qkv_own, qkv_far, probs, out_weight, gain)


def last_back_kernel(
    inv, qo, qr, p_ref, gm_ref, fnt, dqa, ga, xo, xr, w, g1, v2, upbg, dbg,
    own_ref, far_ref, vec_ref, keep, send, dqb, *, shard,
):
    pair = pl.program_id(0)
    half, width = xo.shape[1], xo.shape[2]
    rows = 2 * half
    tiles = width // LANES
    base = pl.multiple_of(pair * rows, rows)
    ca, cb = dqa.shape[1] // 3, dqb.shape[1] // 3

    @pl.when(pair == 0)
    def _():
        vec_ref[...] = jnp.zeros_like(vec_ref)
        vec_ref[4:7, :] = v2[0:3, :]
        vec_ref[7:8, :] = dbg[...]
        for i in range(4):
            vec_ref[8 + i : 9 + i, :] = upbg[:, i * width : (i + 1) * width]

    def add_vec(i, at, value):
        vec_ref[i : i + 1, at : at + value.shape[1]] += column_sums(value.astype(F32))

    heads_back(qo, qr, gm_ref.at[0], p_ref, dqb, base, rows, EARLY, tiles - EARLY)

    grad = None
    late = dqb[pl.ds(base, rows), :]
    for d, cols, at in ((dqa[...], ca, 0), (late, cb, ca)):
        for part in range(3):
            left = part * width + at
            term = dot_nt(d[:, part * cols : (part + 1) * cols], w[:, left : left + cols])
            grad = term if grad is None else grad + term
        add_vec(2, at, d[:, :cols])
        add_vec(3, at, d[:, 2 * cols :])
    unit, rstd = norm_parts(jnp.concatenate([xo[0], xr[0]], axis=0).astype(F32))
    add_vec(0, 0, grad * unit)
    add_vec(1, 0, grad)
    result = (ga[0] + norm_back(grad, unit, rstd, g1[...])).astype(BF16)
    own_ref[0] = result[:half]
    far_ref[0] = result[half:]

    @pl.when(pair == pl.num_programs(0) - 1)
    def _():
        if not shard:
            keep[...] = dot_nn(fnt[...], dqb[...])
            send[...] = jnp.zeros_like(send)
            return
        wire_out(fnt[...], dqb[...], keep, send, 0)
        v = vec_ref[...]
        small = jnp.concatenate([v[0:2], v[4:8], v[0:2]], axis=0)
        rowid = lax.broadcasted_iota(jnp.int32, (8, LANES), 0)
        per_q, per_u = width // (2 * shard), width // (4 * shard)
        none = jnp.zeros((shard - 8, LANES), F32)

        def piece(block, start):
            return pltpu.roll(block, lax.rem(width - start, width), 1)[:, :LANES]

        def block(i):
            a = piece(small, i * shard)
            b = piece(v[2:4], lax.rem(i, per_q) * 2 * shard)
            brow = jnp.where(i < per_q, b[0:1], b[1:2])
            c = piece(v[8:12], lax.rem(i, per_u) * 4 * shard)
            ci = lax.div(i, per_u)
            crow = jnp.where(
                ci == 0, c[0:1], jnp.where(ci == 1, c[1:2], jnp.where(ci == 2, c[2:3], c[3:4]))
            )
            return jnp.where(rowid < 6, a, jnp.where(rowid == 6, brow, crow))

        n = keep.shape[0] // shard
        right = keep.shape[1] - LANES

        def fill(p, carry):
            at = pl.ds(pl.multiple_of(2 * shard * p, 2 * shard), 2 * shard)
            for ref, first in ((keep, 0), (send, n)):
                two = [block(inv[first + 2 * p]), none, block(inv[first + 2 * p + 1]), none]
                ref[at, right:] = jnp.concatenate(two, axis=0).astype(BF16)
            return carry

        lax.fori_loop(0, n // 2, fill, 0)


def last_back(
    inv, qkv_own, qkv_far, probs, gm, fnt, dqa, ga, x_own, x_far, weight, gain, v2, upbg, dbg,
    shards, packed,
):
    pairs, rows, width = gm.shape
    half = rows // 2
    late = width // LANES - EARLY
    cols = 3 * late * LANES
    pair3 = lambda p, *_: (p, 0, 0)
    pair2 = lambda p, *_: (p, 0)
    if packed:
        wire = [kept((width // 2, cols + LANES), BF16)] * 2
    else:
        wire = [struct((width, cols), F32), struct((8, LANES), F32)]
    vec = kept((16, width), F32)
    return pl.pallas_call(
        partial(last_back_kernel, shard=width // shards if packed else 0),
        grid_spec=pltpu.PrefetchScalarGridSpec(
            num_scalar_prefetch=1,
            grid=(pairs,),
            in_specs=[
                pl.BlockSpec((1, half, 3 * width), pair3),
                pl.BlockSpec((1, half, 3 * width), pair3),
                pl.BlockSpec((1, late, 2 * rows, rows), lambda p, *_: (p, EARLY // late, 0, 0)),
                pl.BlockSpec((1, rows, width), pair3),
                spec_of(fnt),
                pl.BlockSpec((rows, dqa.shape[1]), pair2),
                pl.BlockSpec((1, rows, width), pair3),
                pl.BlockSpec((1, half, width), pair3),
                pl.BlockSpec((1, half, width), pair3),
            ]
            + [spec_of(a) for a in (weight, gain, v2, upbg, dbg)],
            out_specs=[
                pl.BlockSpec((1, half, width), pair3),
                pl.BlockSpec((1, half, width), pair3),
                spec_of(vec),
            ]
            + [spec_of(o) for o in wire],
            scratch_shapes=[pltpu.VMEM((pairs * rows, cols), BF16)],
        ),
        out_shape=[kept((pairs, half, width), BF16)] * 2 + [vec] + wire,
        compiler_params=params_of(36),
        cost_estimate=pl.CostEstimate(
            flops=pairs * 32 * late * rows * rows * LANES + 8 * pairs * rows * width * width,
            bytes_accessed=16 * MIB,
            transcendentals=0,
        ),
        name="last_back",
    )(inv, qkv_own, qkv_far, probs, gm, fnt, dqa, ga, x_own, x_far, weight, gain, v2, upbg, dbg)


def core_of(i):
    return 1 if i & CORE_BIT else 0


def shard_order(me, shards):
    half = shards // 2
    bits = half.bit_length() - 1
    tables = []
    for order in ORDERS:
        row = []
        for p in range(half):
            rel = 0
            for i, bit in enumerate(order):
                if p >> (bits - 1 - i) & 1:
                    rel |= bit
            row.append(rel)
        tables.append(row)
    both = []
    for core in range(2):
        row = tables[core] + [r | CORE_BIT for r in tables[1 - core]]
        both.append(row)
    both = np.array(both, np.int32)
    back = np.argsort(both, axis=1).astype(np.int32)
    core = jnp.where(me & CORE_BIT, 1, 0)
    rel = jnp.where(core == 0, jnp.asarray(both[0]), jnp.asarray(both[1]))
    ids = jnp.arange(shards, dtype=jnp.int32) ^ me
    hot = (ids[:, None] == jnp.arange(shards, dtype=jnp.int32)[None, :]).astype(jnp.int32)
    table = jnp.where(core == 0, jnp.asarray(back[0]), jnp.asarray(back[1]))
    return me ^ rel, jnp.sum(hot * table[None, :], axis=1)


def add_up(terms):
    total = terms[0].astype(F32)
    for t in terms[1:]:
        total = total + t.astype(F32)
    return total


def tie(*values):
    return lax.optimization_barrier(values)


class Reduction:
    def __init__(self, keep, send, shards):
        self.shards, self.stage, self.n = shards, 0, keep.shape[0]
        self.terms = [keep]
        self.incoming = lax.ppermute(send, AXES, [(i, i ^ CORE_BIT) for i in range(shards)])

    def hold(self, *others):
        self.incoming = after(self.incoming, *others)

    def step(self):
        self.terms.append(self.incoming)
        self.n //= 2
        out = add_up([t[self.n :] for t in self.terms]).astype(BF16)
        self.terms = [t[: self.n] for t in self.terms]
        route = [(i, i ^ ORDERS[core_of(i)][self.stage]) for i in range(self.shards)]
        self.incoming = lax.ppermute(out, AXES, route)
        self.stage += 1
        return out

    def result(self):
        return add_up(self.terms + [self.incoming])


def after(value, *others):
    return tie(value, *others)[0]


def swap_sides(block):
    return lax.ppermute(block, "mod", [(0, 1), (1, 0)])


def on_device(
    tokens, patch_counts, token_mask, ln1_gain, ln1_bias, qkv_weight, qv_bias, out_weight,
    out_bias, ln2_gain, ln2_bias, up_weight, up_bias, down_weight, down_bias, cotangent,
):
    shards = lax.axis_size("pairs") * lax.axis_size("mod")
    pairs_here, real, width = tokens.shape
    pairs = pairs_here // 2
    half = real + PAD
    rows = width // shards
    packed = shards == 32 and width % (8 * shards) == 0
    side = lax.axis_index("mod").astype(jnp.int32)
    me = lax.axis_index("pairs").astype(jnp.int32) * 2 + side
    ours = lambda a: jnp.where(side == 0, a[:pairs], a[pairs:])
    theirs = lambda a: jnp.where(side == 0, a[pairs:], a[:pairs])
    padded = lambda a: jnp.pad(a, ((0, 0), (0, PAD), (0, 0)))
    x_sent = theirs(tokens)
    x_raw = swap_sides(x_sent)
    row_ids = side * real + jnp.arange(real, dtype=jnp.int32)
    ok = jnp.logical_and(row_ids[None, :] < (TXT + patch_counts)[:, None], token_mask == 1)
    ok = ok.astype(BF16)
    ok_far = swap_sides(after(theirs(ok), x_sent))
    gap = jnp.zeros((pairs, PAD), BF16)
    ok_row = jnp.concatenate([ours(ok), gap, ok_far, gap], axis=1)[:, None, :]
    tokens, cotangent = tie(tokens, cotangent, x_sent)[:2]
    x_own = padded(ours(tokens))
    cot_own = padded(ours(cotangent))
    cot_sent = theirs(cotangent)

    counts = ours(patch_counts)
    info = jnp.concatenate([counts, side[None]])
    if packed:
        inv, place = shard_order(me, shards)
    else:
        inv = place = jnp.zeros((8,), jnp.int32)

    row = lambda v: v.reshape(1, -1)
    g1, b1, g2, b2 = row(ln1_gain), row(ln1_bias), row(ln2_gain), row(ln2_bias)
    qvb = qv_bias.reshape(2, 1, width)
    fn_own, qkv_own = norm_qkv(x_own, g1, b1, qkv_weight, qvb)
    x_raw, cot_sent, _ = tie(x_raw, cot_sent, fn_own)
    x_far = padded(x_raw)
    cot_far = padded(swap_sides(cot_sent))
    fn_far, qkv_far = norm_qkv(x_far, g1, b1, qkv_weight, qvb)
    mixed, att, sn, probs = attend(
        qkv_own, qkv_far, x_own, x_far, ok_row, out_weight, row(out_bias), g2, b2
    )
    flat = lambda a: a.reshape(-1, width)
    slope, lo_own, lo_far, gy, dbg, keep1, send1 = mlp_up(
        info, place, flat(sn), flat(att), cot_own, cot_far, up_weight, row(up_bias),
        down_weight, row(down_bias), shards, packed,
    )
    shape4 = (2, pairs, half, width)
    if packed:
        r1 = Reduction(keep1, send1, shards)
        inv = after(inv, r1.step())
    gs, upbg, keep2, send2 = mlp_back(inv, gy, slope, flat(sn), up_weight, down_weight, shards, packed)
    if packed:
        r1.hold(upbg)
        r2 = Reduction(keep2, after(send2, r1.step()), shards)
        inv = after(inv, r2.step())
    ga, gm, dqa, fnt, v2, keep3, send3 = attend_back(
        inv, gs.reshape(shape4), gy.reshape(shape4), att, mixed, fn_own, fn_far, qkv_own, qkv_far,
        probs, out_weight, g2, shards, packed,
    )
    if packed:
        r1.hold(v2)
        sent = r1.step()
        r2.hold(sent)
        sent = r2.step()
        r3 = Reduction(keep3, after(send3, sent), shards)
        inv = after(inv, r3.step())
    lo_back = swap_sides(after(lo_far, v2))
    ig_own, ig_far, vec, keep4, send4 = last_back(
        inv, qkv_own, qkv_far, probs, gm, fnt, dqa, ga, x_own, x_far, qkv_weight, g1, v2, upbg,
        dbg, shards, packed,
    )
    ig_back = swap_sides(ig_far)

    def settle(own, back):
        own, back = own[:, :real], back[:, :real]
        return jnp.where(
            side == 0, jnp.concatenate([own, back]), jnp.concatenate([back, own])
        )

    early = 3 * EARLY * LANES
    if packed:
        r1.hold(ig_own)
        r2.hold(r1.step())
        r3.hold(r2.step())
        r4 = Reduction(keep4, after(send4, r3.step()), shards)
        sent = r4.step()
        for r in (r2, r3, r4, r3, r4, r4):
            r.hold(sent)
            sent = r.step()
        layer_out = settle(lo_own, lo_back)
        down_g, up_g, mid, last = (r.result() for r in (r1, r2, r3, r4))
        vecs = last[:8, -LANES:]
        last = last[:, :-LANES]
        ln1g, ln1b, outb, ln2g, ln2b, downb = (vecs[i, :rows] for i in range(6))
        qvg, upg = vecs[6, : 2 * rows], vecs[7, : 4 * rows]
    else:
        layer_out = settle(lo_own, lo_back)
        total = lambda v: lax.psum_scatter(v, AXES, scatter_dimension=0, tiled=True)
        down_g, up_g, mid, last = total(keep1), total(keep2), total(keep3), total(keep4)
        ln1g, ln1b, outb, ln2g, ln2b, downb = (total(vec[i]) for i in (0, 1, 4, 5, 6, 7))
        qvg, upg = total(vec[2:4].reshape(-1)), total(vec[8:12].reshape(-1))
    out_g = mid[:, early:]
    ca, cb = early // 3, last.shape[1] // 3
    parts = []
    for i in range(3):
        parts += [mid[:, i * ca : (i + 1) * ca], last[:, i * cb : (i + 1) * cb]]
    qkv_g = jnp.concatenate(parts, axis=1)
    input_grad = settle(ig_own, ig_back)
    return (
        layer_out, input_grad, ln1g, ln1b, qkv_g, qvg, out_g, outb, ln2g, ln2b, up_g, upg,
        down_g, downb,
    )


def solution(mesh):
    rows3 = P("pairs", "mod", None)
    vec, mat = P(AXES), P(AXES, None)
    return jax.shard_map(
        on_device,
        mesh=mesh,
        in_specs=(rows3, P("pairs"), P("pairs", "mod")) + (P(),) * 12 + (rows3,),
        out_specs=(rows3, rows3, vec, vec, mat, vec, mat, vec, vec, vec, mat, vec, mat, vec),
        check_vma=False,
    )
```

```python
from functools import partial

import jax
import jax.numpy as jnp
import numpy as np
from jax import lax
from jax.experimental import pallas as pl
from jax.experimental.pallas import tpu as pltpu
from jax.sharding import PartitionSpec as P

HEAD_DIM = 64
TXT = 40
EPS = 1e-06
MASKED = -1e30
AXES = ("pairs", "mod")
BF16 = jnp.bfloat16
F32 = jnp.float32
LANES = 128
PAD = 4
MIB = 1 << 20
MLP_MIB = 34

CORE_BIT = 2
ORDERS = ((4, 8, 1, 16), (8, 4, 1, 16))
SIDE_STAGES = (2, 0, 1, 3)
SIDE = 512
EARLY = 4


def dot_nn(a, b):
    return jnp.dot(a, b, preferred_element_type=F32)


def dot_nt(a, b):
    return lax.dot_general(a, b, (((1,), (1,)), ((), ())), preferred_element_type=F32)


def dot_tn(a, b):
    return lax.dot_general(a, b, (((0,), (0,)), ((), ())), preferred_element_type=F32)


def norm_parts(v):
    center = v - jnp.mean(v, axis=-1, keepdims=True)
    rstd = lax.rsqrt(jnp.mean(center * center, axis=-1, keepdims=True) + EPS)
    return center * rstd, rstd


def norm_back(grad, unit, rstd, gain):
    d = grad * gain
    return rstd * (
        d
        - jnp.mean(d, axis=-1, keepdims=True)
        - unit * jnp.mean(d * unit, axis=-1, keepdims=True)
    )


def gelu_and_slope(v):
    phi = 0.5 + 0.5 * lax.erf(v * 0.7071067811865476)
    bell = jnp.exp2(v * v * -0.7213475204444817)
    return v * phi, phi + v * bell * 0.3989422804014327


def lane_block(i, size=LANES):
    return pl.ds(pl.multiple_of(i * size, LANES), size)


def spec_of(a):
    return pl.BlockSpec(a.shape, lambda *_: (0,) * len(a.shape))


def resident():
    return pl.BlockSpec(memory_space=pltpu.VMEM)


def struct(shape, dtype):
    return jax.ShapeDtypeStruct(shape, dtype)


def kept(shape, dtype):
    return pltpu.HBM(shape, dtype)


def params_of(mib):
    return pltpu.CompilerParams(vmem_limit_bytes=mib * MIB)


def column_sums(value):
    return jnp.sum(value, axis=0, keepdims=True)


def wire_rows(left, inv, tall, out, shard):
    tall[...] = jnp.transpose(left.astype(F32))
    count = tall.shape[0] // shard

    def two(i, carry):
        rows = [
            tall[pl.ds(pl.multiple_of(inv[2 * i + k] * shard + 8 * g, 8), 8), :]
            for k in range(2)
            for g in range(shard // 8)
        ]
        at = pl.multiple_of(2 * shard * i, 2 * shard)
        out[pl.ds(at, 2 * shard), :] = jnp.concatenate(rows, axis=0).astype(BF16)
        return carry

    lax.fori_loop(0, count // 2, two, 0)


def own_rows(info, p, far, half):
    side = info[2] if far == 0 else 1 - info[2]
    real = half - PAD
    row = lax.broadcasted_iota(jnp.int32, (half, 1), 0)
    return row < jnp.minimum(TXT + info[p] - side * real, real)


def norm_qkv_kernel(x_ref, g_ref, b_ref, w_ref, qvb_ref, fn_ref, qkv_ref):
    j = pl.program_id(0)
    rows, width = fn_ref.shape[0] * fn_ref.shape[1], fn_ref.shape[2]

    @pl.when(j == 0)
    def _():
        unit, _ = norm_parts(x_ref[...].reshape(rows, width).astype(F32))
        fn_ref[...] = (unit * g_ref[...] + b_ref[...]).astype(BF16).reshape(fn_ref.shape)

    fn = fn_ref[...].reshape(rows, width)
    out = dot_nn(fn, w_ref[...]) + jnp.where(j == 1, 0.0, 1.0) * qvb_ref[0]
    qkv_ref[...] = out.astype(BF16).reshape(qkv_ref.shape)


def norm_qkv(x, gain, shift, weight, qv_bias):
    pairs, half, width = x.shape
    return pl.pallas_call(
        norm_qkv_kernel,
        grid=(3,),
        in_specs=[
            spec_of(x),
            spec_of(gain),
            spec_of(shift),
            pl.BlockSpec((width, width), lambda j: (0, j)),
            pl.BlockSpec((1, 1, width), lambda j: (j // 2, 0, 0)),
        ],
        out_specs=[spec_of(x), pl.BlockSpec((pairs, half, width), lambda j: (0, 0, j))],
        out_shape=[kept((pairs, half, width), BF16), kept((pairs, half, 3 * width), BF16)],
        compiler_params=params_of(24),
        cost_estimate=pl.CostEstimate(
            flops=6 * pairs * half * width * width,
            bytes_accessed=2 * (3 * width * width + 5 * pairs * half * width),
            transcendentals=0,
        ),
        name="norm_qkv",
    )(x, gain, shift, weight, qv_bias)


def stacked(block):
    first = lax.broadcasted_iota(jnp.int32, (1, LANES), 1) < HEAD_DIM
    zero = jnp.zeros((), block.dtype)
    return jnp.concatenate([jnp.where(first, block, zero), jnp.where(first, zero, block)], axis=0)


def attend_kernel(
    qo, qr, xo, xr, okrow, ow, ob, g2, b2, mixed_ref, att_ref, sn_ref, p_ref, mix_s
):
    half, width = xo.shape[1], xo.shape[2]
    rows = 2 * half
    ok8 = jnp.concatenate([okrow[0].astype(F32), jnp.zeros((7, rows), F32)], axis=0).astype(BF16)
    ok_col = dot_tn(ok8, jnp.ones((8, LANES), BF16))
    bias = jnp.where(ok_col > 0.5, 0.0, MASKED)[:, :1]

    def both(col):
        cols = lane_block(col)
        return jnp.concatenate([qo[0, :, cols], qr[0, :, cols]], axis=0)

    tiles = width // LANES

    def two_heads(hp, carry):
        q = both(hp) * jnp.asarray(HEAD_DIM**-0.5, BF16)
        s = dot_nt(stacked(both(tiles + hp)), q)
        probs = []
        for h in range(2):
            sh = s[h * rows : (h + 1) * rows, :] + bias
            e = jnp.exp(sh - jnp.max(sh, axis=0, keepdims=True))
            probs.append((e * (1.0 / column_sums(e))).astype(BF16))
        prob = jnp.concatenate(probs, axis=0)
        p_ref[0, hp] = prob
        mix_s[:, lane_block(hp)] = dot_tn(prob, stacked(both(2 * tiles + hp))).astype(BF16)
        return carry

    lax.fori_loop(0, tiles, two_heads, 0)
    mixed = mix_s[...]
    mixed_ref[...] = mixed.reshape(mixed_ref.shape)
    x = jnp.concatenate([xo[0], xr[0]], axis=0).astype(F32)
    att = x + dot_nn(mixed, ow[...]) + ob[...]
    att_ref[...] = att.reshape(att_ref.shape)
    unit, _ = norm_parts(att)
    sn_ref[...] = (unit * g2[...] + b2[...]).astype(BF16).reshape(sn_ref.shape)


def attend(qkv_own, qkv_far, x_own, x_far, okrow, out_weight, out_bias, gain, shift):
    pairs, half, width = x_own.shape
    tiles = width // LANES
    rows = 2 * half
    pair3 = lambda p: (p, 0, 0)
    rows4 = pl.BlockSpec((2, 1, half, width), lambda p: (0, p, 0, 0))
    return pl.pallas_call(
        attend_kernel,
        grid=(pairs,),
        in_specs=[
            pl.BlockSpec((1, half, 3 * width), pair3),
            pl.BlockSpec((1, half, 3 * width), pair3),
            pl.BlockSpec((1, half, width), pair3),
            pl.BlockSpec((1, half, width), pair3),
            pl.BlockSpec((1, 1, rows), pair3),
        ]
        + [spec_of(a) for a in (out_weight, out_bias, gain, shift)],
        out_specs=[
            rows4,
            rows4,
            rows4,
            pl.BlockSpec((1, tiles, 2 * rows, rows), lambda p: (p, 0, 0, 0)),
        ],
        out_shape=[
            kept((2, pairs, half, width), BF16),
            kept((2, pairs, half, width), F32),
            struct((2, pairs, half, width), BF16),
            kept((pairs, tiles, 2 * rows, rows), BF16),
        ],
        scratch_shapes=[pltpu.VMEM((rows, width), BF16)],
        compiler_params=params_of(32),
        cost_estimate=pl.CostEstimate(
            flops=pairs * 16 * tiles * rows * rows * LANES,
            bytes_accessed=2 * pairs * rows * width * 8 + 4 * pairs * tiles * rows * rows,
            transcendentals=2 * pairs * tiles * rows * rows,
        ),
        name="attend",
    )(qkv_own, qkv_far, x_own, x_far, okrow, out_weight, out_bias, gain, shift)


def mlp_kernel(
    info, inv, place, sn, att_hbm, co, cr, up, upb, down, downb,
    own_ref, far_ref, gy_ref, dbg_ref, gs_ref, upbg_ref, keep, send,
    acc, att, down_buf, up_buf, tall, snt, att_sem, down_sems, up_sems, *, shards,
):
    j = pl.program_id(0)
    last = pl.num_programs(0) - 1
    pairs, half, width = co.shape
    tile = upb.shape[1]
    up_j = up[:, lane_block(j, tile)]
    down_j = down[pl.ds(pl.multiple_of(j * tile, tile), tile), :]
    att_copy = pltpu.make_async_copy(att_hbm, att, att_sem)
    slot = lax.rem(j, 2)
    tall_shard, wide_shard = down.shape[0] // shards if shards else 0, width // shards if shards else 0

    @pl.when(j == 0)
    def _():
        att_copy.start()
        for far, c in enumerate((co, cr)):
            for p in range(pairs):
                at = (far * pairs + p) * half
                gy_ref[at : at + half, :] = jnp.where(
                    own_rows(info, p, far, half), c[p].astype(F32), 0.0
                ).astype(BF16)
        dbg_ref[...] = column_sums(gy_ref[...].astype(F32))
        acc[...] = jnp.zeros_like(acc)
        gs_ref[...] = jnp.zeros_like(gs_ref)
        if shards:
            wire_rows(sn[...], inv, tall, snt, wide_shard)

    def down_copies(step, act):
        count = tile // tall_shard
        for i in range(count):
            pos = place[step * count + i]
            src = down_buf.at[lax.rem(step, 2), pl.ds(i * tall_shard, tall_shard), :]
            sem = down_sems.at[lax.rem(step, 2), i]
            n = 2 * keep.shape[0]
            for ref, ours in ((keep, pos < n), (send, pos >= n)):

                @pl.when(ours)
                def _():
                    q = lax.rem(pos, n)
                    at = pl.multiple_of(lax.rem(q, 2) * tall_shard, tall_shard)
                    act(pltpu.make_async_copy(src, ref.at[lax.div(q, 2), pl.ds(at, tall_shard), :], sem))

    def up_copies(step, act):
        n = keep.shape[0]
        rows = 2 * wide_shard
        at = pl.multiple_of(2 * tall_shard + step * rows, rows)
        for i, ref in enumerate((keep, send)):
            src = up_buf.at[lax.rem(step, 2), pl.ds(i * n, n), :, :]
            act(pltpu.make_async_copy(src, ref.at[:, pl.ds(at, rows), :], up_sems.at[lax.rem(step, 2), i]))

    if shards:

        @pl.when(j > 1)
        def _():
            down_copies(j - 2, lambda c: c.wait())
            up_copies(j - 2, lambda c: c.wait())

    h, slope = gelu_and_slope(dot_nn(sn[...], up_j) + upb[...])
    h = h.astype(BF16)
    acc[...] += dot_nn(h, down_j)
    gp = (dot_nt(gy_ref[...], down_j) * slope).astype(BF16)
    upbg_ref[...] = column_sums(gp.astype(F32))
    gs_ref[...] += dot_nt(gp, up_j)
    if not shards:
        keep[...] = dot_tn(h, gy_ref[...])
        send[...] = dot_tn(sn[...], gp)
    else:
        down_buf[slot] = dot_tn(h, gy_ref[...]).astype(BF16)
        down_copies(j, lambda c: c.start())
        up_buf[slot] = dot_nn(snt[...], gp).astype(BF16).reshape(up_buf.shape[1:])
        up_copies(j, lambda c: c.start())

    @pl.when(j == last)
    def _():
        att_copy.wait()
        final = att[...] + acc[...] + downb[...]
        for far, o in enumerate((own_ref, far_ref)):
            for p in range(pairs):
                at = (far * pairs + p) * half
                o[p] = jnp.where(
                    own_rows(info, p, far, half), final[at : at + half, :], 0.0
                ).astype(BF16)
        if shards:
            for step in (last - 1, last):
                down_copies(step, lambda c: c.wait())
                up_copies(step, lambda c: c.wait())


def mlp(info, inv, place, sn, att, cot_own, cot_far, up, up_bias, down, down_bias, shards):
    pairs, half, width = cot_own.shape
    rows = 2 * pairs * half
    ff = up.shape[1]
    tile = width
    cols = lambda j, *_: (0, j)
    if shards:
        wire = [kept((shards // 4, 4 * ff // shards, width), BF16)] * 2
        wire_specs = [pl.BlockSpec(memory_space=pl.ANY)] * 2
        blocks, count = (shards // 2, 2 * width // shards), tile * shards // ff
    else:
        wire = [struct((ff, width), F32), struct((width, ff), F32)]
        wire_specs = [pl.BlockSpec((tile, width), lambda j, *_: (j, 0)), pl.BlockSpec((width, tile), cols)]
        blocks, count = (width // 16, 16), 1
    rows3 = kept((pairs, half, width), BF16)
    return pl.pallas_call(
        partial(mlp_kernel, shards=shards),
        grid_spec=pltpu.PrefetchScalarGridSpec(
            num_scalar_prefetch=3,
            grid=(ff // tile,),
            in_specs=[
                spec_of(sn),
                pl.BlockSpec(memory_space=pl.ANY),
                spec_of(cot_own),
                spec_of(cot_far),
                resident(),
                pl.BlockSpec((1, tile), cols),
                resident(),
                spec_of(down_bias),
            ],
            out_specs=[
                spec_of(rows3),
                spec_of(rows3),
                spec_of(sn),
                spec_of(down_bias),
                spec_of(sn),
                pl.BlockSpec((1, tile), cols),
            ]
            + wire_specs,
            scratch_shapes=[
                pltpu.VMEM((rows, width), F32),
                pltpu.VMEM((rows, width), F32),
                pltpu.VMEM((2, tile, width), BF16),
                pltpu.VMEM((2,) + blocks + (tile,), BF16),
                pltpu.VMEM((width, rows), F32),
                pltpu.VMEM((width, rows), BF16),
                pltpu.SemaphoreType.DMA,
                pltpu.SemaphoreType.DMA((2, count)),
                pltpu.SemaphoreType.DMA((2, 2)),
            ],
        ),
        out_shape=[
            rows3,
            rows3,
            struct((rows, width), BF16),
            kept((1, width), F32),
            struct((rows, width), F32),
            kept((1, ff), F32),
        ]
        + wire,
        compiler_params=params_of(MLP_MIB if shards else 56),
        cost_estimate=pl.CostEstimate(
            flops=12 * rows * width * ff, bytes_accessed=24 * MIB, transcendentals=2 * rows * ff
        ),
        name="mlp",
    )(info, inv, place, sn, att, cot_own, cot_far, up, up_bias, down, down_bias)


def heads_back(qo, qr, gm_ref, p_ref, dqkv, base, rows, hp0, count):
    first = lax.broadcasted_iota(jnp.int32, (1, LANES), 1) < HEAD_DIM
    tiles = gm_ref.shape[-1] // LANES
    scale = jnp.asarray(HEAD_DIM**-0.5, BF16)

    def both(col):
        cols = lane_block(col)
        return jnp.concatenate([qo[0, :, cols], qr[0, :, cols]], axis=0)

    def two_heads(i, carry):
        hp = hp0 + i
        gm = gm_ref[:, lane_block(hp)]
        dp = dot_nt(stacked(both(2 * tiles + hp)), gm)
        prob = p_ref[0, i]
        ds = []
        for h in range(2):
            dph = dp[h * rows : (h + 1) * rows, :]
            pf = prob[h * rows : (h + 1) * rows, :].astype(F32)
            ds.append((pf * (dph - column_sums(dph * pf))).astype(BF16))
        ds = jnp.concatenate(ds, axis=0)
        dv = dot_nn(prob, gm)
        dk = dot_nn(ds, both(hp) * scale)
        dq = dot_tn(ds, stacked(both(tiles + hp) * scale))
        pick = lambda d: jnp.where(first, d[:rows, :], d[rows:, :])
        for part, d in enumerate((dq, pick(dk), pick(dv))):
            dqkv[pl.ds(base, rows), lane_block(part * count + i)] = d.astype(BF16)
        return carry

    lax.fori_loop(0, count, two_heads, 0)


def wire_out(left_t, right, keep, send, at):
    n = keep.shape[0]
    grad = dot_nn(left_t, right).astype(BF16)
    keep[:, at : at + grad.shape[1]] = grad[:n]
    send[:, at : at + grad.shape[1]] = grad[n:]


def second_back_kernel(gs, gy, att, ow, g2, ga_ref, br_ref, gm_ref, vec_ref):
    rows, width = gm_ref.shape[1], gm_ref.shape[2]

    @pl.when(pl.program_id(0) == 0)
    def _():
        vec_ref[...] = jnp.zeros_like(vec_ref)

    grad_second = gs[...].reshape(rows, width)
    unit, rstd = norm_parts(att[...].reshape(rows, width))
    grad_att = gy[...].reshape(rows, width).astype(F32) + norm_back(
        grad_second, unit, rstd, g2[...]
    )
    ga_ref[0] = grad_att
    branch = grad_att.astype(BF16)
    br_ref[0] = branch
    gm_ref[0] = dot_nt(branch, ow[...]).astype(BF16)
    for i, v in enumerate((branch.astype(F32), grad_second * unit, grad_second)):
        vec_ref[i : i + 1, :] += column_sums(v)


def second_back(gs, gy, att, out_weight, gain):
    _, pairs, half, width = gs.shape
    rows = 2 * half
    rows4 = pl.BlockSpec((2, 1, half, width), lambda p: (0, p, 0, 0))
    rows3 = pl.BlockSpec((1, rows, width), lambda p: (p, 0, 0))
    vec = kept((8, width), F32)
    return pl.pallas_call(
        second_back_kernel,
        grid=(pairs,),
        in_specs=[rows4, rows4, rows4, spec_of(out_weight), spec_of(gain)],
        out_specs=[rows3, rows3, rows3, spec_of(vec)],
        out_shape=[
            kept((pairs, rows, width), F32),
            struct((pairs, rows, width), BF16),
            struct((pairs, rows, width), BF16),
            vec,
        ],
        compiler_params=params_of(24),
        cost_estimate=pl.CostEstimate(
            flops=2 * pairs * rows * width * width, bytes_accessed=10 * MIB, transcendentals=0
        ),
        name="second_back",
    )(gs, gy, att, out_weight, gain)


def attend_back_kernel(
    inv, br, mixed, fno, fnr, qo, qr, p_ref, gm_ref, dqkv, fnt, tok_ref, keep, send, gbs, fns, mxs, tall,
    *, shard,
):
    pair = pl.program_id(0)
    half, width = fno.shape[1], fno.shape[2]
    rows = 2 * half
    base = pl.multiple_of(pair * rows, rows)
    tok_ref[...] = jnp.zeros_like(tok_ref)
    gbs[pl.ds(base, rows), :] = br[0]
    fns[pl.ds(base, half), :] = fno[0]
    fns[pl.ds(base + half, half), :] = fnr[0]
    mxs[pl.ds(base, rows), :] = mixed[...].reshape(rows, width)
    heads_back(qo, qr, gm_ref.at[0], p_ref, dqkv, base, rows, 0, EARLY)

    @pl.when(pair == pl.num_programs(0) - 1)
    def _():
        early = dqkv.shape[1]
        if not shard:
            keep[:, :early] = dot_tn(fns[...], dqkv[...])
            keep[:, early:] = dot_tn(mxs[...], gbs[...])
            fnt[...] = jnp.transpose(fns[...].astype(F32)).astype(BF16)
            send[...] = jnp.zeros_like(send)
            return
        wire_rows(mxs[...], inv, tall, fnt, shard)
        wire_out(fnt[...], gbs[...], keep, send, early)
        wire_rows(fns[...], inv, tall, fnt, shard)
        for at in range(0, early, width):
            wire_out(fnt[...], dqkv[:, at : at + width], keep, send, at)


def attend_back(
    inv, branch, mixed, fn_own, fn_far, qkv_own, qkv_far, probs, gm, shards, packed
):
    pairs, half, width = fn_own.shape
    rows = 2 * half
    early = 3 * EARLY * LANES
    pair3 = lambda p, *_: (p, 0, 0)
    rows4 = pl.BlockSpec((2, 1, half, width), lambda p, *_: (0, p, 0, 0))
    if packed:
        wire = [kept((width // 2, early + width), BF16)] * 2
    else:
        wire = [struct((width, early + width), F32), struct((8, LANES), F32)]
    outs = [
        struct((pairs * rows, early), BF16),
        struct((width, pairs * rows), BF16),
        kept((8, LANES), F32),
    ] + wire
    return pl.pallas_call(
        partial(attend_back_kernel, shard=width // shards if packed else 0),
        grid_spec=pltpu.PrefetchScalarGridSpec(
            num_scalar_prefetch=1,
            grid=(pairs,),
            in_specs=[
                pl.BlockSpec((1, rows, width), pair3),
                rows4,
                pl.BlockSpec((1, half, width), pair3),
                pl.BlockSpec((1, half, width), pair3),
                pl.BlockSpec((1, half, 3 * width), pair3),
                pl.BlockSpec((1, half, 3 * width), pair3),
                pl.BlockSpec((1, EARLY, 2 * rows, rows), lambda p, *_: (p, 0, 0, 0)),
                pl.BlockSpec((1, rows, width), pair3),
            ],
            out_specs=[spec_of(o) for o in outs],
            scratch_shapes=[
                pltpu.VMEM((pairs * rows, width), BF16),
                pltpu.VMEM((pairs * rows, width), BF16),
                pltpu.VMEM((pairs * rows, width), BF16),
                pltpu.VMEM((width, pairs * rows), F32),
            ],
        ),
        out_shape=outs,
        compiler_params=params_of(40 if packed else 50),
        cost_estimate=pl.CostEstimate(
            flops=pairs * 32 * EARLY * rows * rows * LANES + 6 * pairs * rows * width * width,
            bytes_accessed=16 * MIB,
            transcendentals=0,
        ),
        name="attend_back",
    )(inv, branch, mixed, fn_own, fn_far, qkv_own, qkv_far, probs, gm)


def last_back_kernel(
    inv, qo, qr, p_ref, gm_ref, fnt, dqa, ga, xo, xr, w, g1, v2, upbg, dbg,
    own_ref, far_ref, vec_ref, keep, send, dqb, *, shard,
):
    pair = pl.program_id(0)
    half, width = xo.shape[1], xo.shape[2]
    rows = 2 * half
    tiles = width // LANES
    base = pl.multiple_of(pair * rows, rows)
    ca, cb = dqa.shape[1] // 3, dqb.shape[1] // 3

    @pl.when(pair == 0)
    def _():
        vec_ref[...] = jnp.zeros_like(vec_ref)
        vec_ref[4:7, :] = v2[0:3, :]
        vec_ref[7:8, :] = dbg[...]
        for i in range(4):
            vec_ref[8 + i : 9 + i, :] = upbg[:, i * width : (i + 1) * width]

    def add_vec(i, at, value):
        vec_ref[i : i + 1, at : at + value.shape[1]] += column_sums(value.astype(F32))

    heads_back(qo, qr, gm_ref.at[0], p_ref, dqb, base, rows, EARLY, tiles - EARLY)

    grad = None
    late = dqb[pl.ds(base, rows), :]
    for d, cols, at in ((dqa[...], ca, 0), (late, cb, ca)):
        for part in range(3):
            left = part * width + at
            term = dot_nt(d[:, part * cols : (part + 1) * cols], w[:, left : left + cols])
            grad = term if grad is None else grad + term
        add_vec(2, at, d[:, :cols])
        add_vec(3, at, d[:, 2 * cols :])
    unit, rstd = norm_parts(jnp.concatenate([xo[0], xr[0]], axis=0).astype(F32))
    add_vec(0, 0, grad * unit)
    add_vec(1, 0, grad)
    result = (ga[0] + norm_back(grad, unit, rstd, g1[...])).astype(BF16)
    own_ref[0] = result[:half]
    far_ref[0] = result[half:]

    @pl.when(pair == pl.num_programs(0) - 1)
    def _():
        if not shard:
            keep[...] = dot_nn(fnt[...], dqb[...])
            send[...] = jnp.zeros_like(send)
            return
        wire_out(fnt[...], dqb[...], keep, send, 0)
        v = vec_ref[...]
        small = jnp.concatenate([v[0:2], v[4:8], v[0:2]], axis=0)
        rowid = lax.broadcasted_iota(jnp.int32, (8, LANES), 0)
        per_q, per_u = width // (2 * shard), width // (4 * shard)
        none = jnp.zeros((shard - 8, LANES), F32)

        def piece(block, start):
            return pltpu.roll(block, lax.rem(width - start, width), 1)[:, :LANES]

        def block(i):
            a = piece(small, i * shard)
            b = piece(v[2:4], lax.rem(i, per_q) * 2 * shard)
            brow = jnp.where(i < per_q, b[0:1], b[1:2])
            c = piece(v[8:12], lax.rem(i, per_u) * 4 * shard)
            ci = lax.div(i, per_u)
            crow = jnp.where(
                ci == 0, c[0:1], jnp.where(ci == 1, c[1:2], jnp.where(ci == 2, c[2:3], c[3:4]))
            )
            return jnp.where(rowid < 6, a, jnp.where(rowid == 6, brow, crow))

        n = keep.shape[0] // shard
        right = keep.shape[1] - LANES

        def fill(p, carry):
            at = pl.ds(pl.multiple_of(2 * shard * p, 2 * shard), 2 * shard)
            for ref, first in ((keep, 0), (send, n)):
                two = [block(inv[first + 2 * p]), none, block(inv[first + 2 * p + 1]), none]
                ref[at, right:] = jnp.concatenate(two, axis=0).astype(BF16)
            return carry

        lax.fori_loop(0, n // 2, fill, 0)


def last_back(
    inv, qkv_own, qkv_far, probs, gm, fnt, dqa, ga, x_own, x_far, weight, gain, v2, upbg, dbg,
    shards, packed,
):
    pairs, rows, width = gm.shape
    half = rows // 2
    late = width // LANES - EARLY
    cols = 3 * late * LANES
    pair3 = lambda p, *_: (p, 0, 0)
    pair2 = lambda p, *_: (p, 0)
    if packed:
        wire = [kept((width // 2, cols + LANES), BF16)] * 2
    else:
        wire = [struct((width, cols), F32), struct((8, LANES), F32)]
    vec = kept((16, width), F32)
    return pl.pallas_call(
        partial(last_back_kernel, shard=width // shards if packed else 0),
        grid_spec=pltpu.PrefetchScalarGridSpec(
            num_scalar_prefetch=1,
            grid=(pairs,),
            in_specs=[
                pl.BlockSpec((1, half, 3 * width), pair3),
                pl.BlockSpec((1, half, 3 * width), pair3),
                pl.BlockSpec((1, late, 2 * rows, rows), lambda p, *_: (p, EARLY // late, 0, 0)),
                pl.BlockSpec((1, rows, width), pair3),
                spec_of(fnt),
                pl.BlockSpec((rows, dqa.shape[1]), pair2),
                pl.BlockSpec((1, rows, width), pair3),
                pl.BlockSpec((1, half, width), pair3),
                pl.BlockSpec((1, half, width), pair3),
            ]
            + [spec_of(a) for a in (weight, gain, v2, upbg, dbg)],
            out_specs=[
                pl.BlockSpec((1, half, width), pair3),
                pl.BlockSpec((1, half, width), pair3),
                spec_of(vec),
            ]
            + [spec_of(o) for o in wire],
            scratch_shapes=[pltpu.VMEM((pairs * rows, cols), BF16)],
        ),
        out_shape=[kept((pairs, half, width), BF16)] * 2 + [vec] + wire,
        compiler_params=params_of(36),
        cost_estimate=pl.CostEstimate(
            flops=pairs * 32 * late * rows * rows * LANES + 8 * pairs * rows * width * width,
            bytes_accessed=16 * MIB,
            transcendentals=0,
        ),
        name="last_back",
    )(inv, qkv_own, qkv_far, probs, gm, fnt, dqa, ga, x_own, x_far, weight, gain, v2, upbg, dbg)


def core_of(i):
    return 1 if i & CORE_BIT else 0


def shard_order(me, shards):
    half = shards // 2
    bits = half.bit_length() - 1
    tables = []
    for order in ORDERS:
        row = []
        for p in range(half):
            rel = 0
            for i, bit in enumerate(order):
                if p >> (bits - 1 - i) & 1:
                    rel |= bit
            row.append(rel)
        tables.append(row)
    both = []
    for core in range(2):
        row = tables[core] + [r | CORE_BIT for r in tables[1 - core]]
        both.append(row)
    both = np.array(both, np.int32)
    back = np.argsort(both, axis=1).astype(np.int32)
    core = jnp.where(me & CORE_BIT, 1, 0)
    rel = jnp.where(core == 0, jnp.asarray(both[0]), jnp.asarray(both[1]))
    ids = jnp.arange(shards, dtype=jnp.int32) ^ me
    hot = (ids[:, None] == jnp.arange(shards, dtype=jnp.int32)[None, :]).astype(jnp.int32)
    table = jnp.where(core == 0, jnp.asarray(back[0]), jnp.asarray(back[1]))
    return me ^ rel, jnp.sum(hot * table[None, :], axis=1)


def add_up(terms):
    total = terms[0].astype(F32)
    for t in terms[1:]:
        total = total + t.astype(F32)
    return total


def tie(*values):
    return lax.optimization_barrier(values)


def exchange(block, stage, shards):
    bits = [CORE_BIT if stage is None else ORDERS[core_of(i)][stage] for i in range(shards)]
    return lax.ppermute(block, AXES, [(i, i ^ bit) for i, bit in enumerate(bits)])


def halves(block, axis):
    if axis < 3:
        return tuple(lax.slice_in_dim(block, i, i + 1, axis=axis) for i in range(2))
    return block[0, 0, 0, 0], block[0, 0, 0, 1]


class Reduction:
    def __init__(self, terms, shards, stages=(0, 1, 2, 3)):
        self.terms, self.shards, self.stages, self.done = terms, shards, stages, 0
        self.incoming, self.came = None, []

    def hold(self, *others):
        self.incoming = after(self.incoming, *others)

    def fold(self):
        if self.incoming is not None:
            self.terms.append(self.incoming)
            self.came.append(self.incoming)
            self.incoming = None

    def parts(self):
        self.fold()
        stage = self.stages[self.done]
        self.done += 1
        pieces = [halves(t, stage) for t in self.terms]
        self.terms = [p[0] for p in pieces]
        return add_up([p[1] for p in pieces]).astype(BF16)

    def step(self):
        stage = self.stages[self.done]
        out = self.parts()
        self.incoming = exchange(out, stage, self.shards)
        return out

    def result(self):
        self.fold()
        return add_up(self.terms)


def part_pairs_kernel(keep, got, p1, p2, p3, q1, q2, q3, mine, sent, *, tall, short):
    take = lambda ref: ref[...].reshape(ref.shape[-2:]).astype(F32)
    wide = take(keep) + take(got)
    left = wide[:, :SIDE] + take(p1) + take(p2) + take(p3)
    right = wide[:, SIDE:] + take(q1) + take(q2) + take(q3)
    for cols, block in ((slice(0, SIDE), left), (slice(SIDE, wide.shape[1]), right)):
        mine[:tall, cols] = block[:tall]
        theirs = [block[tall : 2 * tall]]
        for at in range(2 * tall, block.shape[0], 2 * short):
            to = tall + (at - 2 * tall) // 2
            mine[to : to + short, cols] = block[at : at + short]
            theirs.append(block[at + short : at + 2 * short])
        sent[:, cols] = jnp.concatenate(theirs, axis=0).astype(BF16)


def part_pairs(keep, got, left, right, tall, short):
    rows, width = keep.shape[-2], keep.shape[-1]
    first = lambda a: pl.BlockSpec(
        (1,) * (len(a.shape) - 2) + a.shape[-2:], lambda i: (0,) * len(a.shape)
    )
    args = (keep, got, *left, *right)
    outs = [struct((rows // 2, width), F32), struct((rows // 2, width), BF16)]
    return pl.pallas_call(
        partial(part_pairs_kernel, tall=tall, short=short),
        grid=(1,),
        in_specs=[first(a) for a in args],
        out_specs=[spec_of(o) for o in outs],
        out_shape=outs,
        cost_estimate=pl.CostEstimate(flops=0, bytes_accessed=4 * MIB, transcendentals=0),
        name="part_pairs",
    )(*args)


def finish_pair_kernel(mine, got, down_ref, up_ref):
    total = mine[...] + got[...].astype(F32)
    tall, short, width = down_ref.shape[0], up_ref.shape[0], total.shape[1]
    down_ref[...] = total[:tall]
    for i in range(up_ref.shape[1] // width):
        at = tall + i * short
        up_ref[:, i * width : (i + 1) * width] = total[at : at + short]


def finish_pair(mine, got, tall, short):
    width = mine.shape[1]
    outs = [
        struct((tall, width), F32),
        struct((short, (mine.shape[0] - tall) // short * width), F32),
    ]
    return pl.pallas_call(
        finish_pair_kernel,
        grid=(1,),
        in_specs=[spec_of(mine), spec_of(got)],
        out_specs=[spec_of(o) for o in outs],
        out_shape=outs,
        cost_estimate=pl.CostEstimate(flops=0, bytes_accessed=2 * MIB, transcendentals=0),
        name="finish_pair",
    )(mine, got)


def by_bits(block, shards):
    return block.reshape(2, 2, 2, 2, block.shape[0] // (shards // 2), block.shape[1])


def after(value, *others):
    return tie(value, *others)[0]


def swap_sides(block):
    return lax.ppermute(block, "mod", [(0, 1), (1, 0)])


def on_device(
    tokens, patch_counts, token_mask, ln1_gain, ln1_bias, qkv_weight, qv_bias, out_weight,
    out_bias, ln2_gain, ln2_bias, up_weight, up_bias, down_weight, down_bias, cotangent,
):
    shards = lax.axis_size("pairs") * lax.axis_size("mod")
    pairs_here, real, width = tokens.shape
    pairs = pairs_here // 2
    half = real + PAD
    rows = width // shards
    packed = shards == 32 and width % (8 * shards) == 0
    side = lax.axis_index("mod").astype(jnp.int32)
    me = lax.axis_index("pairs").astype(jnp.int32) * 2 + side
    ours = lambda a: jnp.where(side == 0, a[:pairs], a[pairs:])
    theirs = lambda a: jnp.where(side == 0, a[pairs:], a[:pairs])
    padded = lambda a: jnp.pad(a, ((0, 0), (0, PAD), (0, 0)))
    x_sent = theirs(tokens)
    x_raw = swap_sides(x_sent)
    row_ids = side * real + jnp.arange(real, dtype=jnp.int32)
    ok = jnp.logical_and(row_ids[None, :] < (TXT + patch_counts)[:, None], token_mask == 1)
    ok = ok.astype(BF16)
    ok_far = swap_sides(after(theirs(ok), x_sent))
    gap = jnp.zeros((pairs, PAD), BF16)
    ok_row = jnp.concatenate([ours(ok), gap, ok_far, gap], axis=1)[:, None, :]
    tokens, cotangent = tie(tokens, cotangent, x_sent)[:2]
    x_own = padded(ours(tokens))
    cot_own = padded(ours(cotangent))
    cot_sent = theirs(cotangent)

    counts = ours(patch_counts)
    info = jnp.concatenate([counts, side[None]])
    if packed:
        inv, place = shard_order(me, shards)
    else:
        inv = place = jnp.zeros((8,), jnp.int32)

    row = lambda v: v.reshape(1, -1)
    g1, b1, g2, b2 = row(ln1_gain), row(ln1_bias), row(ln2_gain), row(ln2_bias)
    qvb = qv_bias.reshape(2, 1, width)
    fn_own, qkv_own = norm_qkv(x_own, g1, b1, qkv_weight, qvb)
    x_raw, cot_sent, _ = tie(x_raw, cot_sent, fn_own)
    x_far = padded(x_raw)
    cot_far = padded(swap_sides(cot_sent))
    fn_far, qkv_far = norm_qkv(x_far, g1, b1, qkv_weight, qvb)
    mixed, att, sn, probs = attend(
        qkv_own, qkv_far, x_own, x_far, ok_row, out_weight, row(out_bias), g2, b2
    )
    flat = lambda a: a.reshape(-1, width)
    tall = down_weight.shape[0] // shards
    tiles = up_weight.shape[1] // width
    lo_own, lo_far, gy, dbg, gs, upbg, keep1, send1 = mlp(
        info, inv, place, flat(sn), flat(att), cot_own, cot_far, up_weight, row(up_bias),
        down_weight, row(down_bias), shards if packed else 0,
    )
    shape4 = (2, pairs, half, width)

    gy4, gs4 = gy.reshape(shape4), gs.reshape(shape4)
    if packed:
        got1 = exchange(send1, None, shards)
    ga, branch, gm, v2 = second_back(gs4, gy4, att, out_weight, g2)
    if packed:
        got1 = after(got1, v2)
        eight = lambda t: t.reshape((2, 2, 2) + t.shape[1:])
        r1 = Reduction([eight(keep1)[..., :SIDE], eight(got1)[..., :SIDE]], shards)
        r2 = Reduction(
            [eight(keep1)[..., SIDE:], eight(got1)[..., SIDE:]], shards, SIDE_STAGES
        )
        inv = after(inv, r1.step(), r2.step())
    dqa, fnt, token, keep3, send3 = attend_back(
        inv, branch, mixed, fn_own, fn_far, qkv_own, qkv_far, probs, gm, shards, packed
    )
    if packed:
        r1.incoming, r2.incoming, _ = tie(r1.incoming, r2.incoming, token)
        inv = after(inv, r1.step(), r2.step())
        got3 = exchange(send3, None, shards)
    lo_back = swap_sides(after(lo_far, token))
    ig_own, ig_far, vec, keep4, send4 = last_back(
        inv, qkv_own, qkv_far, probs, gm, fnt, dqa, ga, x_own, x_far, qkv_weight, g1, v2, upbg,
        dbg, shards, packed,
    )
    if not packed:
        ig_back = swap_sides(ig_far)

    def settle(own, back):
        own, back = own[:, :real], back[:, :real]
        return jnp.where(
            side == 0, jnp.concatenate([own, back]), jnp.concatenate([back, own])
        )

    early = 3 * EARLY * LANES
    if packed:
        whole1 = got1
        r1.incoming, r2.incoming, lo_back, got3, _ = tie(
            r1.incoming, r2.incoming, lo_back, got3, ig_own
        )
        sent = r1.step(), r2.step()
        r3 = Reduction([by_bits(keep3, shards), by_bits(after(got3, *sent), shards)], shards)
        got4 = after(exchange(send4, None, shards), r3.step())
        r4 = Reduction([by_bits(keep4, shards), by_bits(got4, shards)], shards)
        layer_out = settle(lo_own, lo_back)
        sent = r4.step()
        r1.hold(sent, layer_out)
        r2.hold(sent, layer_out)
        r1.fold()
        r2.fold()
        mine1, sent = part_pairs(keep1, whole1, r1.came, r2.came, tall, rows)
        got1 = exchange(sent, 3, shards)
        ig_back = swap_sides(after(ig_far, sent))
        for r in (r3, r4, r3, r4, r3):
            r.hold(sent)
            sent = r.step()
        input_grad = settle(ig_own, after(ig_back, sent))
        r4.hold(sent, input_grad)
        got1 = after(got1, r4.step())
        down_g, up_g = finish_pair(mine1, got1, tall, rows)
        mid, last = r3.result(), r4.result()
        vecs = last[:8, -LANES:]
        last = last[:, :-LANES]
        ln1g, ln1b, outb, ln2g, ln2b, downb = (vecs[i, :rows] for i in range(6))
        qvg, upg = vecs[6, : 2 * rows], vecs[7, : 4 * rows]
    else:
        layer_out = settle(lo_own, lo_back)
        input_grad = settle(ig_own, ig_back)
        total = lambda v: lax.psum_scatter(v, AXES, scatter_dimension=0, tiled=True)
        down_g, up_g, mid, last = total(keep1), total(send1), total(keep3), total(keep4)
        ln1g, ln1b, outb, ln2g, ln2b, downb = (total(vec[i]) for i in (0, 1, 4, 5, 6, 7))
        qvg, upg = total(vec[2:4].reshape(-1)), total(vec[8:12].reshape(-1))
    out_g = mid[:, early:]
    ca, cb = early // 3, last.shape[1] // 3
    parts = []
    for i in range(3):
        parts += [mid[:, i * ca : (i + 1) * ca], last[:, i * cb : (i + 1) * cb]]
    qkv_g = jnp.concatenate(parts, axis=1)
    return (
        layer_out, input_grad, ln1g, ln1b, qkv_g, qvg, out_g, outb, ln2g, ln2b, up_g, upg,
        down_g, downb,
    )


def solution(mesh):
    rows3 = P("pairs", "mod", None)
    vec, mat = P(AXES), P(AXES, None)
    return jax.shard_map(
        on_device,
        mesh=mesh,
        in_specs=(rows3, P("pairs"), P("pairs", "mod")) + (P(),) * 12 + (rows3,),
        out_specs=(rows3, rows3, vec, vec, mat, vec, mat, vec, vec, vec, mat, vec, mat, vec),
        check_vma=False,
    )
```

```python
from functools import partial

import jax
import jax.numpy as jnp
import numpy as np
from jax import lax
from jax.experimental import pallas as pl
from jax.experimental.pallas import tpu as pltpu
from jax.sharding import PartitionSpec as P

HEAD_DIM = 64
TXT = 40
EPS = 1e-06
MASKED = -1e30
AXES = ("pairs", "mod")
BF16 = jnp.bfloat16
F32 = jnp.float32
LANES = 128
PAD = 4
MIB = 1 << 20
MLP_MIB = 34

CORE_BIT = 2
ORDERS = ((4, 8, 1, 16), (8, 4, 1, 16))
SIDE_STAGES = (2, 0, 1, 3)
SIDE = 512
EARLY = 4


def dot_nn(a, b):
    return jnp.dot(a, b, preferred_element_type=F32)


def dot_nt(a, b):
    return lax.dot_general(a, b, (((1,), (1,)), ((), ())), preferred_element_type=F32)


def dot_tn(a, b):
    return lax.dot_general(a, b, (((0,), (0,)), ((), ())), preferred_element_type=F32)


def norm_parts(v):
    center = v - jnp.mean(v, axis=-1, keepdims=True)
    rstd = lax.rsqrt(jnp.mean(center * center, axis=-1, keepdims=True) + EPS)
    return center * rstd, rstd


def norm_back(grad, unit, rstd, gain):
    d = grad * gain
    return rstd * (
        d
        - jnp.mean(d, axis=-1, keepdims=True)
        - unit * jnp.mean(d * unit, axis=-1, keepdims=True)
    )


def gelu_and_slope(v):
    phi = 0.5 + 0.5 * lax.erf(v * 0.7071067811865476)
    bell = jnp.exp2(v * v * -0.7213475204444817)
    return v * phi, phi + v * bell * 0.3989422804014327


def lane_block(i, size=LANES):
    return pl.ds(pl.multiple_of(i * size, LANES), size)


def spec_of(a):
    return pl.BlockSpec(a.shape, lambda *_: (0,) * len(a.shape))


def resident():
    return pl.BlockSpec(memory_space=pltpu.VMEM)


def struct(shape, dtype):
    return jax.ShapeDtypeStruct(shape, dtype)


def kept(shape, dtype):
    return pltpu.HBM(shape, dtype)


def params_of(mib):
    return pltpu.CompilerParams(vmem_limit_bytes=mib * MIB)


def column_sums(value):
    return jnp.sum(value, axis=0, keepdims=True)


def wire_rows(left, inv, tall, out, shard):
    tall[...] = jnp.transpose(left.astype(F32))
    count = tall.shape[0] // shard

    def two(i, carry):
        rows = [
            tall[pl.ds(pl.multiple_of(inv[2 * i + k] * shard + 8 * g, 8), 8), :]
            for k in range(2)
            for g in range(shard // 8)
        ]
        at = pl.multiple_of(2 * shard * i, 2 * shard)
        out[pl.ds(at, 2 * shard), :] = jnp.concatenate(rows, axis=0).astype(BF16)
        return carry

    lax.fori_loop(0, count // 2, two, 0)


def own_rows(info, p, far, half):
    side = info[2] if far == 0 else 1 - info[2]
    real = half - PAD
    row = lax.broadcasted_iota(jnp.int32, (half, 1), 0)
    return row < jnp.minimum(TXT + info[p] - side * real, real)


def norm_qkv_kernel(x_ref, g_ref, b_ref, w_ref, qvb_ref, fn_ref, qkv_ref):
    j = pl.program_id(0)
    rows, width = fn_ref.shape[0] * fn_ref.shape[1], fn_ref.shape[2]

    @pl.when(j == 0)
    def _():
        unit, _ = norm_parts(x_ref[...].reshape(rows, width).astype(F32))
        fn_ref[...] = (unit * g_ref[...] + b_ref[...]).astype(BF16).reshape(fn_ref.shape)

    fn = fn_ref[...].reshape(rows, width)
    out = dot_nn(fn, w_ref[...]) + jnp.where(j == 1, 0.0, 1.0) * qvb_ref[0]
    qkv_ref[...] = out.astype(BF16).reshape(qkv_ref.shape)


def norm_qkv(x, gain, shift, weight, qv_bias, place=kept):
    pairs, half, width = x.shape
    return pl.pallas_call(
        norm_qkv_kernel,
        grid=(3,),
        in_specs=[
            spec_of(x),
            spec_of(gain),
            spec_of(shift),
            pl.BlockSpec((width, width), lambda j: (0, j)),
            pl.BlockSpec((1, 1, width), lambda j: (j // 2, 0, 0)),
        ],
        out_specs=[spec_of(x), pl.BlockSpec((pairs, half, width), lambda j: (0, 0, j))],
        out_shape=[kept((pairs, half, width), BF16), place((pairs, half, 3 * width), BF16)],
        compiler_params=params_of(24),
        cost_estimate=pl.CostEstimate(
            flops=6 * pairs * half * width * width,
            bytes_accessed=2 * (3 * width * width + 5 * pairs * half * width),
            transcendentals=0,
        ),
        name="norm_qkv",
    )(x, gain, shift, weight, qv_bias)


def stacked(block):
    first = lax.broadcasted_iota(jnp.int32, (1, LANES), 1) < HEAD_DIM
    zero = jnp.zeros((), block.dtype)
    return jnp.concatenate([jnp.where(first, block, zero), jnp.where(first, zero, block)], axis=0)


def attend_kernel(
    qo, qr, xo, xr, okrow, ow, ob, g2, b2, mixed_ref, att_ref, sn_ref, p_ref, mix_s
):
    half, width = xo.shape[1], xo.shape[2]
    rows = 2 * half
    ok8 = jnp.concatenate([okrow[0].astype(F32), jnp.zeros((7, rows), F32)], axis=0).astype(BF16)
    ok_col = dot_tn(ok8, jnp.ones((8, LANES), BF16))
    bias = jnp.where(ok_col > 0.5, 0.0, MASKED)[:, :1]

    def both(col):
        cols = lane_block(col)
        return jnp.concatenate([qo[0, :, cols], qr[0, :, cols]], axis=0)

    tiles = width // LANES

    def two_heads(hp, carry):
        q = both(hp) * jnp.asarray(HEAD_DIM**-0.5, BF16)
        s = dot_nt(stacked(both(tiles + hp)), q)
        probs = []
        for h in range(2):
            sh = s[h * rows : (h + 1) * rows, :] + bias
            e = jnp.exp(sh - jnp.max(sh, axis=0, keepdims=True))
            probs.append((e * (1.0 / column_sums(e))).astype(BF16))
        prob = jnp.concatenate(probs, axis=0)
        p_ref[0, hp] = prob
        mix_s[:, lane_block(hp)] = dot_tn(prob, stacked(both(2 * tiles + hp))).astype(BF16)
        return carry

    lax.fori_loop(0, tiles, two_heads, 0, unroll=2)
    mixed = mix_s[...]
    mixed_ref[...] = mixed.reshape(mixed_ref.shape)
    x = jnp.concatenate([xo[0], xr[0]], axis=0).astype(F32)
    att = x + dot_nn(mixed, ow[...]) + ob[...]
    att_ref[...] = att.reshape(att_ref.shape)
    unit, _ = norm_parts(att)
    sn_ref[...] = (unit * g2[...] + b2[...]).astype(BF16).reshape(sn_ref.shape)


def attend(qkv_own, qkv_far, x_own, x_far, okrow, out_weight, out_bias, gain, shift):
    pairs, half, width = x_own.shape
    tiles = width // LANES
    rows = 2 * half
    pair3 = lambda p: (p, 0, 0)
    rows4 = pl.BlockSpec((2, 1, half, width), lambda p: (0, p, 0, 0))
    return pl.pallas_call(
        attend_kernel,
        grid=(pairs,),
        in_specs=[
            pl.BlockSpec((1, half, 3 * width), pair3),
            pl.BlockSpec((1, half, 3 * width), pair3),
            pl.BlockSpec((1, half, width), pair3),
            pl.BlockSpec((1, half, width), pair3),
            pl.BlockSpec((1, 1, rows), pair3),
        ]
        + [spec_of(a) for a in (out_weight, out_bias, gain, shift)],
        out_specs=[
            rows4,
            rows4,
            rows4,
            pl.BlockSpec((1, tiles, 2 * rows, rows), lambda p: (p, 0, 0, 0)),
        ],
        out_shape=[
            kept((2, pairs, half, width), BF16),
            kept((2, pairs, half, width), F32),
            struct((2, pairs, half, width), BF16),
            kept((pairs, tiles, 2 * rows, rows), BF16),
        ],
        scratch_shapes=[pltpu.VMEM((rows, width), BF16)],
        compiler_params=params_of(32),
        cost_estimate=pl.CostEstimate(
            flops=pairs * 16 * tiles * rows * rows * LANES,
            bytes_accessed=2 * pairs * rows * width * 8 + 4 * pairs * tiles * rows * rows,
            transcendentals=2 * pairs * tiles * rows * rows,
        ),
        name="attend",
    )(qkv_own, qkv_far, x_own, x_far, okrow, out_weight, out_bias, gain, shift)


def mlp_kernel(
    info, inv, place, sn, att_hbm, co, cr, up, upb, down, downb,
    own_ref, far_ref, gy_ref, dbg_ref, gs_ref, upbg_ref, keep, send,
    acc, att, down_buf, up_buf, tall, snt, att_sem, down_sems, up_sems, *, shards,
):
    j = pl.program_id(0)
    last = pl.num_programs(0) - 1
    pairs, half, width = co.shape
    tile = upb.shape[1]
    up_j = up[:, lane_block(j, tile)]
    down_j = down[pl.ds(pl.multiple_of(j * tile, tile), tile), :]
    att_copy = pltpu.make_async_copy(att_hbm, att, att_sem)
    slot = lax.rem(j, 2)
    tall_shard, wide_shard = down.shape[0] // shards if shards else 0, width // shards if shards else 0

    @pl.when(j == 0)
    def _():
        att_copy.start()
        for far, c in enumerate((co, cr)):
            for p in range(pairs):
                at = (far * pairs + p) * half
                gy_ref[at : at + half, :] = jnp.where(
                    own_rows(info, p, far, half), c[p].astype(F32), 0.0
                ).astype(BF16)
        dbg_ref[...] = column_sums(gy_ref[...].astype(F32))
        acc[...] = jnp.zeros_like(acc)
        gs_ref[...] = jnp.zeros_like(gs_ref)
        if shards:
            wire_rows(sn[...], inv, tall, snt, wide_shard)

    def down_copies(step, act):
        count = tile // tall_shard
        for i in range(count):
            pos = place[step * count + i]
            src = down_buf.at[lax.rem(step, 2), pl.ds(i * tall_shard, tall_shard), :]
            sem = down_sems.at[lax.rem(step, 2), i]
            n = 2 * keep.shape[0]
            for ref, ours in ((keep, pos < n), (send, pos >= n)):

                @pl.when(ours)
                def _():
                    q = lax.rem(pos, n)
                    at = pl.multiple_of(lax.rem(q, 2) * tall_shard, tall_shard)
                    act(pltpu.make_async_copy(src, ref.at[lax.div(q, 2), pl.ds(at, tall_shard), :], sem))

    def up_copies(step, act):
        n = keep.shape[0]
        rows = 2 * wide_shard
        at = pl.multiple_of(2 * tall_shard + step * rows, rows)
        for i, ref in enumerate((keep, send)):
            src = up_buf.at[lax.rem(step, 2), pl.ds(i * n, n), :, :]
            act(pltpu.make_async_copy(src, ref.at[:, pl.ds(at, rows), :], up_sems.at[lax.rem(step, 2), i]))

    if shards:

        @pl.when(j > 1)
        def _():
            down_copies(j - 2, lambda c: c.wait())
            up_copies(j - 2, lambda c: c.wait())

    h, slope = gelu_and_slope(dot_nn(sn[...], up_j) + upb[...])
    h = h.astype(BF16)
    acc[...] += dot_nn(h, down_j)
    gp = (dot_nt(gy_ref[...], down_j) * slope).astype(BF16)
    upbg_ref[...] = column_sums(gp.astype(F32))
    gs_ref[...] += dot_nt(gp, up_j)
    if not shards:
        keep[...] = dot_tn(h, gy_ref[...])
        send[...] = dot_tn(sn[...], gp)
    else:
        down_buf[slot] = dot_tn(h, gy_ref[...]).astype(BF16)
        down_copies(j, lambda c: c.start())
        up_buf[slot] = dot_nn(snt[...], gp).astype(BF16).reshape(up_buf.shape[1:])
        up_copies(j, lambda c: c.start())

    @pl.when(j == last)
    def _():
        att_copy.wait()
        final = att[...] + acc[...] + downb[...]
        for far, o in enumerate((own_ref, far_ref)):
            for p in range(pairs):
                at = (far * pairs + p) * half
                o[p] = jnp.where(
                    own_rows(info, p, far, half), final[at : at + half, :], 0.0
                ).astype(BF16)
        if shards:
            for step in (last - 1, last):
                down_copies(step, lambda c: c.wait())
                up_copies(step, lambda c: c.wait())


def mlp(info, inv, place, sn, att, cot_own, cot_far, up, up_bias, down, down_bias, shards):
    pairs, half, width = cot_own.shape
    rows = 2 * pairs * half
    ff = up.shape[1]
    tile = width
    cols = lambda j, *_: (0, j)
    if shards:
        wire = [kept((shards // 4, 4 * ff // shards, width), BF16)] * 2
        wire_specs = [pl.BlockSpec(memory_space=pl.ANY)] * 2
        blocks, count = (shards // 2, 2 * width // shards), tile * shards // ff
    else:
        wire = [struct((ff, width), F32), struct((width, ff), F32)]
        wire_specs = [pl.BlockSpec((tile, width), lambda j, *_: (j, 0)), pl.BlockSpec((width, tile), cols)]
        blocks, count = (width // 16, 16), 1
    rows3 = kept((pairs, half, width), BF16)
    return pl.pallas_call(
        partial(mlp_kernel, shards=shards),
        grid_spec=pltpu.PrefetchScalarGridSpec(
            num_scalar_prefetch=3,
            grid=(ff // tile,),
            in_specs=[
                spec_of(sn),
                pl.BlockSpec(memory_space=pltpu.HBM),
                spec_of(cot_own),
                spec_of(cot_far),
                resident(),
                pl.BlockSpec((1, tile), cols),
                resident(),
                spec_of(down_bias),
            ],
            out_specs=[
                spec_of(rows3),
                spec_of(rows3),
                spec_of(sn),
                spec_of(down_bias),
                spec_of(sn),
                pl.BlockSpec((1, tile), cols),
            ]
            + wire_specs,
            scratch_shapes=[
                pltpu.VMEM((rows, width), F32),
                pltpu.VMEM((rows, width), F32),
                pltpu.VMEM((2, tile, width), BF16),
                pltpu.VMEM((2,) + blocks + (tile,), BF16),
                pltpu.VMEM((width, rows), F32),
                pltpu.VMEM((width, rows), BF16),
                pltpu.SemaphoreType.DMA,
                pltpu.SemaphoreType.DMA((2, count)),
                pltpu.SemaphoreType.DMA((2, 2)),
            ],
        ),
        out_shape=[
            rows3,
            rows3,
            struct((rows, width), BF16),
            kept((1, width), F32),
            struct((rows, width), F32),
            kept((1, ff), F32),
        ]
        + wire,
        compiler_params=params_of(MLP_MIB if shards else 56),
        cost_estimate=pl.CostEstimate(
            flops=12 * rows * width * ff, bytes_accessed=24 * MIB, transcendentals=2 * rows * ff
        ),
        name="mlp",
    )(info, inv, place, sn, att, cot_own, cot_far, up, up_bias, down, down_bias)


def heads_back(qo, qr, gm_ref, p_ref, dqkv, base, rows, hp0, count):
    first = lax.broadcasted_iota(jnp.int32, (1, LANES), 1) < HEAD_DIM
    tiles = gm_ref.shape[-1] // LANES
    scale = jnp.asarray(HEAD_DIM**-0.5, BF16)

    def both(col):
        cols = lane_block(col)
        return jnp.concatenate([qo[0, :, cols], qr[0, :, cols]], axis=0)

    def two_heads(i, carry):
        hp = hp0 + i
        gm = gm_ref[:, lane_block(hp)]
        dp = dot_nt(stacked(both(2 * tiles + hp)), gm)
        prob = p_ref[0, i]
        ds = []
        for h in range(2):
            dph = dp[h * rows : (h + 1) * rows, :]
            pf = prob[h * rows : (h + 1) * rows, :].astype(F32)
            ds.append((pf * (dph - column_sums(dph * pf))).astype(BF16))
        ds = jnp.concatenate(ds, axis=0)
        dv = dot_nn(prob, gm)
        dk = dot_nn(ds, both(hp) * scale)
        dq = dot_tn(ds, stacked(both(tiles + hp) * scale))
        pick = lambda d: jnp.where(first, d[:rows, :], d[rows:, :])
        for part, d in enumerate((dq, pick(dk), pick(dv))):
            dqkv[pl.ds(base, rows), lane_block(part * count + i)] = d.astype(BF16)
        return carry

    lax.fori_loop(0, count, two_heads, 0, unroll=2)


def wire_out(left_t, right, keep, send, at):
    n = keep.shape[0]
    grad = dot_nn(left_t, right).astype(BF16)
    keep[:, at : at + grad.shape[1]] = grad[:n]
    send[:, at : at + grad.shape[1]] = grad[n:]


def second_back_kernel(gs, gy, att, ow, g2, ga_ref, br_ref, gm_ref, vec_ref):
    rows, width = gm_ref.shape[1], gm_ref.shape[2]

    @pl.when(pl.program_id(0) == 0)
    def _():
        vec_ref[...] = jnp.zeros_like(vec_ref)

    grad_second = gs[...].reshape(rows, width)
    unit, rstd = norm_parts(att[...].reshape(rows, width))
    grad_att = gy[...].reshape(rows, width).astype(F32) + norm_back(
        grad_second, unit, rstd, g2[...]
    )
    ga_ref[0] = grad_att
    branch = grad_att.astype(BF16)
    br_ref[0] = branch
    gm_ref[0] = dot_nt(branch, ow[...]).astype(BF16)
    for i, v in enumerate((branch.astype(F32), grad_second * unit, grad_second)):
        vec_ref[i : i + 1, :] += column_sums(v)


def second_back(gs, gy, att, out_weight, gain):
    _, pairs, half, width = gs.shape
    rows = 2 * half
    rows4 = pl.BlockSpec((2, 1, half, width), lambda p: (0, p, 0, 0))
    rows3 = pl.BlockSpec((1, rows, width), lambda p: (p, 0, 0))
    vec = kept((8, width), F32)
    return pl.pallas_call(
        second_back_kernel,
        grid=(pairs,),
        in_specs=[rows4, rows4, rows4, spec_of(out_weight), spec_of(gain)],
        out_specs=[rows3, rows3, rows3, spec_of(vec)],
        out_shape=[
            kept((pairs, rows, width), F32),
            struct((pairs, rows, width), BF16),
            struct((pairs, rows, width), BF16),
            vec,
        ],
        compiler_params=params_of(24),
        cost_estimate=pl.CostEstimate(
            flops=2 * pairs * rows * width * width, bytes_accessed=10 * MIB, transcendentals=0
        ),
        name="second_back",
    )(gs, gy, att, out_weight, gain)


def attend_back_kernel(
    inv, br, mixed, fno, fnr, qo, qr, p_ref, gm_ref, dqkv, fnt, tok_ref, keep, send, gbs, fns, mxs, tall,
    *, shard,
):
    pair = pl.program_id(0)
    half, width = fno.shape[1], fno.shape[2]
    rows = 2 * half
    base = pl.multiple_of(pair * rows, rows)
    tok_ref[...] = jnp.zeros_like(tok_ref)
    gbs[pl.ds(base, rows), :] = br[0]
    fns[pl.ds(base, half), :] = fno[0]
    fns[pl.ds(base + half, half), :] = fnr[0]
    mxs[pl.ds(base, rows), :] = mixed[...].reshape(rows, width)
    heads_back(qo, qr, gm_ref.at[0], p_ref, dqkv, base, rows, 0, EARLY)

    @pl.when(pair == pl.num_programs(0) - 1)
    def _():
        early = dqkv.shape[1]
        if not shard:
            keep[:, :early] = dot_tn(fns[...], dqkv[...])
            keep[:, early:] = dot_tn(mxs[...], gbs[...])
            fnt[...] = jnp.transpose(fns[...].astype(F32)).astype(BF16)
            send[...] = jnp.zeros_like(send)
            return
        wire_rows(mxs[...], inv, tall, fnt, shard)
        wire_out(fnt[...], gbs[...], keep, send, early)
        wire_rows(fns[...], inv, tall, fnt, shard)
        for at in range(0, early, width):
            wire_out(fnt[...], dqkv[:, at : at + width], keep, send, at)


def attend_back(
    inv, branch, mixed, fn_own, fn_far, qkv_own, qkv_far, probs, gm, shards, packed
):
    pairs, half, width = fn_own.shape
    rows = 2 * half
    early = 3 * EARLY * LANES
    pair3 = lambda p, *_: (p, 0, 0)
    rows4 = pl.BlockSpec((2, 1, half, width), lambda p, *_: (0, p, 0, 0))
    if packed:
        wire = [kept((width // 2, early + width), BF16)] * 2
    else:
        wire = [struct((width, early + width), F32), struct((8, LANES), F32)]
    outs = [
        struct((pairs * rows, early), BF16),
        struct((width, pairs * rows), BF16),
        kept((8, LANES), F32),
    ] + wire
    return pl.pallas_call(
        partial(attend_back_kernel, shard=width // shards if packed else 0),
        grid_spec=pltpu.PrefetchScalarGridSpec(
            num_scalar_prefetch=1,
            grid=(pairs,),
            in_specs=[
                pl.BlockSpec((1, rows, width), pair3),
                rows4,
                pl.BlockSpec((1, half, width), pair3),
                pl.BlockSpec((1, half, width), pair3),
                pl.BlockSpec((1, half, 3 * width), pair3),
                pl.BlockSpec((1, half, 3 * width), pair3),
                pl.BlockSpec((1, EARLY, 2 * rows, rows), lambda p, *_: (p, 0, 0, 0)),
                pl.BlockSpec((1, rows, width), pair3),
            ],
            out_specs=[spec_of(o) for o in outs],
            scratch_shapes=[
                pltpu.VMEM((pairs * rows, width), BF16),
                pltpu.VMEM((pairs * rows, width), BF16),
                pltpu.VMEM((pairs * rows, width), BF16),
                pltpu.VMEM((width, pairs * rows), F32),
            ],
        ),
        out_shape=outs,
        compiler_params=params_of(40 if packed else 50),
        cost_estimate=pl.CostEstimate(
            flops=pairs * 32 * EARLY * rows * rows * LANES + 6 * pairs * rows * width * width,
            bytes_accessed=16 * MIB,
            transcendentals=0,
        ),
        name="attend_back",
    )(inv, branch, mixed, fn_own, fn_far, qkv_own, qkv_far, probs, gm)


def last_back_kernel(
    inv, qo, qr, p_ref, gm_ref, fnt, dqa, ga, xo, xr, w, g1, v2, upbg, dbg,
    own_ref, far_ref, vec_ref, keep, send, dqb, *, shard,
):
    pair = pl.program_id(0)
    half, width = xo.shape[1], xo.shape[2]
    rows = 2 * half
    tiles = width // LANES
    base = pl.multiple_of(pair * rows, rows)
    ca, cb = dqa.shape[1] // 3, dqb.shape[1] // 3

    @pl.when(pair == 0)
    def _():
        vec_ref[...] = jnp.zeros_like(vec_ref)
        vec_ref[4:7, :] = v2[0:3, :]
        vec_ref[7:8, :] = dbg[...]
        for i in range(4):
            vec_ref[8 + i : 9 + i, :] = upbg[:, i * width : (i + 1) * width]

    def add_vec(i, at, value):
        vec_ref[i : i + 1, at : at + value.shape[1]] += column_sums(value.astype(F32))

    heads_back(qo, qr, gm_ref.at[0], p_ref, dqb, base, rows, EARLY, tiles - EARLY)

    grad = None
    late = dqb[pl.ds(base, rows), :]
    for d, cols, at in ((dqa[...], ca, 0), (late, cb, ca)):
        for part in range(3):
            left = part * width + at
            term = dot_nt(d[:, part * cols : (part + 1) * cols], w[:, left : left + cols])
            grad = term if grad is None else grad + term
        add_vec(2, at, d[:, :cols])
        add_vec(3, at, d[:, 2 * cols :])
    unit, rstd = norm_parts(jnp.concatenate([xo[0], xr[0]], axis=0).astype(F32))
    add_vec(0, 0, grad * unit)
    add_vec(1, 0, grad)
    result = (ga[0] + norm_back(grad, unit, rstd, g1[...])).astype(BF16)
    own_ref[0] = result[:half]
    far_ref[0] = result[half:]

    @pl.when(pair == pl.num_programs(0) - 1)
    def _():
        if not shard:
            keep[...] = dot_nn(fnt[...], dqb[...])
            send[...] = jnp.zeros_like(send)
            return
        wire_out(fnt[...], dqb[...], keep, send, 0)
        v = vec_ref[...]
        small = jnp.concatenate([v[0:2], v[4:8], v[0:2]], axis=0)
        rowid = lax.broadcasted_iota(jnp.int32, (8, LANES), 0)
        per_q, per_u = width // (2 * shard), width // (4 * shard)
        none = jnp.zeros((shard - 8, LANES), F32)

        def piece(block, start):
            return pltpu.roll(block, lax.rem(width - start, width), 1)[:, :LANES]

        def block(i):
            a = piece(small, i * shard)
            b = piece(v[2:4], lax.rem(i, per_q) * 2 * shard)
            brow = jnp.where(i < per_q, b[0:1], b[1:2])
            c = piece(v[8:12], lax.rem(i, per_u) * 4 * shard)
            ci = lax.div(i, per_u)
            crow = jnp.where(
                ci == 0, c[0:1], jnp.where(ci == 1, c[1:2], jnp.where(ci == 2, c[2:3], c[3:4]))
            )
            return jnp.where(rowid < 6, a, jnp.where(rowid == 6, brow, crow))

        n = keep.shape[0] // shard
        right = keep.shape[1] - LANES

        def fill(p, carry):
            at = pl.ds(pl.multiple_of(2 * shard * p, 2 * shard), 2 * shard)
            for ref, first in ((keep, 0), (send, n)):
                two = [block(inv[first + 2 * p]), none, block(inv[first + 2 * p + 1]), none]
                ref[at, right:] = jnp.concatenate(two, axis=0).astype(BF16)
            return carry

        lax.fori_loop(0, n // 2, fill, 0)


def last_back(
    inv, qkv_own, qkv_far, probs, gm, fnt, dqa, ga, x_own, x_far, weight, gain, v2, upbg, dbg,
    shards, packed,
):
    pairs, rows, width = gm.shape
    half = rows // 2
    late = width // LANES - EARLY
    cols = 3 * late * LANES
    pair3 = lambda p, *_: (p, 0, 0)
    pair2 = lambda p, *_: (p, 0)
    if packed:
        wire = [kept((width // 2, cols + LANES), BF16)] * 2
    else:
        wire = [struct((width, cols), F32), struct((8, LANES), F32)]
    vec = kept((16, width), F32)
    return pl.pallas_call(
        partial(last_back_kernel, shard=width // shards if packed else 0),
        grid_spec=pltpu.PrefetchScalarGridSpec(
            num_scalar_prefetch=1,
            grid=(pairs,),
            in_specs=[
                pl.BlockSpec((1, half, 3 * width), pair3),
                pl.BlockSpec((1, half, 3 * width), pair3),
                pl.BlockSpec((1, late, 2 * rows, rows), lambda p, *_: (p, EARLY // late, 0, 0)),
                pl.BlockSpec((1, rows, width), pair3),
                spec_of(fnt),
                pl.BlockSpec((rows, dqa.shape[1]), pair2),
                pl.BlockSpec((1, rows, width), pair3),
                pl.BlockSpec((1, half, width), pair3),
                pl.BlockSpec((1, half, width), pair3),
            ]
            + [spec_of(a) for a in (weight, gain, v2, upbg, dbg)],
            out_specs=[
                pl.BlockSpec((1, half, width), pair3),
                pl.BlockSpec((1, half, width), pair3),
                spec_of(vec),
            ]
            + [spec_of(o) for o in wire],
            scratch_shapes=[pltpu.VMEM((pairs * rows, cols), BF16)],
        ),
        out_shape=[kept((pairs, half, width), BF16)] * 2 + [vec] + wire,
        compiler_params=params_of(36),
        cost_estimate=pl.CostEstimate(
            flops=pairs * 32 * late * rows * rows * LANES + 8 * pairs * rows * width * width,
            bytes_accessed=16 * MIB,
            transcendentals=0,
        ),
        name="last_back",
    )(inv, qkv_own, qkv_far, probs, gm, fnt, dqa, ga, x_own, x_far, weight, gain, v2, upbg, dbg)


def core_of(i):
    return 1 if i & CORE_BIT else 0


def shard_order(me, shards):
    half = shards // 2
    bits = half.bit_length() - 1
    tables = []
    for order in ORDERS:
        row = []
        for p in range(half):
            rel = 0
            for i, bit in enumerate(order):
                if p >> (bits - 1 - i) & 1:
                    rel |= bit
            row.append(rel)
        tables.append(row)
    both = []
    for core in range(2):
        row = tables[core] + [r | CORE_BIT for r in tables[1 - core]]
        both.append(row)
    both = np.array(both, np.int32)
    back = np.argsort(both, axis=1).astype(np.int32)
    core = jnp.where(me & CORE_BIT, 1, 0)
    rel = jnp.where(core == 0, jnp.asarray(both[0]), jnp.asarray(both[1]))
    ids = jnp.arange(shards, dtype=jnp.int32) ^ me
    hot = (ids[:, None] == jnp.arange(shards, dtype=jnp.int32)[None, :]).astype(jnp.int32)
    table = jnp.where(core == 0, jnp.asarray(back[0]), jnp.asarray(back[1]))
    return me ^ rel, jnp.sum(hot * table[None, :], axis=1)


def add_up(terms):
    total = terms[0].astype(F32)
    for t in terms[1:]:
        total = total + t.astype(F32)
    return total


def tie(*values):
    return lax.optimization_barrier(values)


def exchange(block, stage, shards):
    bits = [CORE_BIT if stage is None else ORDERS[core_of(i)][stage] for i in range(shards)]
    return lax.ppermute(block, AXES, [(i, i ^ bit) for i, bit in enumerate(bits)])


def halves(block, axis):
    if axis < 3:
        return tuple(lax.slice_in_dim(block, i, i + 1, axis=axis) for i in range(2))
    return block[0, 0, 0, 0], block[0, 0, 0, 1]


class Reduction:
    def __init__(self, terms, shards, stages=(0, 1, 2, 3)):
        self.terms, self.shards, self.stages, self.done = terms, shards, stages, 0
        self.incoming, self.came = None, []

    def hold(self, *others):
        self.incoming = after(self.incoming, *others)

    def fold(self):
        if self.incoming is not None:
            self.terms.append(self.incoming)
            self.came.append(self.incoming)
            self.incoming = None

    def parts(self):
        self.fold()
        stage = self.stages[self.done]
        self.done += 1
        pieces = [halves(t, stage) for t in self.terms]
        self.terms = [p[0] for p in pieces]
        return add_up([p[1] for p in pieces]).astype(BF16)

    def step(self):
        stage = self.stages[self.done]
        out = self.parts()
        self.incoming = exchange(out, stage, self.shards)
        return out

    def result(self):
        self.fold()
        return add_up(self.terms)


def part_pairs_kernel(keep, got, p1, p2, p3, q1, q2, q3, mine, sent, *, tall, short):
    take = lambda ref: ref[...].reshape(ref.shape[-2:]).astype(F32)
    wide = take(keep) + take(got)
    left = wide[:, :SIDE] + take(p1) + take(p2) + take(p3)
    right = wide[:, SIDE:] + take(q1) + take(q2) + take(q3)
    for cols, block in ((slice(0, SIDE), left), (slice(SIDE, wide.shape[1]), right)):
        mine[:tall, cols] = block[:tall]
        theirs = [block[tall : 2 * tall]]
        for at in range(2 * tall, block.shape[0], 2 * short):
            to = tall + (at - 2 * tall) // 2
            mine[to : to + short, cols] = block[at : at + short]
            theirs.append(block[at + short : at + 2 * short])
        sent[:, cols] = jnp.concatenate(theirs, axis=0).astype(BF16)


def part_pairs(keep, got, left, right, tall, short):
    rows, width = keep.shape[-2], keep.shape[-1]
    first = lambda a: pl.BlockSpec(
        (1,) * (len(a.shape) - 2) + a.shape[-2:], lambda i: (0,) * len(a.shape)
    )
    args = (keep, got, *left, *right)
    outs = [struct((rows // 2, width), F32), struct((rows // 2, width), BF16)]
    return pl.pallas_call(
        partial(part_pairs_kernel, tall=tall, short=short),
        grid=(1,),
        in_specs=[first(a) for a in args],
        out_specs=[spec_of(o) for o in outs],
        out_shape=outs,
        cost_estimate=pl.CostEstimate(flops=0, bytes_accessed=4 * MIB, transcendentals=0),
        name="part_pairs",
    )(*args)


def finish_pair_kernel(mine, got, down_ref, up_ref):
    total = mine[...] + got[...].astype(F32)
    tall, short, width = down_ref.shape[0], up_ref.shape[0], total.shape[1]
    down_ref[...] = total[:tall]
    for i in range(up_ref.shape[1] // width):
        at = tall + i * short
        up_ref[:, i * width : (i + 1) * width] = total[at : at + short]


def finish_pair(mine, got, tall, short):
    width = mine.shape[1]
    outs = [
        struct((tall, width), F32),
        struct((short, (mine.shape[0] - tall) // short * width), F32),
    ]
    return pl.pallas_call(
        finish_pair_kernel,
        grid=(1,),
        in_specs=[spec_of(mine), spec_of(got)],
        out_specs=[spec_of(o) for o in outs],
        out_shape=outs,
        cost_estimate=pl.CostEstimate(flops=0, bytes_accessed=2 * MIB, transcendentals=0),
        name="finish_pair",
    )(mine, got)


def by_bits(block, shards):
    return block.reshape(2, 2, 2, 2, block.shape[0] // (shards // 2), block.shape[1])


def after(value, *others):
    return tie(value, *others)[0]


def swap_sides(block):
    return lax.ppermute(block, "mod", [(0, 1), (1, 0)])


def on_device(
    tokens, patch_counts, token_mask, ln1_gain, ln1_bias, qkv_weight, qv_bias, out_weight,
    out_bias, ln2_gain, ln2_bias, up_weight, up_bias, down_weight, down_bias, cotangent,
):
    shards = lax.axis_size("pairs") * lax.axis_size("mod")
    pairs_here, real, width = tokens.shape
    pairs = pairs_here // 2
    half = real + PAD
    rows = width // shards
    packed = shards == 32 and width % (8 * shards) == 0
    side = lax.axis_index("mod").astype(jnp.int32)
    me = lax.axis_index("pairs").astype(jnp.int32) * 2 + side
    ours = lambda a: jnp.where(side == 0, a[:pairs], a[pairs:])
    theirs = lambda a: jnp.where(side == 0, a[pairs:], a[:pairs])
    padded = lambda a: jnp.pad(a, ((0, 0), (0, PAD), (0, 0)))
    x_sent = theirs(tokens)
    x_raw = swap_sides(x_sent)
    row_ids = side * real + jnp.arange(real, dtype=jnp.int32)
    ok = jnp.logical_and(row_ids[None, :] < (TXT + patch_counts)[:, None], token_mask == 1)
    ok = ok.astype(BF16)
    ok_far = swap_sides(after(theirs(ok), x_sent))
    gap = jnp.zeros((pairs, PAD), BF16)
    ok_row = jnp.concatenate([ours(ok), gap, ok_far, gap], axis=1)[:, None, :]
    tokens, cotangent = tie(tokens, cotangent, x_sent)[:2]
    x_own = padded(ours(tokens))
    cot_own = padded(ours(cotangent))
    cot_sent = theirs(cotangent)

    counts = ours(patch_counts)
    info = jnp.concatenate([counts, side[None]])
    if packed:
        inv, place = shard_order(me, shards)
    else:
        inv = place = jnp.zeros((8,), jnp.int32)

    row = lambda v: v.reshape(1, -1)
    g1, b1, g2, b2 = row(ln1_gain), row(ln1_bias), row(ln2_gain), row(ln2_bias)
    qvb = qv_bias.reshape(2, 1, width)
    fn_own, qkv_own = norm_qkv(x_own, g1, b1, qkv_weight, qvb)
    x_raw, cot_sent, _ = tie(x_raw, cot_sent, fn_own)
    x_far = padded(x_raw)
    cot_far = padded(swap_sides(cot_sent))
    fn_far, qkv_far = norm_qkv(x_far, g1, b1, qkv_weight, qvb, struct)
    mixed, att, sn, probs = attend(
        qkv_own, qkv_far, x_own, x_far, ok_row, out_weight, row(out_bias), g2, b2
    )
    flat = lambda a: a.reshape(-1, width)
    tall = down_weight.shape[0] // shards
    tiles = up_weight.shape[1] // width
    lo_own, lo_far, gy, dbg, gs, upbg, keep1, send1 = mlp(
        info, inv, place, flat(sn), flat(att), cot_own, cot_far, up_weight, row(up_bias),
        down_weight, row(down_bias), shards if packed else 0,
    )
    shape4 = (2, pairs, half, width)

    gy4, gs4 = gy.reshape(shape4), gs.reshape(shape4)
    if packed:
        got1 = exchange(send1, None, shards)
    ga, branch, gm, v2 = second_back(gs4, gy4, att, out_weight, g2)
    if packed:
        got1 = after(got1, v2)
        eight = lambda t: t.reshape((2, 2, 2) + t.shape[1:])
        r1 = Reduction([eight(keep1)[..., :SIDE], eight(got1)[..., :SIDE]], shards)
        r2 = Reduction(
            [eight(keep1)[..., SIDE:], eight(got1)[..., SIDE:]], shards, SIDE_STAGES
        )
        inv = after(inv, r1.step(), r2.step())
    dqa, fnt, token, keep3, send3 = attend_back(
        inv, branch, mixed, fn_own, fn_far, qkv_own, qkv_far, probs, gm, shards, packed
    )
    if packed:
        r1.incoming, r2.incoming, _ = tie(r1.incoming, r2.incoming, token)
        inv = after(inv, r1.step(), r2.step())
        got3 = exchange(send3, None, shards)
    lo_back = swap_sides(after(lo_far, token))
    ig_own, ig_far, vec, keep4, send4 = last_back(
        inv, qkv_own, qkv_far, probs, gm, fnt, dqa, ga, x_own, x_far, qkv_weight, g1, v2, upbg,
        dbg, shards, packed,
    )
    if not packed:
        ig_back = swap_sides(ig_far)

    def settle(own, back):
        own, back = own[:, :real], back[:, :real]
        return jnp.where(
            side == 0, jnp.concatenate([own, back]), jnp.concatenate([back, own])
        )

    early = 3 * EARLY * LANES
    if packed:
        whole1 = got1
        r1.incoming, r2.incoming, lo_back, got3, _ = tie(
            r1.incoming, r2.incoming, lo_back, got3, ig_own
        )
        sent = r1.step(), r2.step()
        r3 = Reduction([by_bits(keep3, shards), by_bits(after(got3, *sent), shards)], shards)
        got4 = after(exchange(send4, None, shards), r3.step())
        r4 = Reduction([by_bits(keep4, shards), by_bits(got4, shards)], shards)
        layer_out = settle(lo_own, lo_back)
        sent = r4.step()
        r1.hold(sent, layer_out)
        r2.hold(sent, layer_out)
        r1.fold()
        r2.fold()
        mine1, sent = part_pairs(keep1, whole1, r1.came, r2.came, tall, rows)
        got1 = exchange(sent, 3, shards)
        ig_back = swap_sides(after(ig_far, sent))
        for r in (r3, r4, r3, r4, r3):
            r.hold(sent)
            sent = r.step()
        input_grad = settle(ig_own, after(ig_back, sent))
        r4.hold(sent, input_grad)
        got1 = after(got1, r4.step())
        down_g, up_g = finish_pair(mine1, got1, tall, rows)
        mid, last = r3.result(), r4.result()
        vecs = last[:8, -LANES:]
        last = last[:, :-LANES]
        ln1g, ln1b, outb, ln2g, ln2b, downb = (vecs[i, :rows] for i in range(6))
        qvg, upg = vecs[6, : 2 * rows], vecs[7, : 4 * rows]
    else:
        layer_out = settle(lo_own, lo_back)
        input_grad = settle(ig_own, ig_back)
        total = lambda v: lax.psum_scatter(v, AXES, scatter_dimension=0, tiled=True)
        down_g, up_g, mid, last = total(keep1), total(send1), total(keep3), total(keep4)
        ln1g, ln1b, outb, ln2g, ln2b, downb = (total(vec[i]) for i in (0, 1, 4, 5, 6, 7))
        qvg, upg = total(vec[2:4].reshape(-1)), total(vec[8:12].reshape(-1))
    out_g = mid[:, early:]
    ca, cb = early // 3, last.shape[1] // 3
    parts = []
    for i in range(3):
        parts += [mid[:, i * ca : (i + 1) * ca], last[:, i * cb : (i + 1) * cb]]
    qkv_g = jnp.concatenate(parts, axis=1)
    return (
        layer_out, input_grad, ln1g, ln1b, qkv_g, qvg, out_g, outb, ln2g, ln2b, up_g, upg,
        down_g, downb,
    )


def solution(mesh):
    rows3 = P("pairs", "mod", None)
    vec, mat = P(AXES), P(AXES, None)
    return jax.shard_map(
        on_device,
        mesh=mesh,
        in_specs=(rows3, P("pairs"), P("pairs", "mod")) + (P(),) * 12 + (rows3,),
        out_specs=(rows3, rows3, vec, vec, mat, vec, mat, vec, vec, vec, mat, vec, mat, vec),
        check_vma=False,
    )
```

```python
from functools import partial

import jax
import jax.numpy as jnp
import numpy as np
from jax import lax
from jax.experimental import pallas as pl
from jax.experimental.pallas import tpu as pltpu
from jax.sharding import PartitionSpec as P

HEAD_DIM = 64
TXT = 40
EPS = 1e-06
MASKED = -1e30
AXES = ("pairs", "mod")
BF16 = jnp.bfloat16
F32 = jnp.float32
LANES = 128
PAD = 4
MIB = 1 << 20
MLP_MIB = 34

CORE_BIT = 2
ORDERS = ((4, 8, 1, 16), (8, 4, 1, 16))
SIDE_STAGES = (2, 0, 1, 3)
SIDE = 512
EARLY = 4


def dot_nn(a, b):
    return jnp.dot(a, b, preferred_element_type=F32)


def dot_nt(a, b):
    return lax.dot_general(a, b, (((1,), (1,)), ((), ())), preferred_element_type=F32)


def dot_tn(a, b):
    return lax.dot_general(a, b, (((0,), (0,)), ((), ())), preferred_element_type=F32)


def norm_parts(v):
    center = v - jnp.mean(v, axis=-1, keepdims=True)
    rstd = lax.rsqrt(jnp.mean(center * center, axis=-1, keepdims=True) + EPS)
    return center * rstd, rstd


def norm_back(grad, unit, rstd, gain):
    d = grad * gain
    return rstd * (
        d
        - jnp.mean(d, axis=-1, keepdims=True)
        - unit * jnp.mean(d * unit, axis=-1, keepdims=True)
    )


def gelu_and_slope(v):
    phi = 0.5 + 0.5 * lax.erf(v * 0.7071067811865476)
    bell = jnp.exp2(v * v * -0.7213475204444817)
    return v * phi, phi + v * bell * 0.3989422804014327


def lane_block(i, size=LANES):
    return pl.ds(pl.multiple_of(i * size, LANES), size)


def spec_of(a):
    return pl.BlockSpec(a.shape, lambda *_: (0,) * len(a.shape))


def resident():
    return pl.BlockSpec(memory_space=pltpu.VMEM)


def struct(shape, dtype):
    return jax.ShapeDtypeStruct(shape, dtype)


def kept(shape, dtype):
    return pltpu.HBM(shape, dtype)


def params_of(mib):
    return pltpu.CompilerParams(vmem_limit_bytes=mib * MIB)


def column_sums(value):
    return jnp.sum(value, axis=0, keepdims=True)


def wire_rows(left, inv, tall, out, shard):
    tall[...] = jnp.transpose(left.astype(F32))
    count = tall.shape[0] // shard

    def two(i, carry):
        rows = [
            tall[pl.ds(pl.multiple_of(inv[2 * i + k] * shard + 8 * g, 8), 8), :]
            for k in range(2)
            for g in range(shard // 8)
        ]
        at = pl.multiple_of(2 * shard * i, 2 * shard)
        out[pl.ds(at, 2 * shard), :] = jnp.concatenate(rows, axis=0).astype(BF16)
        return carry

    lax.fori_loop(0, count // 2, two, 0)


def own_rows(info, p, far, half):
    side = info[2] if far == 0 else 1 - info[2]
    real = half - PAD
    row = lax.broadcasted_iota(jnp.int32, (half, 1), 0)
    return row < jnp.minimum(TXT + info[p] - side * real, real)


def norm_qkv_kernel(x_ref, g_ref, b_ref, w_ref, qvb_ref, fn_ref, qkv_ref):
    j = pl.program_id(0)
    rows, width = fn_ref.shape[0] * fn_ref.shape[1], fn_ref.shape[2]

    @pl.when(j == 0)
    def _():
        unit, _ = norm_parts(x_ref[...].reshape(rows, width).astype(F32))
        fn_ref[...] = (unit * g_ref[...] + b_ref[...]).astype(BF16).reshape(fn_ref.shape)

    fn = fn_ref[...].reshape(rows, width)
    out = dot_nn(fn, w_ref[...]) + jnp.where(j == 1, 0.0, 1.0) * qvb_ref[0]
    qkv_ref[...] = out.astype(BF16).reshape(qkv_ref.shape)


def norm_qkv(x, gain, shift, weight, qv_bias, place=kept):
    pairs, half, width = x.shape
    return pl.pallas_call(
        norm_qkv_kernel,
        grid=(3,),
        in_specs=[
            spec_of(x),
            spec_of(gain),
            spec_of(shift),
            pl.BlockSpec((width, width), lambda j: (0, j)),
            pl.BlockSpec((1, 1, width), lambda j: (j // 2, 0, 0)),
        ],
        out_specs=[spec_of(x), pl.BlockSpec((pairs, half, width), lambda j: (0, 0, j))],
        out_shape=[kept((pairs, half, width), BF16), place((pairs, half, 3 * width), BF16)],
        compiler_params=params_of(24),
        cost_estimate=pl.CostEstimate(
            flops=6 * pairs * half * width * width,
            bytes_accessed=2 * (3 * width * width + 5 * pairs * half * width),
            transcendentals=0,
        ),
        name="norm_qkv",
    )(x, gain, shift, weight, qv_bias)


def stacked(block):
    first = lax.broadcasted_iota(jnp.int32, (1, LANES), 1) < HEAD_DIM
    zero = jnp.zeros((), block.dtype)
    return jnp.concatenate([jnp.where(first, block, zero), jnp.where(first, zero, block)], axis=0)


def attend_kernel(
    qo, qr, xo, xr, okrow, ow, ob, g2, b2, mixed_ref, att_ref, sn_ref, p_ref, mix_s
):
    half, width = xo.shape[1], xo.shape[2]
    rows = 2 * half
    ok8 = jnp.concatenate([okrow[0].astype(F32), jnp.zeros((7, rows), F32)], axis=0).astype(BF16)
    ok_col = dot_tn(ok8, jnp.ones((8, LANES), BF16))
    bias = jnp.where(ok_col > 0.5, 0.0, MASKED)[:, :1]

    def both(col):
        cols = lane_block(col)
        return jnp.concatenate([qo[0, :, cols], qr[0, :, cols]], axis=0)

    tiles = width // LANES

    def two_heads(hp, carry):
        q = both(hp) * jnp.asarray(HEAD_DIM**-0.5, BF16)
        s = dot_nt(stacked(both(tiles + hp)), q)
        probs = []
        for h in range(2):
            sh = s[h * rows : (h + 1) * rows, :] + bias
            e = jnp.exp(sh - jnp.max(sh, axis=0, keepdims=True))
            probs.append((e * (1.0 / column_sums(e))).astype(BF16))
        prob = jnp.concatenate(probs, axis=0)
        p_ref[0, hp] = prob
        mix_s[:, lane_block(hp)] = dot_tn(prob, stacked(both(2 * tiles + hp))).astype(BF16)
        return carry

    lax.fori_loop(0, tiles, two_heads, 0, unroll=2)
    mixed = mix_s[...]
    mixed_ref[...] = mixed.reshape(mixed_ref.shape)
    x = jnp.concatenate([xo[0], xr[0]], axis=0).astype(F32)
    att = x + dot_nn(mixed, ow[...]) + ob[...]
    att_ref[...] = att.reshape(att_ref.shape)
    unit, _ = norm_parts(att)
    sn_ref[...] = (unit * g2[...] + b2[...]).astype(BF16).reshape(sn_ref.shape)


def attend(qkv_own, qkv_far, x_own, x_far, okrow, out_weight, out_bias, gain, shift):
    pairs, half, width = x_own.shape
    tiles = width // LANES
    rows = 2 * half
    pair3 = lambda p: (p, 0, 0)
    rows4 = pl.BlockSpec((2, 1, half, width), lambda p: (0, p, 0, 0))
    return pl.pallas_call(
        attend_kernel,
        grid=(pairs,),
        in_specs=[
            pl.BlockSpec((1, half, 3 * width), pair3),
            pl.BlockSpec((1, half, 3 * width), pair3),
            pl.BlockSpec((1, half, width), pair3),
            pl.BlockSpec((1, half, width), pair3),
            pl.BlockSpec((1, 1, rows), pair3),
        ]
        + [spec_of(a) for a in (out_weight, out_bias, gain, shift)],
        out_specs=[
            rows4,
            rows4,
            rows4,
            pl.BlockSpec((1, tiles, 2 * rows, rows), lambda p: (p, 0, 0, 0)),
        ],
        out_shape=[
            kept((2, pairs, half, width), BF16),
            kept((2, pairs, half, width), F32),
            struct((2, pairs, half, width), BF16),
            kept((pairs, tiles, 2 * rows, rows), BF16),
        ],
        scratch_shapes=[pltpu.VMEM((rows, width), BF16)],
        compiler_params=params_of(20),
        cost_estimate=pl.CostEstimate(
            flops=pairs * 16 * tiles * rows * rows * LANES,
            bytes_accessed=2 * pairs * rows * width * 8 + 4 * pairs * tiles * rows * rows,
            transcendentals=2 * pairs * tiles * rows * rows,
        ),
        name="attend",
    )(qkv_own, qkv_far, x_own, x_far, okrow, out_weight, out_bias, gain, shift)


def mlp_kernel(
    info, inv, place, sn, att_hbm, co, cr, up, upb, down, downb,
    own_ref, far_ref, gy_ref, dbg_ref, gs_ref, upbg_ref, keep, send,
    acc, att, down_buf, up_buf, tall, snt, att_sem, down_sems, up_sems, *, shards,
):
    j = pl.program_id(0)
    last = pl.num_programs(0) - 1
    pairs, half, width = co.shape
    tile = upb.shape[1]
    up_j = up[:, lane_block(j, tile)]
    down_j = down[pl.ds(pl.multiple_of(j * tile, tile), tile), :]
    att_copy = pltpu.make_async_copy(att_hbm, att, att_sem)
    slot = lax.rem(j, 2)
    tall_shard, wide_shard = down.shape[0] // shards if shards else 0, width // shards if shards else 0

    @pl.when(j == 0)
    def _():
        att_copy.start()
        for far, c in enumerate((co, cr)):
            for p in range(pairs):
                at = (far * pairs + p) * half
                gy_ref[at : at + half, :] = jnp.where(
                    own_rows(info, p, far, half), c[p].astype(F32), 0.0
                ).astype(BF16)
        dbg_ref[...] = column_sums(gy_ref[...].astype(F32))
        acc[...] = jnp.zeros_like(acc)
        gs_ref[...] = jnp.zeros_like(gs_ref)
        if shards:
            wire_rows(sn[...], inv, tall, snt, wide_shard)

    def down_copies(step, act):
        count = tile // tall_shard
        for i in range(count):
            pos = place[step * count + i]
            src = down_buf.at[lax.rem(step, 2), pl.ds(i * tall_shard, tall_shard), :]
            sem = down_sems.at[lax.rem(step, 2), i]
            n = 2 * keep.shape[0]
            for ref, ours in ((keep, pos < n), (send, pos >= n)):

                @pl.when(ours)
                def _():
                    q = lax.rem(pos, n)
                    at = pl.multiple_of(lax.rem(q, 2) * tall_shard, tall_shard)
                    act(pltpu.make_async_copy(src, ref.at[lax.div(q, 2), pl.ds(at, tall_shard), :], sem))

    def up_copies(step, act):
        n = keep.shape[0]
        rows = 2 * wide_shard
        at = pl.multiple_of(2 * tall_shard + step * rows, rows)
        for i, ref in enumerate((keep, send)):
            src = up_buf.at[lax.rem(step, 2), pl.ds(i * n, n), :, :]
            act(pltpu.make_async_copy(src, ref.at[:, pl.ds(at, rows), :], up_sems.at[lax.rem(step, 2), i]))

    if shards:

        @pl.when(j > 1)
        def _():
            down_copies(j - 2, lambda c: c.wait())
            up_copies(j - 2, lambda c: c.wait())

    h, slope = gelu_and_slope(dot_nn(sn[...], up_j) + upb[...])
    h = h.astype(BF16)
    acc[...] += dot_nn(h, down_j)
    gp = (dot_nt(gy_ref[...], down_j) * slope).astype(BF16)
    upbg_ref[...] = column_sums(gp.astype(F32))
    gs_ref[...] += dot_nt(gp, up_j)
    if not shards:
        keep[...] = dot_tn(h, gy_ref[...])
        send[...] = dot_tn(sn[...], gp)
    else:
        down_buf[slot] = dot_tn(h, gy_ref[...]).astype(BF16)
        down_copies(j, lambda c: c.start())
        up_buf[slot] = dot_nn(snt[...], gp).astype(BF16).reshape(up_buf.shape[1:])
        up_copies(j, lambda c: c.start())

    @pl.when(j == last)
    def _():
        att_copy.wait()
        final = att[...] + acc[...] + downb[...]
        for far, o in enumerate((own_ref, far_ref)):
            for p in range(pairs):
                at = (far * pairs + p) * half
                o[p] = jnp.where(
                    own_rows(info, p, far, half), final[at : at + half, :], 0.0
                ).astype(BF16)
        if shards:
            for step in (last - 1, last):
                down_copies(step, lambda c: c.wait())
                up_copies(step, lambda c: c.wait())


def mlp(info, inv, place, sn, att, cot_own, cot_far, up, up_bias, down, down_bias, shards):
    pairs, half, width = cot_own.shape
    rows = 2 * pairs * half
    ff = up.shape[1]
    tile = width
    cols = lambda j, *_: (0, j)
    if shards:
        wire = [kept((shards // 4, 4 * ff // shards, width), BF16)] * 2
        wire_specs = [pl.BlockSpec(memory_space=pl.ANY)] * 2
        blocks, count = (shards // 2, 2 * width // shards), tile * shards // ff
    else:
        wire = [struct((ff, width), F32), struct((width, ff), F32)]
        wire_specs = [pl.BlockSpec((tile, width), lambda j, *_: (j, 0)), pl.BlockSpec((width, tile), cols)]
        blocks, count = (width // 16, 16), 1
    rows3 = kept((pairs, half, width), BF16)
    return pl.pallas_call(
        partial(mlp_kernel, shards=shards),
        grid_spec=pltpu.PrefetchScalarGridSpec(
            num_scalar_prefetch=3,
            grid=(ff // tile,),
            in_specs=[
                spec_of(sn),
                pl.BlockSpec(memory_space=pltpu.HBM),
                spec_of(cot_own),
                spec_of(cot_far),
                resident(),
                pl.BlockSpec((1, tile), cols),
                resident(),
                spec_of(down_bias),
            ],
            out_specs=[
                spec_of(rows3),
                spec_of(rows3),
                spec_of(sn),
                spec_of(down_bias),
                spec_of(sn),
                pl.BlockSpec((1, tile), cols),
            ]
            + wire_specs,
            scratch_shapes=[
                pltpu.VMEM((rows, width), F32),
                pltpu.VMEM((rows, width), F32),
                pltpu.VMEM((2, tile, width), BF16),
                pltpu.VMEM((2,) + blocks + (tile,), BF16),
                pltpu.VMEM((width, rows), F32),
                pltpu.VMEM((width, rows), BF16),
                pltpu.SemaphoreType.DMA,
                pltpu.SemaphoreType.DMA((2, count)),
                pltpu.SemaphoreType.DMA((2, 2)),
            ],
        ),
        out_shape=[
            rows3,
            rows3,
            struct((rows, width), BF16),
            kept((1, width), F32),
            struct((rows, width), F32),
            kept((1, ff), F32),
        ]
        + wire,
        compiler_params=params_of(MLP_MIB if shards else 56),
        cost_estimate=pl.CostEstimate(
            flops=12 * rows * width * ff, bytes_accessed=24 * MIB, transcendentals=2 * rows * ff
        ),
        name="mlp",
    )(
        info, inv, place, sn, pltpu.with_memory_space_constraint(att, pltpu.HBM), cot_own, cot_far, up,
        up_bias, down, down_bias,
    )


def heads_back(qo, qr, gm_ref, p_ref, dqkv, base, rows, hp0, count):
    first = lax.broadcasted_iota(jnp.int32, (1, LANES), 1) < HEAD_DIM
    tiles = gm_ref.shape[-1] // LANES
    scale = jnp.asarray(HEAD_DIM**-0.5, BF16)

    def both(col):
        cols = lane_block(col)
        return jnp.concatenate([qo[0, :, cols], qr[0, :, cols]], axis=0)

    def two_heads(i, carry):
        hp = hp0 + i
        gm = gm_ref[:, lane_block(hp)]
        dp = dot_nt(stacked(both(2 * tiles + hp)), gm)
        prob = p_ref[0, i]
        ds = []
        for h in range(2):
            dph = dp[h * rows : (h + 1) * rows, :]
            pf = prob[h * rows : (h + 1) * rows, :].astype(F32)
            ds.append((pf * (dph - column_sums(dph * pf))).astype(BF16))
        ds = jnp.concatenate(ds, axis=0)
        dv = dot_nn(prob, gm)
        dk = dot_nn(ds, both(hp) * scale)
        dq = dot_tn(ds, stacked(both(tiles + hp) * scale))
        pick = lambda d: jnp.where(first, d[:rows, :], d[rows:, :])
        for part, d in enumerate((dq, pick(dk), pick(dv))):
            dqkv[pl.ds(base, rows), lane_block(part * count + i)] = d.astype(BF16)
        return carry

    lax.fori_loop(0, count, two_heads, 0, unroll=2)


def wire_out(left_t, right, keep, send, at):
    n = keep.shape[0]
    grad = dot_nn(left_t, right).astype(BF16)
    keep[:, at : at + grad.shape[1]] = grad[:n]
    send[:, at : at + grad.shape[1]] = grad[n:]


def second_back_kernel(gs, gy, att, ow, g2, ga_ref, br_ref, gm_ref, vec_ref):
    rows, width = gm_ref.shape[1], gm_ref.shape[2]

    @pl.when(pl.program_id(0) == 0)
    def _():
        vec_ref[...] = jnp.zeros_like(vec_ref)

    grad_second = gs[...].reshape(rows, width)
    unit, rstd = norm_parts(att[...].reshape(rows, width))
    grad_att = gy[...].reshape(rows, width).astype(F32) + norm_back(
        grad_second, unit, rstd, g2[...]
    )
    ga_ref[0] = grad_att
    branch = grad_att.astype(BF16)
    br_ref[0] = branch
    gm_ref[0] = dot_nt(branch, ow[...]).astype(BF16)
    for i, v in enumerate((branch.astype(F32), grad_second * unit, grad_second)):
        vec_ref[i : i + 1, :] += column_sums(v)


def second_back(gs, gy, att, out_weight, gain):
    _, pairs, half, width = gs.shape
    rows = 2 * half
    rows4 = pl.BlockSpec((2, 1, half, width), lambda p: (0, p, 0, 0))
    rows3 = pl.BlockSpec((1, rows, width), lambda p: (p, 0, 0))
    vec = kept((8, width), F32)
    return pl.pallas_call(
        second_back_kernel,
        grid=(pairs,),
        in_specs=[rows4, rows4, rows4, spec_of(out_weight), spec_of(gain)],
        out_specs=[rows3, rows3, rows3, spec_of(vec)],
        out_shape=[
            kept((pairs, rows, width), F32),
            struct((pairs, rows, width), BF16),
            struct((pairs, rows, width), BF16),
            vec,
        ],
        compiler_params=params_of(16),
        cost_estimate=pl.CostEstimate(
            flops=2 * pairs * rows * width * width, bytes_accessed=10 * MIB, transcendentals=0
        ),
        name="second_back",
    )(gs, gy, att, out_weight, gain)


def attend_back_kernel(
    inv, br, mixed, fno, fnr, qo, qr, p_ref, gm_ref, dqkv, fnt, tok_ref, keep, send, gbs, fns, mxs, tall,
    *, shard,
):
    pair = pl.program_id(0)
    half, width = fno.shape[1], fno.shape[2]
    rows = 2 * half
    base = pl.multiple_of(pair * rows, rows)
    tok_ref[...] = jnp.zeros_like(tok_ref)
    gbs[pl.ds(base, rows), :] = br[0]
    fns[pl.ds(base, half), :] = fno[0]
    fns[pl.ds(base + half, half), :] = fnr[0]
    mxs[pl.ds(base, rows), :] = mixed[...].reshape(rows, width)
    heads_back(qo, qr, gm_ref.at[0], p_ref, dqkv, base, rows, 0, EARLY)

    @pl.when(pair == pl.num_programs(0) - 1)
    def _():
        early = dqkv.shape[1]
        if not shard:
            keep[:, :early] = dot_tn(fns[...], dqkv[...])
            keep[:, early:] = dot_tn(mxs[...], gbs[...])
            fnt[...] = jnp.transpose(fns[...].astype(F32)).astype(BF16)
            send[...] = jnp.zeros_like(send)
            return
        wire_rows(mxs[...], inv, tall, fnt, shard)
        wire_out(fnt[...], gbs[...], keep, send, early)
        wire_rows(fns[...], inv, tall, fnt, shard)
        for at in range(0, early, width):
            wire_out(fnt[...], dqkv[:, at : at + width], keep, send, at)


def attend_back(
    inv, branch, mixed, fn_own, fn_far, qkv_own, qkv_far, probs, gm, shards, packed
):
    pairs, half, width = fn_own.shape
    rows = 2 * half
    early = 3 * EARLY * LANES
    pair3 = lambda p, *_: (p, 0, 0)
    rows4 = pl.BlockSpec((2, 1, half, width), lambda p, *_: (0, p, 0, 0))
    if packed:
        wire = [kept((width // 2, early + width), BF16)] * 2
    else:
        wire = [struct((width, early + width), F32), struct((8, LANES), F32)]
    outs = [
        struct((pairs * rows, early), BF16),
        struct((width, pairs * rows), BF16),
        kept((8, LANES), F32),
    ] + wire
    return pl.pallas_call(
        partial(attend_back_kernel, shard=width // shards if packed else 0),
        grid_spec=pltpu.PrefetchScalarGridSpec(
            num_scalar_prefetch=1,
            grid=(pairs,),
            in_specs=[
                pl.BlockSpec((1, rows, width), pair3),
                rows4,
                pl.BlockSpec((1, half, width), pair3),
                pl.BlockSpec((1, half, width), pair3),
                pl.BlockSpec((1, half, 3 * width), pair3),
                pl.BlockSpec((1, half, 3 * width), pair3),
                pl.BlockSpec((1, EARLY, 2 * rows, rows), lambda p, *_: (p, 0, 0, 0)),
                pl.BlockSpec((1, rows, width), pair3),
            ],
            out_specs=[spec_of(o) for o in outs],
            scratch_shapes=[
                pltpu.VMEM((pairs * rows, width), BF16),
                pltpu.VMEM((pairs * rows, width), BF16),
                pltpu.VMEM((pairs * rows, width), BF16),
                pltpu.VMEM((width, pairs * rows), F32),
            ],
        ),
        out_shape=outs,
        compiler_params=params_of(28 if packed else 50),
        cost_estimate=pl.CostEstimate(
            flops=pairs * 32 * EARLY * rows * rows * LANES + 6 * pairs * rows * width * width,
            bytes_accessed=16 * MIB,
            transcendentals=0,
        ),
        name="attend_back",
    )(inv, branch, mixed, fn_own, fn_far, qkv_own, qkv_far, probs, gm)


def last_back_kernel(
    inv, qo, qr, p_ref, gm_ref, fnt, dqa, ga, xo, xr, w, g1, v2, upbg, dbg,
    own_ref, far_ref, vec_ref, keep, send, dqb, *, shard,
):
    pair = pl.program_id(0)
    half, width = xo.shape[1], xo.shape[2]
    rows = 2 * half
    tiles = width // LANES
    base = pl.multiple_of(pair * rows, rows)
    ca, cb = dqa.shape[1] // 3, dqb.shape[1] // 3

    @pl.when(pair == 0)
    def _():
        vec_ref[...] = jnp.zeros_like(vec_ref)
        vec_ref[4:7, :] = v2[0:3, :]
        vec_ref[7:8, :] = dbg[...]
        for i in range(4):
            vec_ref[8 + i : 9 + i, :] = upbg[:, i * width : (i + 1) * width]

    def add_vec(i, at, value):
        vec_ref[i : i + 1, at : at + value.shape[1]] += column_sums(value.astype(F32))

    heads_back(qo, qr, gm_ref.at[0], p_ref, dqb, base, rows, EARLY, tiles - EARLY)

    grad = None
    late = dqb[pl.ds(base, rows), :]
    for d, cols, at in ((dqa[...], ca, 0), (late, cb, ca)):
        for part in range(3):
            left = part * width + at
            term = dot_nt(d[:, part * cols : (part + 1) * cols], w[:, left : left + cols])
            grad = term if grad is None else grad + term
        add_vec(2, at, d[:, :cols])
        add_vec(3, at, d[:, 2 * cols :])
    unit, rstd = norm_parts(jnp.concatenate([xo[0], xr[0]], axis=0).astype(F32))
    add_vec(0, 0, grad * unit)
    add_vec(1, 0, grad)
    result = (ga[0] + norm_back(grad, unit, rstd, g1[...])).astype(BF16)
    own_ref[0] = result[:half]
    far_ref[0] = result[half:]

    @pl.when(pair == pl.num_programs(0) - 1)
    def _():
        if not shard:
            keep[...] = dot_nn(fnt[...], dqb[...])
            send[...] = jnp.zeros_like(send)
            return
        wire_out(fnt[...], dqb[...], keep, send, 0)
        v = vec_ref[...]
        small = jnp.concatenate([v[0:2], v[4:8], v[0:2]], axis=0)
        rowid = lax.broadcasted_iota(jnp.int32, (8, LANES), 0)
        per_q, per_u = width // (2 * shard), width // (4 * shard)
        none = jnp.zeros((shard - 8, LANES), F32)

        def piece(block, start):
            return pltpu.roll(block, lax.rem(width - start, width), 1)[:, :LANES]

        def block(i):
            a = piece(small, i * shard)
            b = piece(v[2:4], lax.rem(i, per_q) * 2 * shard)
            brow = jnp.where(i < per_q, b[0:1], b[1:2])
            c = piece(v[8:12], lax.rem(i, per_u) * 4 * shard)
            ci = lax.div(i, per_u)
            crow = jnp.where(
                ci == 0, c[0:1], jnp.where(ci == 1, c[1:2], jnp.where(ci == 2, c[2:3], c[3:4]))
            )
            return jnp.where(rowid < 6, a, jnp.where(rowid == 6, brow, crow))

        n = keep.shape[0] // shard
        right = keep.shape[1] - LANES

        def fill(p, carry):
            at = pl.ds(pl.multiple_of(2 * shard * p, 2 * shard), 2 * shard)
            for ref, first in ((keep, 0), (send, n)):
                two = [block(inv[first + 2 * p]), none, block(inv[first + 2 * p + 1]), none]
                ref[at, right:] = jnp.concatenate(two, axis=0).astype(BF16)
            return carry

        lax.fori_loop(0, n // 2, fill, 0)


def last_back(
    inv, qkv_own, qkv_far, probs, gm, fnt, dqa, ga, x_own, x_far, weight, gain, v2, upbg, dbg,
    shards, packed,
):
    pairs, rows, width = gm.shape
    half = rows // 2
    late = width // LANES - EARLY
    cols = 3 * late * LANES
    pair3 = lambda p, *_: (p, 0, 0)
    pair2 = lambda p, *_: (p, 0)
    if packed:
        wire = [kept((width // 2, cols + LANES), BF16)] * 2
    else:
        wire = [struct((width, cols), F32), struct((8, LANES), F32)]
    vec = kept((16, width), F32)
    return pl.pallas_call(
        partial(last_back_kernel, shard=width // shards if packed else 0),
        grid_spec=pltpu.PrefetchScalarGridSpec(
            num_scalar_prefetch=1,
            grid=(pairs,),
            in_specs=[
                pl.BlockSpec((1, half, 3 * width), pair3),
                pl.BlockSpec((1, half, 3 * width), pair3),
                pl.BlockSpec((1, late, 2 * rows, rows), lambda p, *_: (p, EARLY // late, 0, 0)),
                pl.BlockSpec((1, rows, width), pair3),
                spec_of(fnt),
                pl.BlockSpec((rows, dqa.shape[1]), pair2),
                pl.BlockSpec((1, rows, width), pair3),
                pl.BlockSpec((1, half, width), pair3),
                pl.BlockSpec((1, half, width), pair3),
            ]
            + [spec_of(a) for a in (weight, gain, v2, upbg, dbg)],
            out_specs=[
                pl.BlockSpec((1, half, width), pair3),
                pl.BlockSpec((1, half, width), pair3),
                spec_of(vec),
            ]
            + [spec_of(o) for o in wire],
            scratch_shapes=[pltpu.VMEM((pairs * rows, cols), BF16)],
        ),
        out_shape=[kept((pairs, half, width), BF16)] * 2 + [vec] + wire,
        compiler_params=params_of(22),
        cost_estimate=pl.CostEstimate(
            flops=pairs * 32 * late * rows * rows * LANES + 8 * pairs * rows * width * width,
            bytes_accessed=16 * MIB,
            transcendentals=0,
        ),
        name="last_back",
    )(inv, qkv_own, qkv_far, probs, gm, fnt, dqa, ga, x_own, x_far, weight, gain, v2, upbg, dbg)


def core_of(i):
    return 1 if i & CORE_BIT else 0


def shard_order(me, shards):
    half = shards // 2
    bits = half.bit_length() - 1
    tables = []
    for order in ORDERS:
        row = []
        for p in range(half):
            rel = 0
            for i, bit in enumerate(order):
                if p >> (bits - 1 - i) & 1:
                    rel |= bit
            row.append(rel)
        tables.append(row)
    both = []
    for core in range(2):
        row = tables[core] + [r | CORE_BIT for r in tables[1 - core]]
        both.append(row)
    both = np.array(both, np.int32)
    back = np.argsort(both, axis=1).astype(np.int32)
    core = jnp.where(me & CORE_BIT, 1, 0)
    rel = jnp.where(core == 0, jnp.asarray(both[0]), jnp.asarray(both[1]))
    ids = jnp.arange(shards, dtype=jnp.int32) ^ me
    hot = (ids[:, None] == jnp.arange(shards, dtype=jnp.int32)[None, :]).astype(jnp.int32)
    table = jnp.where(core == 0, jnp.asarray(back[0]), jnp.asarray(back[1]))
    return me ^ rel, jnp.sum(hot * table[None, :], axis=1)


def add_up(terms):
    total = terms[0].astype(F32)
    for t in terms[1:]:
        total = total + t.astype(F32)
    return total


def tie(*values):
    return lax.optimization_barrier(values)


def exchange(block, stage, shards):
    bits = [CORE_BIT if stage is None else ORDERS[core_of(i)][stage] for i in range(shards)]
    return lax.ppermute(block, AXES, [(i, i ^ bit) for i, bit in enumerate(bits)])


def halves(block, axis):
    if axis < 3:
        return tuple(lax.slice_in_dim(block, i, i + 1, axis=axis) for i in range(2))
    return block[0, 0, 0, 0], block[0, 0, 0, 1]


class Reduction:
    def __init__(self, terms, shards, stages=(0, 1, 2, 3)):
        self.terms, self.shards, self.stages, self.done = terms, shards, stages, 0
        self.incoming, self.came = None, []

    def hold(self, *others):
        self.incoming = after(self.incoming, *others)

    def fold(self):
        if self.incoming is not None:
            self.terms.append(self.incoming)
            self.came.append(self.incoming)
            self.incoming = None

    def parts(self):
        self.fold()
        stage = self.stages[self.done]
        self.done += 1
        pieces = [halves(t, stage) for t in self.terms]
        self.terms = [p[0] for p in pieces]
        return add_up([p[1] for p in pieces]).astype(BF16)

    def step(self):
        stage = self.stages[self.done]
        out = self.parts()
        self.incoming = exchange(out, stage, self.shards)
        return out

    def result(self):
        self.fold()
        return add_up(self.terms)


def part_pairs_kernel(keep, got, p1, p2, p3, q1, q2, q3, mine, sent, *, tall, short):
    take = lambda ref: ref[...].reshape(ref.shape[-2:]).astype(F32)
    wide = take(keep) + take(got)
    left = wide[:, :SIDE] + take(p1) + take(p2) + take(p3)
    right = wide[:, SIDE:] + take(q1) + take(q2) + take(q3)
    for cols, block in ((slice(0, SIDE), left), (slice(SIDE, wide.shape[1]), right)):
        mine[:tall, cols] = block[:tall]
        theirs = [block[tall : 2 * tall]]
        for at in range(2 * tall, block.shape[0], 2 * short):
            to = tall + (at - 2 * tall) // 2
            mine[to : to + short, cols] = block[at : at + short]
            theirs.append(block[at + short : at + 2 * short])
        sent[:, cols] = jnp.concatenate(theirs, axis=0).astype(BF16)


def part_pairs(keep, got, left, right, tall, short):
    rows, width = keep.shape[-2], keep.shape[-1]
    first = lambda a: pl.BlockSpec(
        (1,) * (len(a.shape) - 2) + a.shape[-2:], lambda i: (0,) * len(a.shape)
    )
    args = (keep, got, *left, *right)
    outs = [struct((rows // 2, width), F32), struct((rows // 2, width), BF16)]
    return pl.pallas_call(
        partial(part_pairs_kernel, tall=tall, short=short),
        grid=(1,),
        in_specs=[first(a) for a in args],
        out_specs=[spec_of(o) for o in outs],
        out_shape=outs,
        cost_estimate=pl.CostEstimate(flops=0, bytes_accessed=4 * MIB, transcendentals=0),
        name="part_pairs",
    )(*args)


def finish_rest_kernel(*refs, count, early):
    mids, lasts, outs = refs[:count], refs[count : 2 * count], refs[2 * count :]
    flat = lambda ref: ref[...].reshape(ref.shape[-2:]).astype(F32)

    def total(part):
        value = flat(part[0])
        for ref in part[1:]:
            value = value + flat(ref)
        return value

    mid, last = total(mids), total(lasts)
    qkv_ref, out_ref, *vecs = outs
    width = out_ref.shape[1]
    out_ref[...] = mid[:, early:]
    ca = early // 3
    cb = width - ca
    for i in range(3):
        qkv_ref[:, i * width : i * width + ca] = mid[:, i * ca : (i + 1) * ca]
        qkv_ref[:, i * width + ca : (i + 1) * width] = last[:, i * cb : (i + 1) * cb]
    for i, ref in enumerate(vecs):
        ref[...] = last[i, 3 * cb : 3 * cb + ref.shape[0]]


def finish_rest(mid, last, early):
    rows = mid[0].shape[-2]
    width = mid[0].shape[-1] - early
    outs = [struct((rows, 3 * width), F32), struct((rows, width), F32)]
    outs += [struct((n * rows,), F32) for n in (1, 1, 1, 1, 1, 1, 2, 4)]
    first = lambda a: pl.BlockSpec(
        (1,) * (len(a.shape) - 2) + a.shape[-2:], lambda i: (0,) * len(a.shape)
    )
    return pl.pallas_call(
        partial(finish_rest_kernel, count=len(mid), early=early),
        grid=(1,),
        in_specs=[first(a) for a in mid + last],
        out_specs=[spec_of(o) for o in outs],
        out_shape=outs,
        cost_estimate=pl.CostEstimate(flops=0, bytes_accessed=2 * MIB, transcendentals=0),
        name="finish_rest",
    )(*mid, *last)


def finish_pair_kernel(mine, got, down_ref, up_ref):
    total = mine[...] + got[...].astype(F32)
    tall, short, width = down_ref.shape[0], up_ref.shape[0], total.shape[1]
    down_ref[...] = total[:tall]
    for i in range(up_ref.shape[1] // width):
        at = tall + i * short
        up_ref[:, i * width : (i + 1) * width] = total[at : at + short]


def finish_pair(mine, got, tall, short):
    width = mine.shape[1]
    outs = [
        struct((tall, width), F32),
        struct((short, (mine.shape[0] - tall) // short * width), F32),
    ]
    return pl.pallas_call(
        finish_pair_kernel,
        grid=(1,),
        in_specs=[spec_of(mine), spec_of(got)],
        out_specs=[spec_of(o) for o in outs],
        out_shape=outs,
        cost_estimate=pl.CostEstimate(flops=0, bytes_accessed=2 * MIB, transcendentals=0),
        name="finish_pair",
    )(mine, got)


def by_bits(block, shards):
    return block.reshape(2, 2, 2, 2, block.shape[0] // (shards // 2), block.shape[1])


def after(value, *others):
    return tie(value, *others)[0]


def swap_sides(block):
    return lax.ppermute(block, "mod", [(0, 1), (1, 0)])


def on_device(
    tokens, patch_counts, token_mask, ln1_gain, ln1_bias, qkv_weight, qv_bias, out_weight,
    out_bias, ln2_gain, ln2_bias, up_weight, up_bias, down_weight, down_bias, cotangent,
):
    shards = lax.axis_size("pairs") * lax.axis_size("mod")
    pairs_here, real, width = tokens.shape
    pairs = pairs_here // 2
    half = real + PAD
    rows = width // shards
    packed = shards == 32 and width % (8 * shards) == 0
    side = lax.axis_index("mod").astype(jnp.int32)
    me = lax.axis_index("pairs").astype(jnp.int32) * 2 + side
    ours = lambda a: jnp.where(side == 0, a[:pairs], a[pairs:])
    theirs = lambda a: jnp.where(side == 0, a[pairs:], a[:pairs])
    padded = lambda a: jnp.pad(a, ((0, 0), (0, PAD), (0, 0)))
    x_sent = theirs(tokens)
    x_raw = swap_sides(x_sent)
    row_ids = side * real + jnp.arange(real, dtype=jnp.int32)
    ok = jnp.logical_and(row_ids[None, :] < (TXT + patch_counts)[:, None], token_mask == 1)
    ok = ok.astype(BF16)
    ok_far = swap_sides(after(theirs(ok), x_sent))
    gap = jnp.zeros((pairs, PAD), BF16)
    ok_row = jnp.concatenate([ours(ok), gap, ok_far, gap], axis=1)[:, None, :]
    tokens, cotangent = tie(tokens, cotangent, x_sent)[:2]
    x_own = padded(ours(tokens))
    cot_own = padded(ours(cotangent))
    cot_sent = theirs(cotangent)

    counts = ours(patch_counts)
    info = jnp.concatenate([counts, side[None]])
    if packed:
        inv, place = shard_order(me, shards)
    else:
        inv = place = jnp.zeros((8,), jnp.int32)

    row = lambda v: v.reshape(1, -1)
    g1, b1, g2, b2 = row(ln1_gain), row(ln1_bias), row(ln2_gain), row(ln2_bias)
    qvb = qv_bias.reshape(2, 1, width)
    fn_own, qkv_own = norm_qkv(x_own, g1, b1, qkv_weight, qvb)
    x_raw, cot_sent, _ = tie(x_raw, cot_sent, fn_own)
    x_far = padded(x_raw)
    cot_far = padded(swap_sides(cot_sent))
    fn_far, qkv_far = norm_qkv(x_far, g1, b1, qkv_weight, qvb, struct)
    mixed, att, sn, probs = attend(
        qkv_own, qkv_far, x_own, x_far, ok_row, out_weight, row(out_bias), g2, b2
    )
    flat = lambda a: a.reshape(-1, width)
    tall = down_weight.shape[0] // shards
    tiles = up_weight.shape[1] // width
    lo_own, lo_far, gy, dbg, gs, upbg, keep1, send1 = mlp(
        info, inv, place, flat(sn), flat(att), cot_own, cot_far, up_weight, row(up_bias),
        down_weight, row(down_bias), shards if packed else 0,
    )
    shape4 = (2, pairs, half, width)

    gy4, gs4 = gy.reshape(shape4), gs.reshape(shape4)
    if packed:
        got1 = exchange(send1, None, shards)
    ga, branch, gm, v2 = second_back(gs4, gy4, att, out_weight, g2)
    if packed:
        got1 = after(got1, v2)
        eight = lambda t: t.reshape((2, 2, 2) + t.shape[1:])
        r1 = Reduction([eight(keep1)[..., :SIDE], eight(got1)[..., :SIDE]], shards)
        r2 = Reduction(
            [eight(keep1)[..., SIDE:], eight(got1)[..., SIDE:]], shards, SIDE_STAGES
        )
        inv = after(inv, r1.step(), r2.step())
    dqa, fnt, token, keep3, send3 = attend_back(
        inv, branch, mixed, fn_own, fn_far, qkv_own, qkv_far, probs, gm, shards, packed
    )
    if packed:
        r1.incoming, r2.incoming, _ = tie(r1.incoming, r2.incoming, token)
        inv = after(inv, r1.step(), r2.step())
        got3 = exchange(send3, None, shards)
    lo_back = swap_sides(after(lo_far, token))
    ig_own, ig_far, vec, keep4, send4 = last_back(
        inv, qkv_own, qkv_far, probs, gm, fnt, dqa, ga, x_own, x_far, qkv_weight, g1, v2, upbg,
        dbg, shards, packed,
    )
    if not packed:
        ig_back = swap_sides(ig_far)

    def settle(own, back):
        own, back = own[:, :real], back[:, :real]
        return jnp.where(
            side == 0, jnp.concatenate([own, back]), jnp.concatenate([back, own])
        )

    early = 3 * EARLY * LANES
    if packed:
        whole1 = got1
        r1.incoming, r2.incoming, lo_back, got3, _ = tie(
            r1.incoming, r2.incoming, lo_back, got3, ig_own
        )
        sent = r1.step(), r2.step()
        r3 = Reduction([by_bits(keep3, shards), by_bits(after(got3, *sent), shards)], shards)
        got4 = after(exchange(send4, None, shards), r3.step())
        r4 = Reduction([by_bits(keep4, shards), by_bits(got4, shards)], shards)
        layer_out = settle(lo_own, lo_back)
        sent = r4.step()
        r1.hold(sent, layer_out)
        r2.hold(sent, layer_out)
        r1.fold()
        r2.fold()
        mine1, sent = part_pairs(keep1, whole1, r1.came, r2.came, tall, rows)
        got1 = exchange(sent, 3, shards)
        ig_back = swap_sides(after(ig_far, sent))
        for r in (r3, r4, r3, r4, r3):
            r.hold(sent)
            sent = r.step()
        input_grad = settle(ig_own, after(ig_back, sent))
        r4.hold(sent, input_grad)
        got1 = after(got1, r4.step())
        down_g, up_g = finish_pair(mine1, got1, tall, rows)
        r3.fold()
        r4.fold()
        qkv_g, out_g, *vecs = finish_rest(
            [by_bits(keep3, shards), by_bits(got3, shards)] + r3.came,
            [by_bits(keep4, shards), by_bits(got4, shards)] + r4.came,
            early,
        )
        ln1g, ln1b, outb, ln2g, ln2b, downb, qvg, upg = vecs
    else:
        layer_out = settle(lo_own, lo_back)
        input_grad = settle(ig_own, ig_back)
        total = lambda v: lax.psum_scatter(v, AXES, scatter_dimension=0, tiled=True)
        down_g, up_g, mid, last = total(keep1), total(send1), total(keep3), total(keep4)
        ln1g, ln1b, outb, ln2g, ln2b, downb = (total(vec[i]) for i in (0, 1, 4, 5, 6, 7))
        qvg, upg = total(vec[2:4].reshape(-1)), total(vec[8:12].reshape(-1))
        out_g = mid[:, early:]
        ca, cb = early // 3, last.shape[1] // 3
        parts = []
        for i in range(3):
            parts += [mid[:, i * ca : (i + 1) * ca], last[:, i * cb : (i + 1) * cb]]
        qkv_g = jnp.concatenate(parts, axis=1)
    return (
        layer_out, input_grad, ln1g, ln1b, qkv_g, qvg, out_g, outb, ln2g, ln2b, up_g, upg,
        down_g, downb,
    )


def solution(mesh):
    rows3 = P("pairs", "mod", None)
    vec, mat = P(AXES), P(AXES, None)
    return jax.shard_map(
        on_device,
        mesh=mesh,
        in_specs=(rows3, P("pairs"), P("pairs", "mod")) + (P(),) * 12 + (rows3,),
        out_specs=(rows3, rows3, vec, vec, mat, vec, mat, vec, vec, vec, mat, vec, mat, vec),
        check_vma=False,
    )
```

```python
from functools import partial

import jax
import jax.numpy as jnp
import numpy as np
from jax import lax
from jax.experimental import pallas as pl
from jax.experimental.pallas import tpu as pltpu
from jax.sharding import PartitionSpec as P

HEAD_DIM = 64
TXT = 40
EPS = 1e-06
MASKED = -1e30
AXES = ("pairs", "mod")
BF16 = jnp.bfloat16
F32 = jnp.float32
LANES = 128
PAD = 4
MIB = 1 << 20
MLP_MIB = 34

CORE_BIT = 2
ORDERS = ((4, 8, 1, 16), (8, 4, 1, 16))
SIDE_STAGES = (2, 0, 1, 3)
SIDE = 512
EARLY = 4


def dot_nn(a, b):
    return jnp.dot(a, b, preferred_element_type=F32)


def dot_nt(a, b):
    return lax.dot_general(a, b, (((1,), (1,)), ((), ())), preferred_element_type=F32)


def dot_tn(a, b):
    return lax.dot_general(a, b, (((0,), (0,)), ((), ())), preferred_element_type=F32)


def norm_parts(v):
    center = v - jnp.mean(v, axis=-1, keepdims=True)
    rstd = lax.rsqrt(jnp.mean(center * center, axis=-1, keepdims=True) + EPS)
    return center * rstd, rstd


def norm_back(grad, unit, rstd, gain):
    d = grad * gain
    return rstd * (
        d
        - jnp.mean(d, axis=-1, keepdims=True)
        - unit * jnp.mean(d * unit, axis=-1, keepdims=True)
    )


def gelu_and_slope(v):
    phi = 0.5 + 0.5 * lax.erf(v * 0.7071067811865476)
    bell = jnp.exp2(v * v * -0.7213475204444817)
    return v * phi, phi + v * bell * 0.3989422804014327


def lane_block(i, size=LANES):
    return pl.ds(pl.multiple_of(i * size, LANES), size)


def spec_of(a):
    return pl.BlockSpec(a.shape, lambda *_: (0,) * len(a.shape))


def resident():
    return pl.BlockSpec(memory_space=pltpu.VMEM)


def struct(shape, dtype):
    return jax.ShapeDtypeStruct(shape, dtype)


def kept(shape, dtype):
    return pltpu.HBM(shape, dtype)


def params_of(mib):
    return pltpu.CompilerParams(vmem_limit_bytes=mib * MIB)


def column_sums(value):
    return jnp.sum(value, axis=0, keepdims=True)


def wire_rows(left, inv, tall, out, shard):
    tall[...] = jnp.transpose(left.astype(F32))
    count = tall.shape[0] // shard

    def two(i, carry):
        rows = [
            tall[pl.ds(pl.multiple_of(inv[2 * i + k] * shard + 8 * g, 8), 8), :]
            for k in range(2)
            for g in range(shard // 8)
        ]
        at = pl.multiple_of(2 * shard * i, 2 * shard)
        out[pl.ds(at, 2 * shard), :] = jnp.concatenate(rows, axis=0).astype(BF16)
        return carry

    lax.fori_loop(0, count // 2, two, 0)


def own_rows(info, p, far, half):
    side = info[2] if far == 0 else 1 - info[2]
    real = half - PAD
    row = lax.broadcasted_iota(jnp.int32, (half, 1), 0)
    return row < jnp.minimum(TXT + info[p] - side * real, real)


def norm_qkv_kernel(x_ref, g_ref, b_ref, w_ref, qvb_ref, fn_ref, qkv_ref):
    j = pl.program_id(0)
    rows, width = fn_ref.shape[0] * fn_ref.shape[1], fn_ref.shape[2]

    @pl.when(j == 0)
    def _():
        unit, _ = norm_parts(x_ref[...].reshape(rows, width).astype(F32))
        fn_ref[...] = (unit * g_ref[...] + b_ref[...]).astype(BF16).reshape(fn_ref.shape)

    fn = fn_ref[...].reshape(rows, width)
    out = dot_nn(fn, w_ref[...]) + jnp.where(j == 1, 0.0, 1.0) * qvb_ref[0]
    qkv_ref[...] = out.astype(BF16).reshape(qkv_ref.shape)


def norm_qkv(x, gain, shift, weight, qv_bias, place=kept):
    pairs, half, width = x.shape
    return pl.pallas_call(
        norm_qkv_kernel,
        grid=(3,),
        in_specs=[
            spec_of(x),
            spec_of(gain),
            spec_of(shift),
            pl.BlockSpec((width, width), lambda j: (0, j)),
            pl.BlockSpec((1, 1, width), lambda j: (j // 2, 0, 0)),
        ],
        out_specs=[spec_of(x), pl.BlockSpec((pairs, half, width), lambda j: (0, 0, j))],
        out_shape=[kept((pairs, half, width), BF16), place((pairs, half, 3 * width), BF16)],
        compiler_params=params_of(24),
        cost_estimate=pl.CostEstimate(
            flops=6 * pairs * half * width * width,
            bytes_accessed=2 * (3 * width * width + 5 * pairs * half * width),
            transcendentals=0,
        ),
        name="norm_qkv",
    )(x, gain, shift, weight, qv_bias)


def stacked(block):
    first = lax.broadcasted_iota(jnp.int32, (1, LANES), 1) < HEAD_DIM
    zero = jnp.zeros((), block.dtype)
    return jnp.concatenate([jnp.where(first, block, zero), jnp.where(first, zero, block)], axis=0)


def attend_kernel(
    qo, qr, xo, xr, okrow, ow, ob, g2, b2, mixed_ref, att_ref, sn_ref, p_ref, mix_s
):
    half, width = xo.shape[1], xo.shape[2]
    rows = 2 * half
    ok8 = jnp.concatenate([okrow[0].astype(F32), jnp.zeros((7, rows), F32)], axis=0).astype(BF16)
    ok_col = dot_tn(ok8, jnp.ones((8, LANES), BF16))
    bias = jnp.where(ok_col > 0.5, 0.0, MASKED)[:, :1]

    def both(col):
        cols = lane_block(col)
        return jnp.concatenate([qo[0, :, cols], qr[0, :, cols]], axis=0)

    tiles = width // LANES

    def two_heads(hp, carry):
        q = both(hp) * jnp.asarray(HEAD_DIM**-0.5, BF16)
        s = dot_nt(stacked(both(tiles + hp)), q)
        probs = []
        for h in range(2):
            sh = s[h * rows : (h + 1) * rows, :] + bias
            e = jnp.exp(sh - jnp.max(sh, axis=0, keepdims=True))
            probs.append((e * (1.0 / column_sums(e))).astype(BF16))
        prob = jnp.concatenate(probs, axis=0)
        p_ref[0, hp] = prob
        mix_s[:, lane_block(hp)] = dot_tn(prob, stacked(both(2 * tiles + hp))).astype(BF16)
        return carry

    lax.fori_loop(0, tiles, two_heads, 0, unroll=2)
    mixed = mix_s[...]
    mixed_ref[...] = mixed.reshape(mixed_ref.shape)
    x = jnp.concatenate([xo[0], xr[0]], axis=0).astype(F32)
    att = x + dot_nn(mixed, ow[...]) + ob[...]
    att_ref[...] = att.reshape(att_ref.shape)
    unit, _ = norm_parts(att)
    sn_ref[...] = (unit * g2[...] + b2[...]).astype(BF16).reshape(sn_ref.shape)


def attend(qkv_own, qkv_far, x_own, x_far, okrow, out_weight, out_bias, gain, shift):
    pairs, half, width = x_own.shape
    tiles = width // LANES
    rows = 2 * half
    pair3 = lambda p: (p, 0, 0)
    rows4 = pl.BlockSpec((2, 1, half, width), lambda p: (0, p, 0, 0))
    return pl.pallas_call(
        attend_kernel,
        grid=(pairs,),
        in_specs=[
            pl.BlockSpec((1, half, 3 * width), pair3),
            pl.BlockSpec((1, half, 3 * width), pair3),
            pl.BlockSpec((1, half, width), pair3),
            pl.BlockSpec((1, half, width), pair3),
            pl.BlockSpec((1, 1, rows), pair3),
        ]
        + [spec_of(a) for a in (out_weight, out_bias, gain, shift)],
        out_specs=[
            rows4,
            rows4,
            rows4,
            pl.BlockSpec((1, tiles, 2 * rows, rows), lambda p: (p, 0, 0, 0)),
        ],
        out_shape=[
            kept((2, pairs, half, width), BF16),
            kept((2, pairs, half, width), F32),
            struct((2, pairs, half, width), BF16),
            kept((pairs, tiles, 2 * rows, rows), BF16),
        ],
        scratch_shapes=[pltpu.VMEM((rows, width), BF16)],
        compiler_params=params_of(20),
        cost_estimate=pl.CostEstimate(
            flops=pairs * 16 * tiles * rows * rows * LANES,
            bytes_accessed=2 * pairs * rows * width * 8 + 4 * pairs * tiles * rows * rows,
            transcendentals=2 * pairs * tiles * rows * rows,
        ),
        name="attend",
    )(qkv_own, qkv_far, x_own, x_far, okrow, out_weight, out_bias, gain, shift)


def mlp_kernel(
    info, inv, place, sn, att_hbm, co, cr, up, upb, down, downb,
    own_ref, far_ref, gy_ref, dbg_ref, gs_ref, upbg_ref, keep, send,
    acc, att, down_buf, up_buf, tall, snt, att_sem, down_sems, up_sems, *, shards,
):
    j = pl.program_id(0)
    last = pl.num_programs(0) - 1
    pairs, half, width = co.shape
    tile = upb.shape[1]
    up_j = up[:, lane_block(j, tile)]
    down_j = down[pl.ds(pl.multiple_of(j * tile, tile), tile), :]
    att_copy = pltpu.make_async_copy(att_hbm, att, att_sem)
    slot = lax.rem(j, 2)
    tall_shard, wide_shard = down.shape[0] // shards if shards else 0, width // shards if shards else 0

    @pl.when(j == 0)
    def _():
        att_copy.start()
        for far, c in enumerate((co, cr)):
            for p in range(pairs):
                at = (far * pairs + p) * half
                gy_ref[at : at + half, :] = jnp.where(
                    own_rows(info, p, far, half), c[p].astype(F32), 0.0
                ).astype(BF16)
        dbg_ref[...] = column_sums(gy_ref[...].astype(F32))
        acc[...] = jnp.zeros_like(acc)
        gs_ref[...] = jnp.zeros_like(gs_ref)
        if shards:
            wire_rows(sn[...], inv, tall, snt, wide_shard)

    def down_copies(step, act):
        count = tile // tall_shard
        for i in range(count):
            pos = place[step * count + i]
            src = down_buf.at[lax.rem(step, 2), pl.ds(i * tall_shard, tall_shard), :]
            sem = down_sems.at[lax.rem(step, 2), i]
            n = 2 * keep.shape[0]
            for ref, ours in ((keep, pos < n), (send, pos >= n)):

                @pl.when(ours)
                def _():
                    q = lax.rem(pos, n)
                    at = pl.multiple_of(lax.rem(q, 2) * tall_shard, tall_shard)
                    act(pltpu.make_async_copy(src, ref.at[lax.div(q, 2), pl.ds(at, tall_shard), :], sem))

    def up_copies(step, act):
        n = keep.shape[0]
        rows = 2 * wide_shard
        at = pl.multiple_of(2 * tall_shard + step * rows, rows)
        for i, ref in enumerate((keep, send)):
            src = up_buf.at[lax.rem(step, 2), pl.ds(i * n, n), :, :]
            act(pltpu.make_async_copy(src, ref.at[:, pl.ds(at, rows), :], up_sems.at[lax.rem(step, 2), i]))

    if shards:

        @pl.when(j > 1)
        def _():
            down_copies(j - 2, lambda c: c.wait())
            up_copies(j - 2, lambda c: c.wait())

    h, slope = gelu_and_slope(dot_nn(sn[...], up_j) + upb[...])
    h = h.astype(BF16)
    acc[...] += dot_nn(h, down_j)
    gp = (dot_nt(gy_ref[...], down_j) * slope).astype(BF16)
    upbg_ref[...] = column_sums(gp.astype(F32))
    gs_ref[...] += dot_nt(gp, up_j)
    if not shards:
        keep[...] = dot_tn(h, gy_ref[...])
        send[...] = dot_tn(sn[...], gp)
    else:
        down_buf[slot] = dot_tn(h, gy_ref[...]).astype(BF16)
        down_copies(j, lambda c: c.start())
        up_buf[slot] = dot_nn(snt[...], gp).astype(BF16).reshape(up_buf.shape[1:])
        up_copies(j, lambda c: c.start())

    @pl.when(j == last)
    def _():
        att_copy.wait()
        final = att[...] + acc[...] + downb[...]
        for far, o in enumerate((own_ref, far_ref)):
            for p in range(pairs):
                at = (far * pairs + p) * half
                o[p] = jnp.where(
                    own_rows(info, p, far, half), final[at : at + half, :], 0.0
                ).astype(BF16)
        if shards:
            for step in (last - 1, last):
                down_copies(step, lambda c: c.wait())
                up_copies(step, lambda c: c.wait())


def mlp(info, inv, place, sn, att, cot_own, cot_far, up, up_bias, down, down_bias, shards):
    pairs, half, width = cot_own.shape
    rows = 2 * pairs * half
    ff = up.shape[1]
    tile = width
    cols = lambda j, *_: (0, j)
    if shards:
        wire = [kept((shards // 4, 4 * ff // shards, width), BF16)] * 2
        wire_specs = [pl.BlockSpec(memory_space=pl.ANY)] * 2
        blocks, count = (shards // 2, 2 * width // shards), tile * shards // ff
    else:
        wire = [struct((ff, width), F32), struct((width, ff), F32)]
        wire_specs = [pl.BlockSpec((tile, width), lambda j, *_: (j, 0)), pl.BlockSpec((width, tile), cols)]
        blocks, count = (width // 16, 16), 1
    rows3 = kept((pairs, half, width), BF16)
    return pl.pallas_call(
        partial(mlp_kernel, shards=shards),
        grid_spec=pltpu.PrefetchScalarGridSpec(
            num_scalar_prefetch=3,
            grid=(ff // tile,),
            in_specs=[
                spec_of(sn),
                pl.BlockSpec(memory_space=pltpu.HBM),
                spec_of(cot_own),
                spec_of(cot_far),
                resident(),
                pl.BlockSpec((1, tile), cols),
                resident(),
                spec_of(down_bias),
            ],
            out_specs=[
                spec_of(rows3),
                spec_of(rows3),
                spec_of(sn),
                spec_of(down_bias),
                spec_of(sn),
                pl.BlockSpec((1, tile), cols),
            ]
            + wire_specs,
            scratch_shapes=[
                pltpu.VMEM((rows, width), F32),
                pltpu.VMEM((rows, width), F32),
                pltpu.VMEM((2, tile, width), BF16),
                pltpu.VMEM((2,) + blocks + (tile,), BF16),
                pltpu.VMEM((width, rows), F32),
                pltpu.VMEM((width, rows), BF16),
                pltpu.SemaphoreType.DMA,
                pltpu.SemaphoreType.DMA((2, count)),
                pltpu.SemaphoreType.DMA((2, 2)),
            ],
        ),
        out_shape=[
            rows3,
            rows3,
            struct((rows, width), BF16),
            kept((1, width), F32),
            struct((rows, width), F32),
            kept((1, ff), F32),
        ]
        + wire,
        compiler_params=params_of(MLP_MIB if shards else 56),
        cost_estimate=pl.CostEstimate(
            flops=12 * rows * width * ff, bytes_accessed=24 * MIB, transcendentals=2 * rows * ff
        ),
        name="mlp",
    )(
        info, inv, place, sn, pltpu.with_memory_space_constraint(att, pltpu.HBM), cot_own, cot_far, up,
        up_bias, down, down_bias,
    )


def heads_back(qo, qr, gm_ref, p_ref, dqkv, base, rows, hp0, count):
    first = lax.broadcasted_iota(jnp.int32, (1, LANES), 1) < HEAD_DIM
    tiles = gm_ref.shape[-1] // LANES
    scale = jnp.asarray(HEAD_DIM**-0.5, BF16)

    def both(col):
        cols = lane_block(col)
        return jnp.concatenate([qo[0, :, cols], qr[0, :, cols]], axis=0)

    def two_heads(i, carry):
        hp = hp0 + i
        gm = gm_ref[:, lane_block(hp)]
        dp = dot_nt(stacked(both(2 * tiles + hp)), gm)
        prob = p_ref[0, i]
        ds = []
        for h in range(2):
            dph = dp[h * rows : (h + 1) * rows, :]
            pf = prob[h * rows : (h + 1) * rows, :].astype(F32)
            ds.append((pf * (dph - column_sums(dph * pf))).astype(BF16))
        ds = jnp.concatenate(ds, axis=0)
        dv = dot_nn(prob, gm)
        dk = dot_nn(ds, both(hp) * scale)
        dq = dot_tn(ds, stacked(both(tiles + hp) * scale))
        pick = lambda d: jnp.where(first, d[:rows, :], d[rows:, :])
        for part, d in enumerate((dq, pick(dk), pick(dv))):
            dqkv[pl.ds(base, rows), lane_block(part * count + i)] = d.astype(BF16)
        return carry

    lax.fori_loop(0, count, two_heads, 0, unroll=2)


def wire_out(left_t, right, keep, send, at):
    n = keep.shape[0]
    grad = dot_nn(left_t, right).astype(BF16)
    keep[:, at : at + grad.shape[1]] = grad[:n]
    send[:, at : at + grad.shape[1]] = grad[n:]


def second_back_kernel(gs, gy, att, ow, g2, ga_ref, br_ref, gm_ref, vec_ref):
    rows, width = gm_ref.shape[1], gm_ref.shape[2]

    @pl.when(pl.program_id(0) == 0)
    def _():
        vec_ref[...] = jnp.zeros_like(vec_ref)

    grad_second = gs[...].reshape(rows, width)
    unit, rstd = norm_parts(att[...].reshape(rows, width))
    grad_att = gy[...].reshape(rows, width).astype(F32) + norm_back(
        grad_second, unit, rstd, g2[...]
    )
    ga_ref[0] = grad_att
    branch = grad_att.astype(BF16)
    br_ref[0] = branch
    gm_ref[0] = dot_nt(branch, ow[...]).astype(BF16)
    for i, v in enumerate((branch.astype(F32), grad_second * unit, grad_second)):
        vec_ref[i : i + 1, :] += column_sums(v)


def second_back(gs, gy, att, out_weight, gain):
    _, pairs, half, width = gs.shape
    rows = 2 * half
    rows4 = pl.BlockSpec((2, 1, half, width), lambda p: (0, p, 0, 0))
    rows3 = pl.BlockSpec((1, rows, width), lambda p: (p, 0, 0))
    vec = kept((8, width), F32)
    return pl.pallas_call(
        second_back_kernel,
        grid=(pairs,),
        in_specs=[rows4, rows4, rows4, spec_of(out_weight), spec_of(gain)],
        out_specs=[rows3, rows3, rows3, spec_of(vec)],
        out_shape=[
            kept((pairs, rows, width), F32),
            struct((pairs, rows, width), BF16),
            struct((pairs, rows, width), BF16),
            vec,
        ],
        compiler_params=params_of(16),
        cost_estimate=pl.CostEstimate(
            flops=2 * pairs * rows * width * width, bytes_accessed=10 * MIB, transcendentals=0
        ),
        name="second_back",
    )(gs, gy, att, out_weight, gain)


def attend_back_kernel(
    inv, br, mixed, fno, fnr, qo, qr, p_ref, gm_ref, dqkv, fnt, tok_ref, keep, send, gbs, fns, mxs, tall,
    *, shard,
):
    pair = pl.program_id(0)
    half, width = fno.shape[1], fno.shape[2]
    rows = 2 * half
    base = pl.multiple_of(pair * rows, rows)
    tok_ref[...] = jnp.zeros_like(tok_ref)
    gbs[pl.ds(base, rows), :] = br[0]
    fns[pl.ds(base, half), :] = fno[0]
    fns[pl.ds(base + half, half), :] = fnr[0]
    mxs[pl.ds(base, rows), :] = mixed[...].reshape(rows, width)
    heads_back(qo, qr, gm_ref.at[0], p_ref, dqkv, base, rows, 0, EARLY)

    @pl.when(pair == pl.num_programs(0) - 1)
    def _():
        early = dqkv.shape[1]
        if not shard:
            keep[:, :early] = dot_tn(fns[...], dqkv[...])
            keep[:, early:] = dot_tn(mxs[...], gbs[...])
            fnt[...] = jnp.transpose(fns[...].astype(F32)).astype(BF16)
            send[...] = jnp.zeros_like(send)
            return
        wire_rows(mxs[...], inv, tall, fnt, shard)
        wire_out(fnt[...], gbs[...], keep, send, early)
        wire_rows(fns[...], inv, tall, fnt, shard)
        for at in range(0, early, width):
            wire_out(fnt[...], dqkv[:, at : at + width], keep, send, at)


def attend_back(
    inv, branch, mixed, fn_own, fn_far, qkv_own, qkv_far, probs, gm, shards, packed
):
    pairs, half, width = fn_own.shape
    rows = 2 * half
    early = 3 * EARLY * LANES
    pair3 = lambda p, *_: (p, 0, 0)
    rows4 = pl.BlockSpec((2, 1, half, width), lambda p, *_: (0, p, 0, 0))
    if packed:
        wire = [kept((width // 2, early + width), BF16)] * 2
    else:
        wire = [struct((width, early + width), F32), struct((8, LANES), F32)]
    outs = [
        struct((pairs * rows, early), BF16),
        struct((width, pairs * rows), BF16),
        kept((8, LANES), F32),
    ] + wire
    return pl.pallas_call(
        partial(attend_back_kernel, shard=width // shards if packed else 0),
        grid_spec=pltpu.PrefetchScalarGridSpec(
            num_scalar_prefetch=1,
            grid=(pairs,),
            in_specs=[
                pl.BlockSpec((1, rows, width), pair3),
                rows4,
                pl.BlockSpec((1, half, width), pair3),
                pl.BlockSpec((1, half, width), pair3),
                pl.BlockSpec((1, half, 3 * width), pair3),
                pl.BlockSpec((1, half, 3 * width), pair3),
                pl.BlockSpec((1, EARLY, 2 * rows, rows), lambda p, *_: (p, 0, 0, 0)),
                pl.BlockSpec((1, rows, width), pair3),
            ],
            out_specs=[spec_of(o) for o in outs],
            scratch_shapes=[
                pltpu.VMEM((pairs * rows, width), BF16),
                pltpu.VMEM((pairs * rows, width), BF16),
                pltpu.VMEM((pairs * rows, width), BF16),
                pltpu.VMEM((width, pairs * rows), F32),
            ],
        ),
        out_shape=outs,
        compiler_params=params_of(28 if packed else 50),
        cost_estimate=pl.CostEstimate(
            flops=pairs * 32 * EARLY * rows * rows * LANES + 6 * pairs * rows * width * width,
            bytes_accessed=16 * MIB,
            transcendentals=0,
        ),
        name="attend_back",
    )(inv, branch, mixed, fn_own, fn_far, qkv_own, qkv_far, probs, gm)


def last_back_kernel(
    inv, qo, qr, p_ref, gm_ref, fnt, dqa, ga, xo, xr, w, g1, v2, upbg, dbg,
    own_ref, far_ref, vec_ref, keep, send, dqb, *, shard,
):
    pair = pl.program_id(0)
    half, width = xo.shape[1], xo.shape[2]
    rows = 2 * half
    tiles = width // LANES
    base = pl.multiple_of(pair * rows, rows)
    ca, cb = dqa.shape[1] // 3, dqb.shape[1] // 3

    @pl.when(pair == 0)
    def _():
        vec_ref[...] = jnp.zeros_like(vec_ref)
        vec_ref[4:7, :] = v2[0:3, :]
        vec_ref[7:8, :] = dbg[...]
        for i in range(4):
            vec_ref[8 + i : 9 + i, :] = upbg[:, i * width : (i + 1) * width]

    def add_vec(i, at, value):
        vec_ref[i : i + 1, at : at + value.shape[1]] += column_sums(value.astype(F32))

    heads_back(qo, qr, gm_ref.at[0], p_ref, dqb, base, rows, EARLY, tiles - EARLY)

    grad = None
    late = dqb[pl.ds(base, rows), :]
    for d, cols, at in ((dqa[...], ca, 0), (late, cb, ca)):
        for part in range(3):
            left = part * width + at
            term = dot_nt(d[:, part * cols : (part + 1) * cols], w[:, left : left + cols])
            grad = term if grad is None else grad + term
        add_vec(2, at, d[:, :cols])
        add_vec(3, at, d[:, 2 * cols :])
    unit, rstd = norm_parts(jnp.concatenate([xo[0], xr[0]], axis=0).astype(F32))
    add_vec(0, 0, grad * unit)
    add_vec(1, 0, grad)
    result = (ga[0] + norm_back(grad, unit, rstd, g1[...])).astype(BF16)
    own_ref[0] = result[:half]
    far_ref[0] = result[half:]

    @pl.when(pair == pl.num_programs(0) - 1)
    def _():
        if not shard:
            keep[...] = dot_nn(fnt[...], dqb[...])
            send[...] = jnp.zeros_like(send)
            return
        wire_out(fnt[...], dqb[...], keep, send, 0)
        v = vec_ref[...]
        small = jnp.concatenate([v[0:2], v[4:8], v[0:2]], axis=0)
        rowid = lax.broadcasted_iota(jnp.int32, (8, LANES), 0)
        per_q, per_u = width // (2 * shard), width // (4 * shard)
        none = jnp.zeros((shard - 8, LANES), F32)

        def piece(block, start):
            return pltpu.roll(block, lax.rem(width - start, width), 1)[:, :LANES]

        def block(i):
            a = piece(small, i * shard)
            b = piece(v[2:4], lax.rem(i, per_q) * 2 * shard)
            brow = jnp.where(i < per_q, b[0:1], b[1:2])
            c = piece(v[8:12], lax.rem(i, per_u) * 4 * shard)
            ci = lax.div(i, per_u)
            crow = jnp.where(
                ci == 0, c[0:1], jnp.where(ci == 1, c[1:2], jnp.where(ci == 2, c[2:3], c[3:4]))
            )
            return jnp.where(rowid < 6, a, jnp.where(rowid == 6, brow, crow))

        n = keep.shape[0] // shard
        right = keep.shape[1] - LANES

        def fill(p, carry):
            at = pl.ds(pl.multiple_of(2 * shard * p, 2 * shard), 2 * shard)
            for ref, first in ((keep, 0), (send, n)):
                two = [block(inv[first + 2 * p]), none, block(inv[first + 2 * p + 1]), none]
                ref[at, right:] = jnp.concatenate(two, axis=0).astype(BF16)
            return carry

        lax.fori_loop(0, n // 2, fill, 0)


def last_back(
    inv, qkv_own, qkv_far, probs, gm, fnt, dqa, ga, x_own, x_far, weight, gain, v2, upbg, dbg,
    shards, packed,
):
    pairs, rows, width = gm.shape
    half = rows // 2
    late = width // LANES - EARLY
    cols = 3 * late * LANES
    pair3 = lambda p, *_: (p, 0, 0)
    pair2 = lambda p, *_: (p, 0)
    if packed:
        wire = [kept((width // 2, cols + LANES), BF16)] * 2
    else:
        wire = [struct((width, cols), F32), struct((8, LANES), F32)]
    vec = kept((16, width), F32)
    return pl.pallas_call(
        partial(last_back_kernel, shard=width // shards if packed else 0),
        grid_spec=pltpu.PrefetchScalarGridSpec(
            num_scalar_prefetch=1,
            grid=(pairs,),
            in_specs=[
                pl.BlockSpec((1, half, 3 * width), pair3),
                pl.BlockSpec((1, half, 3 * width), pair3),
                pl.BlockSpec((1, late, 2 * rows, rows), lambda p, *_: (p, EARLY // late, 0, 0)),
                pl.BlockSpec((1, rows, width), pair3),
                spec_of(fnt),
                pl.BlockSpec((rows, dqa.shape[1]), pair2),
                pl.BlockSpec((1, rows, width), pair3),
                pl.BlockSpec((1, half, width), pair3),
                pl.BlockSpec((1, half, width), pair3),
            ]
            + [spec_of(a) for a in (weight, gain, v2, upbg, dbg)],
            out_specs=[
                pl.BlockSpec((1, half, width), pair3),
                pl.BlockSpec((1, half, width), pair3),
                spec_of(vec),
            ]
            + [spec_of(o) for o in wire],
            scratch_shapes=[pltpu.VMEM((pairs * rows, cols), BF16)],
        ),
        out_shape=[kept((pairs, half, width), BF16)] * 2 + [vec] + wire,
        compiler_params=params_of(22),
        cost_estimate=pl.CostEstimate(
            flops=pairs * 32 * late * rows * rows * LANES + 8 * pairs * rows * width * width,
            bytes_accessed=16 * MIB,
            transcendentals=0,
        ),
        name="last_back",
    )(inv, qkv_own, qkv_far, probs, gm, fnt, dqa, ga, x_own, x_far, weight, gain, v2, upbg, dbg)


def core_of(i):
    return 1 if i & CORE_BIT else 0


def shard_order(me, shards):
    half = shards // 2
    bits = half.bit_length() - 1
    tables = []
    for order in ORDERS:
        row = []
        for p in range(half):
            rel = 0
            for i, bit in enumerate(order):
                if p >> (bits - 1 - i) & 1:
                    rel |= bit
            row.append(rel)
        tables.append(row)
    both = []
    for core in range(2):
        row = tables[core] + [r | CORE_BIT for r in tables[1 - core]]
        both.append(row)
    both = np.array(both, np.int32)
    back = np.argsort(both, axis=1).astype(np.int32)
    core = jnp.where(me & CORE_BIT, 1, 0)
    rel = jnp.where(core == 0, jnp.asarray(both[0]), jnp.asarray(both[1]))
    ids = jnp.arange(shards, dtype=jnp.int32) ^ me
    hot = (ids[:, None] == jnp.arange(shards, dtype=jnp.int32)[None, :]).astype(jnp.int32)
    table = jnp.where(core == 0, jnp.asarray(back[0]), jnp.asarray(back[1]))
    return me ^ rel, jnp.sum(hot * table[None, :], axis=1)


def add_up(terms):
    total = terms[0].astype(F32)
    for t in terms[1:]:
        total = total + t.astype(F32)
    return total


def tie(*values):
    return lax.optimization_barrier(values)


def exchange(block, stage, shards):
    bits = [CORE_BIT if stage is None else ORDERS[core_of(i)][stage] for i in range(shards)]
    return lax.ppermute(block, AXES, [(i, i ^ bit) for i, bit in enumerate(bits)])


def halves(block, axis):
    if axis < 3:
        return tuple(lax.slice_in_dim(block, i, i + 1, axis=axis) for i in range(2))
    return block[0, 0, 0, 0], block[0, 0, 0, 1]


class Reduction:
    def __init__(self, terms, shards, stages=(0, 1, 2, 3)):
        self.terms, self.shards, self.stages, self.done = terms, shards, stages, 0
        self.incoming, self.came = None, []

    def hold(self, *others):
        self.incoming = after(self.incoming, *others)

    def fold(self):
        if self.incoming is not None:
            self.terms.append(self.incoming)
            self.came.append(self.incoming)
            self.incoming = None

    def parts(self):
        self.fold()
        stage = self.stages[self.done]
        self.done += 1
        pieces = [halves(t, stage) for t in self.terms]
        self.terms = [p[0] for p in pieces]
        return add_up([p[1] for p in pieces]).astype(BF16)

    def step(self):
        stage = self.stages[self.done]
        out = self.parts()
        self.incoming = exchange(out, stage, self.shards)
        return out

    def result(self):
        self.fold()
        return add_up(self.terms)


def part_pairs_kernel(keep, got, p1, p2, p3, q1, q2, q3, mine, sent, *, tall, short):
    take = lambda ref: ref[...].reshape(ref.shape[-2:]).astype(F32)
    wide = take(keep) + take(got)
    left = wide[:, :SIDE] + take(p1) + take(p2) + take(p3)
    right = wide[:, SIDE:] + take(q1) + take(q2) + take(q3)
    for cols, block in ((slice(0, SIDE), left), (slice(SIDE, wide.shape[1]), right)):
        mine[:tall, cols] = block[:tall]
        theirs = [block[tall : 2 * tall]]
        for at in range(2 * tall, block.shape[0], 2 * short):
            to = tall + (at - 2 * tall) // 2
            mine[to : to + short, cols] = block[at : at + short]
            theirs.append(block[at + short : at + 2 * short])
        sent[:, cols] = jnp.concatenate(theirs, axis=0).astype(BF16)


def part_pairs(keep, got, left, right, tall, short):
    rows, width = keep.shape[-2], keep.shape[-1]
    first = lambda a: pl.BlockSpec(
        (1,) * (len(a.shape) - 2) + a.shape[-2:], lambda i: (0,) * len(a.shape)
    )
    args = (keep, got, *left, *right)
    outs = [struct((rows // 2, width), F32), struct((rows // 2, width), BF16)]
    return pl.pallas_call(
        partial(part_pairs_kernel, tall=tall, short=short),
        grid=(1,),
        in_specs=[first(a) for a in args],
        out_specs=[spec_of(o) for o in outs],
        out_shape=outs,
        cost_estimate=pl.CostEstimate(flops=0, bytes_accessed=4 * MIB, transcendentals=0),
        name="part_pairs",
    )(*args)


def finish_rest_kernel(*refs, count, early):
    mids, lasts, outs = refs[:count], refs[count : 2 * count], refs[2 * count :]
    flat = lambda ref: ref[...].reshape(ref.shape[-2:]).astype(F32)

    def total(part):
        value = flat(part[0])
        for ref in part[1:]:
            value = value + flat(ref)
        return value

    mid, last = total(mids), total(lasts)
    qkv_ref, out_ref, *vecs = outs
    width = out_ref.shape[1]
    out_ref[...] = mid[:, early:]
    ca = early // 3
    cb = width - ca
    for i in range(3):
        qkv_ref[:, i * width : i * width + ca] = mid[:, i * ca : (i + 1) * ca]
        qkv_ref[:, i * width + ca : (i + 1) * width] = last[:, i * cb : (i + 1) * cb]
    for i, ref in enumerate(vecs):
        ref[...] = last[i, 3 * cb : 3 * cb + ref.shape[0]]


def finish_rest(mid, last, early):
    rows = mid[0].shape[-2]
    width = mid[0].shape[-1] - early
    outs = [struct((rows, 3 * width), F32), struct((rows, width), F32)]
    outs += [struct((n * rows,), F32) for n in (1, 1, 1, 1, 1, 1, 2, 4)]
    first = lambda a: pl.BlockSpec(
        (1,) * (len(a.shape) - 2) + a.shape[-2:], lambda i: (0,) * len(a.shape)
    )
    return pl.pallas_call(
        partial(finish_rest_kernel, count=len(mid), early=early),
        grid=(1,),
        in_specs=[first(a) for a in mid + last],
        out_specs=[spec_of(o) for o in outs],
        out_shape=outs,
        cost_estimate=pl.CostEstimate(flops=0, bytes_accessed=2 * MIB, transcendentals=0),
        name="finish_rest",
    )(*mid, *last)


def finish_pair_kernel(mine, got, down_ref, up_ref):
    total = mine[...] + got[...].astype(F32)
    tall, short, width = down_ref.shape[0], up_ref.shape[0], total.shape[1]
    down_ref[...] = total[:tall]
    for i in range(up_ref.shape[1] // width):
        at = tall + i * short
        up_ref[:, i * width : (i + 1) * width] = total[at : at + short]


def finish_pair(mine, got, tall, short):
    width = mine.shape[1]
    outs = [
        struct((tall, width), F32),
        struct((short, (mine.shape[0] - tall) // short * width), F32),
    ]
    return pl.pallas_call(
        finish_pair_kernel,
        grid=(1,),
        in_specs=[spec_of(mine), spec_of(got)],
        out_specs=[spec_of(o) for o in outs],
        out_shape=outs,
        cost_estimate=pl.CostEstimate(flops=0, bytes_accessed=2 * MIB, transcendentals=0),
        name="finish_pair",
    )(mine, got)


def by_bits(block, shards):
    return block.reshape(2, 2, 2, 2, block.shape[0] // (shards // 2), block.shape[1])


def after(value, *others):
    return tie(value, *others)[0]


def swap_sides(block):
    return lax.ppermute(block, "mod", [(0, 1), (1, 0)])


def on_device(
    tokens, patch_counts, token_mask, ln1_gain, ln1_bias, qkv_weight, qv_bias, out_weight,
    out_bias, ln2_gain, ln2_bias, up_weight, up_bias, down_weight, down_bias, cotangent,
):
    shards = lax.axis_size("pairs") * lax.axis_size("mod")
    pairs_here, real, width = tokens.shape
    pairs = pairs_here // 2
    half = real + PAD
    rows = width // shards
    packed = shards == 32 and width % (8 * shards) == 0
    side = lax.axis_index("mod").astype(jnp.int32)
    me = lax.axis_index("pairs").astype(jnp.int32) * 2 + side
    ours = lambda a: jnp.where(side == 0, a[:pairs], a[pairs:])
    theirs = lambda a: jnp.where(side == 0, a[pairs:], a[:pairs])
    padded = lambda a: jnp.pad(a, ((0, 0), (0, PAD), (0, 0)))
    x_sent = theirs(tokens)
    x_raw = swap_sides(x_sent)
    row_ids = side * real + jnp.arange(real, dtype=jnp.int32)
    ok = jnp.logical_and(row_ids[None, :] < (TXT + patch_counts)[:, None], token_mask == 1)
    ok = ok.astype(BF16)
    ok_far = swap_sides(after(theirs(ok), x_sent))
    gap = jnp.zeros((pairs, PAD), BF16)
    ok_row = jnp.concatenate([ours(ok), gap, ok_far, gap], axis=1)[:, None, :]
    tokens, cotangent = tie(tokens, cotangent, x_sent)[:2]
    x_own = padded(ours(tokens))
    cot_own = padded(ours(cotangent))
    cot_sent = theirs(cotangent)

    counts = ours(patch_counts)
    info = jnp.concatenate([counts, side[None]])
    if packed:
        inv, place = shard_order(me, shards)
    else:
        inv = place = jnp.zeros((8,), jnp.int32)

    row = lambda v: v.reshape(1, -1)
    g1, b1, g2, b2 = row(ln1_gain), row(ln1_bias), row(ln2_gain), row(ln2_bias)
    qvb = qv_bias.reshape(2, 1, width)
    fn_own, qkv_own = norm_qkv(x_own, g1, b1, qkv_weight, qvb)
    x_raw, cot_sent, _ = tie(x_raw, cot_sent, fn_own)
    x_far = padded(x_raw)
    cot_far = padded(swap_sides(cot_sent))
    fn_far, qkv_far = norm_qkv(x_far, g1, b1, qkv_weight, qvb, struct)
    mixed, att, sn, probs = attend(
        qkv_own, qkv_far, x_own, x_far, ok_row, out_weight, row(out_bias), g2, b2
    )
    flat = lambda a: a.reshape(-1, width)
    tall = down_weight.shape[0] // shards
    tiles = up_weight.shape[1] // width
    lo_own, lo_far, gy, dbg, gs, upbg, keep1, send1 = mlp(
        info, inv, place, flat(sn), flat(att), cot_own, cot_far, up_weight, row(up_bias),
        down_weight, row(down_bias), shards if packed else 0,
    )
    shape4 = (2, pairs, half, width)

    gy4, gs4 = gy.reshape(shape4), gs.reshape(shape4)
    if packed:
        got1 = exchange(send1, None, shards)
    ga, branch, gm, v2 = second_back(gs4, gy4, att, out_weight, g2)
    if packed:
        got1 = after(got1, v2)
        eight = lambda t: t.reshape((2, 2, 2) + t.shape[1:])
        r1 = Reduction([eight(keep1)[..., :SIDE], eight(got1)[..., :SIDE]], shards)
        r2 = Reduction(
            [eight(keep1)[..., SIDE:], eight(got1)[..., SIDE:]], shards, SIDE_STAGES
        )
        inv = after(inv, r1.step(), r2.step())
    dqa, fnt, token, keep3, send3 = attend_back(
        inv, branch, mixed, fn_own, fn_far, qkv_own, qkv_far, probs, gm, shards, packed
    )
    if packed:
        r1.incoming, r2.incoming, _ = tie(r1.incoming, r2.incoming, token)
        inv = after(inv, r1.step(), r2.step())
        got3 = exchange(send3, None, shards)
    lo_back = swap_sides(after(lo_far, token))
    ig_own, ig_far, vec, keep4, send4 = last_back(
        inv, qkv_own, qkv_far, probs, gm, fnt, dqa, ga, x_own, x_far, qkv_weight, g1, v2, upbg,
        dbg, shards, packed,
    )
    if not packed:
        ig_back = swap_sides(ig_far)

    def settle(own, back):
        own, back = own[:, :real], back[:, :real]
        return jnp.where(
            side == 0, jnp.concatenate([own, back]), jnp.concatenate([back, own])
        )

    early = 3 * EARLY * LANES
    if packed:
        whole1 = got1
        r1.incoming, r2.incoming, lo_back, got3, _ = tie(
            r1.incoming, r2.incoming, lo_back, got3, ig_own
        )
        sent = r1.step(), r2.step()
        r3 = Reduction([by_bits(keep3, shards), by_bits(after(got3, *sent), shards)], shards)
        got4 = after(exchange(send4, None, shards), r3.step())
        r4 = Reduction([by_bits(keep4, shards), by_bits(got4, shards)], shards)
        layer_out = settle(lo_own, lo_back)
        sent = r4.step()
        r1.hold(sent, layer_out)
        r2.hold(sent, layer_out)
        r1.fold()
        r2.fold()
        mine1, sent = part_pairs(keep1, whole1, r1.came, r2.came, tall, rows)
        got1 = exchange(sent, 3, shards)
        ig_back = swap_sides(after(ig_far, r1.came[-1]))
        for r in (r3, r4, r3, r4, r3):
            r.hold(sent)
            sent = r.step()
        input_grad = settle(ig_own, after(ig_back, sent))
        r4.hold(sent, input_grad)
        got1 = after(got1, r4.step())
        down_g, up_g = finish_pair(mine1, got1, tall, rows)
        r3.fold()
        r4.fold()
        qkv_g, out_g, *vecs = finish_rest(
            [by_bits(keep3, shards), by_bits(got3, shards)] + r3.came,
            [by_bits(keep4, shards), by_bits(got4, shards)] + r4.came,
            early,
        )
        ln1g, ln1b, outb, ln2g, ln2b, downb, qvg, upg = vecs
    else:
        layer_out = settle(lo_own, lo_back)
        input_grad = settle(ig_own, ig_back)
        total = lambda v: lax.psum_scatter(v, AXES, scatter_dimension=0, tiled=True)
        down_g, up_g, mid, last = total(keep1), total(send1), total(keep3), total(keep4)
        ln1g, ln1b, outb, ln2g, ln2b, downb = (total(vec[i]) for i in (0, 1, 4, 5, 6, 7))
        qvg, upg = total(vec[2:4].reshape(-1)), total(vec[8:12].reshape(-1))
        out_g = mid[:, early:]
        ca, cb = early // 3, last.shape[1] // 3
        parts = []
        for i in range(3):
            parts += [mid[:, i * ca : (i + 1) * ca], last[:, i * cb : (i + 1) * cb]]
        qkv_g = jnp.concatenate(parts, axis=1)
    return (
        layer_out, input_grad, ln1g, ln1b, qkv_g, qvg, out_g, outb, ln2g, ln2b, up_g, upg,
        down_g, downb,
    )


def solution(mesh):
    rows3 = P("pairs", "mod", None)
    vec, mat = P(AXES), P(AXES, None)
    return jax.shard_map(
        on_device,
        mesh=mesh,
        in_specs=(rows3, P("pairs"), P("pairs", "mod")) + (P(),) * 12 + (rows3,),
        out_specs=(rows3, rows3, vec, vec, mat, vec, mat, vec, vec, vec, mat, vec, mat, vec),
        check_vma=False,
    )
```
